32 devices in a mesh: dp: 4 (over y, x), ctx: 2 (over core), tensor: 4 (over z).
Axes of the slice: x: 2, y: 2, z: 4, core: 2. Of those that a mesh axis runs over, the one named last changes fastest.
Arguments:
- hidden_in: float32 [8, 1024, 768], P('dp', ('ctx', 'tensor')), may hold values from -6 to 6
- cotangent: float32 [8, 1024, 768], P('dp', ('ctx', 'tensor')), may hold values from -6 to 6
- segment_ids: int32 [8, 1024], P('dp'), may hold values from -1 to 17, as said below
- attn_gain: float32 [768], replicated, may hold values from 0.5 to 1.5
- attn_shift: float32 [768], replicated, may hold values from -1.75 to 1.75
- query_weight: float32 [768, 768], P('dp', 'tensor'), may hold values from -0.21875 to 0.21875
- key_weight: float32 [768, 768], P('dp', 'tensor'), may hold values from -0.21875 to 0.21875
- value_weight: float32 [768, 768], P('dp', 'tensor'), may hold values from -0.21875 to 0.21875
- query_bias: float32 [768], replicated, may hold values from -1.75 to 1.75
- value_bias: float32 [768], replicated, may hold values from -1.75 to 1.75
- output_weight: float32 [768, 768], P('tensor', 'dp'), may hold values from -3.5 to 3.5
- output_bias: float32 [768], replicated, may hold values from -1.75 to 1.75
- ffn_gain: float32 [768], replicated, may hold values from 0.5 to 1.5
- ffn_shift: float32 [768], replicated, may hold values from -1.75 to 1.75
- inner_weight: float32 [768, 3072], P('dp', 'tensor'), may hold values from -0.21875 to 0.21875
- inner_bias: float32 [3072], replicated, may hold values from -1.75 to 1.75
- outer_weight: float32 [3072, 768], P('tensor', 'dp'), may hold values from -0.15625 to 0.15625
- outer_bias: float32 [768], replicated, may hold values from -1.75 to 1.75
Outputs:
- block_out: float32 [8, 1024, 768], P('dp', ('ctx', 'tensor'))
- grad_input: float32 [8, 1024, 768], P('dp', ('ctx', 'tensor'))
- grad_attn_gain: float32 [768], replicated
- grad_attn_shift: float32 [768], replicated
- grad_query_weight: float32 [768, 768], P('dp', 'tensor')
- grad_key_weight: float32 [768, 768], P('dp', 'tensor')
- grad_value_weight: float32 [768, 768], P('dp', 'tensor')
- grad_query_bias: float32 [768], replicated
- grad_value_bias: float32 [768], replicated
- grad_output_weight: float32 [768, 768], P('tensor', 'dp')
- grad_output_bias: float32 [768], replicated
- grad_ffn_gain: float32 [768], replicated
- grad_ffn_shift: float32 [768], replicated
- grad_inner_weight: float32 [768, 3072], P('dp', 'tensor')
- grad_inner_bias: float32 [3072], replicated
- grad_outer_weight: float32 [3072, 768], P('tensor', 'dp')
- grad_outer_bias: float32 [768], replicated
The draws below stay inside these ranges and needn't reach their ends.
Inputs may be any that keep to these rules, and one draw needn't show every extreme that they name: `segment_ids`: in each sequence the document numbers are 0, 1, 2, ... in order of position, each document at most 800 tokens and all but the last one cut at least 60; a tail of 1 to 128 tokens at each sequence's end is padding and carries -1.
All inputs are finite; a program needn't handle non-finite values.
Results may differ from the reference program's by a relative error of at most 0.015.
Values may be sent and summed in bfloat16 or wider, within the bound.
A program may use at most 128 MiB of HBM per device.

```python
import jax
import jax.numpy as jnp
from jax import lax

D = 768
HEADS = 12
HDIM = 64
FF = 3072
LEN = 1024
NSEQ = 8


def draw_segment_ids(key, part):
    key_sizes, key_tail = jax.random.split(jax.random.fold_in(key, 17))
    most_docs = LEN // 60 + 1
    doc_sizes = jax.random.randint(key_sizes, (NSEQ, most_docs), 60, 801)
    seq_number = jnp.arange(NSEQ)[:, None]
    doc_sizes = jnp.where(seq_number == 0, 60, doc_sizes)
    doc_ends = jnp.cumsum(doc_sizes, axis=1)
    places = jnp.arange(LEN)
    numbers = jnp.sum((doc_ends[:, None, :] <= places[None, :, None]).astype(jnp.int32), axis=2)
    tail_size = jax.random.randint(key_tail, (NSEQ, 1), 1, LEN // 8 + 1)
    tail_size = jnp.where(seq_number == 0, 1, tail_size)
    return jnp.where(places[None, :] >= LEN - tail_size, -1, numbers).astype(jnp.int32)


def steps_of(stream_key, extent, shards, low, top_value):
    level = 1.0
    for dim, blocks in shards:
        steps = jax.random.uniform(jax.random.fold_in(jax.random.fold_in(stream_key, 6), dim), (blocks,), jnp.float32, low / len(shards), top_value / len(shards))
        level = level * jnp.repeat(jnp.exp(steps), extent[dim] // blocks).reshape((-1,) + (1,) * (len(extent) - 1 - dim))
    return level


def bell_draw(stream_key, shape, deviation, most, cuts=(), kind=jnp.bfloat16):
    level = steps_of(stream_key, shape, cuts, -0.22, 0.18) if cuts else 1.0
    values = jax.random.normal(stream_key, shape, jnp.float32) * deviation * level
    return jnp.minimum(jnp.maximum(values, -most), most).astype(kind)


def setup_inputs(seed: int = 0) -> dict:
    key_of = jax.random.split(jax.random.key(seed), 19)
    return {
        "hidden_in": bell_draw(key_of[0], (NSEQ, LEN, D), 1.0, 6.0, ((0, 4), (1, 8)), jnp.float32),
        "cotangent": bell_draw(key_of[1], (NSEQ, LEN, D), 1.0, 6.0, ((0, 4), (1, 8)), jnp.float32),
        "segment_ids": draw_segment_ids(jax.random.fold_in(key_of[18], 71), 0),
        "attn_gain": jnp.clip(1.0 + 0.1 * jax.random.normal(key_of[3], (D,), jnp.float32), 0.5, 1.5),
        "attn_shift": bell_draw(key_of[4], (D,), 0.3, 1.75, (), jnp.float32),
        "query_weight": bell_draw(key_of[5], (D, D), D ** -0.5, 0.21875, ((0, 4), (1, 4)), jnp.float32),
        "key_weight": bell_draw(key_of[6], (D, D), D ** -0.5, 0.21875, ((0, 4), (1, 4)), jnp.float32),
        "value_weight": bell_draw(key_of[7], (D, D), D ** -0.5, 0.21875, ((0, 4), (1, 4)), jnp.float32),
        "query_bias": bell_draw(key_of[8], (D,), 0.3, 1.75, (), jnp.float32),
        "value_bias": bell_draw(key_of[9], (D,), 0.3, 1.75, (), jnp.float32),
        "output_weight": bell_draw(key_of[10], (D, D), (max(D // 256, 1)) ** -0.5, 3.5, ((0, 4), (1, 4)), jnp.float32),
        "output_bias": bell_draw(key_of[11], (D,), 0.3, 1.75, (), jnp.float32),
        "ffn_gain": jnp.clip(1.0 + 0.1 * jax.random.normal(key_of[12], (D,), jnp.float32), 0.5, 1.5),
        "ffn_shift": bell_draw(key_of[13], (D,), 0.3, 1.75, (), jnp.float32),
        "inner_weight": bell_draw(key_of[14], (D, FF), D ** -0.5, 0.21875, ((0, 4), (1, 4)), jnp.float32),
        "inner_bias": bell_draw(key_of[15], (FF,), 0.3, 1.75, (), jnp.float32),
        "outer_weight": bell_draw(key_of[16], (FF, D), (FF // 2) ** -0.5, 0.15625, ((0, 4), (1, 4)), jnp.float32),
        "outer_bias": bell_draw(key_of[17], (D,), 0.3, 1.75, (), jnp.float32),
    }


@jax.custom_vjp
def low(v):
    return lax.optimization_barrier(v.astype(jnp.bfloat16)).astype(jnp.float32)

@jax.custom_vjp
def low_back(v):
    return v

def low_keep(v):
    return (low(v), None)

def low_pass(kept, grad):
    return (grad,)

def back_keep(v):
    return (v, None)

def back_low(kept, grad):
    return (low(grad),)
low.defvjp(low_keep, low_pass)
low_back.defvjp(back_keep, back_low)

def rounded_both(value):
    return low(low_back(value))

def matmul(left, right):
    return jnp.dot(left, right, precision=lax.Precision.HIGHEST)

def layer_norm(rows, gain, shift):
    centred = rows - lax.optimization_barrier(jnp.mean(rows, axis=-1, keepdims=True))
    scaled = centred * lax.rsqrt(lax.optimization_barrier(jnp.mean(centred * centred, axis=-1, keepdims=True)) + 1e-05)
    return scaled * gain + shift

def encoder(rows, segment, params):
    attn_gain, attn_shift, query_weight, key_weight, value_weight, query_bias, value_bias, output_weight, output_bias, ffn_gain, ffn_shift, inner_weight, inner_bias, outer_weight, outer_bias = params
    count = rows.shape[0]
    normed = low(layer_norm(rows, attn_gain, attn_shift))
    queries = rounded_both(matmul(normed, low(query_weight)) + query_bias).reshape(count, HEADS, HDIM)
    key_rows = rounded_both(matmul(normed, low(key_weight))).reshape(count, HEADS, HDIM)
    value_rows = rounded_both(matmul(normed, low(value_weight)) + value_bias).reshape(count, HEADS, HDIM)
    scores = jnp.einsum('qhd,khd->hqk', queries, key_rows, precision=lax.Precision.HIGHEST) * HDIM ** (-0.5)
    scores = low_back(scores)
    segment = segment.astype(jnp.int32)
    position = jnp.arange(count, dtype=jnp.int32)
    allowed = (segment[:, None] == segment[None, :]) & ((segment[None, :] >= 0) | (position[:, None] == position[None, :]))
    allowed = allowed[None, :, :]
    visible = jnp.where(allowed, scores, jnp.zeros_like(scores))
    peak = lax.optimization_barrier(jnp.max(jnp.where(allowed, scores, lax.optimization_barrier(jnp.min(visible, axis=-1, keepdims=True))), axis=-1, keepdims=True))
    expo = jnp.where(allowed, jnp.exp(visible - peak), jnp.zeros_like(scores))
    probs = low(expo / lax.optimization_barrier(jnp.sum(expo, axis=-1, keepdims=True)))
    mixed = jnp.einsum('hqk,khd->qhd', probs, value_rows, precision=lax.Precision.HIGHEST).reshape(count, HEADS * HDIM)
    mixed = rounded_both(mixed)
    middle = rows + low_back(matmul(mixed, low(output_weight))) + output_bias
    normed_f = low(layer_norm(middle, ffn_gain, ffn_shift))
    inner = low_back(matmul(normed_f, low(inner_weight)) + inner_bias)
    active = low(jax.nn.gelu(inner, approximate=False))
    return middle + low_back(matmul(active, low(outer_weight))) + outer_bias

def reference(hidden_in, cotangent, segment_ids, attn_gain, attn_shift, query_weight, key_weight, value_weight, query_bias, value_bias, output_weight, output_bias, ffn_gain, ffn_shift, inner_weight, inner_bias, outer_weight, outer_bias):
    params = (attn_gain, attn_shift, query_weight, key_weight, value_weight, query_bias, value_bias, output_weight, output_bias, ffn_gain, ffn_shift, inner_weight, inner_bias, outer_weight, outer_bias)
    params = tuple((item.astype(jnp.float32) for item in params))
    checked = jax.checkpoint(encoder)
    segments = segment_ids.astype(jnp.int32)

    def forward(rows_all, weights):

        def one_sequence(carry, item):
            return (carry, checked(item[0], item[1], weights))
        _, result = lax.scan(one_sequence, jnp.zeros((), jnp.float32), (rows_all, segments))
        return result
    block_out, pullback = jax.vjp(forward, hidden_in.astype(jnp.float32), params)
    grad_input, grad_params = pullback(cotangent.astype(jnp.float32))
    return (block_out, grad_input, grad_params[0], grad_params[1], grad_params[2], grad_params[3], grad_params[4], grad_params[5], grad_params[6], grad_params[7], grad_params[8], grad_params[9], grad_params[10], grad_params[11], grad_params[12], grad_params[13], grad_params[14])
```

```python
import functools

import jax
import jax.numpy as jnp
from jax import lax
from jax.experimental import pallas as pl
from jax.experimental.pallas import tpu as pltpu
from jax.sharding import PartitionSpec as P

HDIM = 64
LANES = 256
ROOT_HALF = 0.7071067811865476
INV_ROOT_TWO_PI = 0.3989422804014327
MESH = pl.DeviceIdType.MESH
BF = jnp.bfloat16
F32 = jnp.float32
HIDE = -1e30


def dims(left, right, a, b):
    return lax.dot_general(left, right, (((a,), (b,)), ((), ())), preferred_element_type=F32)


def norm_parts(rows):
    centred = rows - jnp.mean(rows, axis=-1, keepdims=True)
    inverse = lax.rsqrt(jnp.mean(centred * centred, axis=-1, keepdims=True) + 1e-05)
    return centred * inverse, inverse


class Place:
    def __init__(self):
        self.d = lax.axis_index("dp")
        self.c = lax.axis_index("ctx")
        self.t = lax.axis_index("tensor")
        col, row = self.d % 2, self.d // 2
        self.dx = row * 2 + (1 - col)
        self.dy = (1 - row) * 2 + col
        self.dd = (1 - row) * 2 + (1 - col)
        self.side = self.t // 2
        self.mid = self.t + self.side * (3 - 2 * self.t)

    def unmirror(self, place):
        return place + self.side * (3 - 2 * place)

    def order(self, k):
        if k == 0:
            return self.unmirror(1 - self.mid)
        return self.unmirror(k + 1)

    def order_at(self, k):
        first = 1 - jnp.minimum(k, 1)
        near = first * (1 - self.mid) + (1 - first) * (k + 1)
        own = jnp.minimum(k, 0)
        return -own * self.t + (1 + own) * self.unmirror(near)


def remote(src, dst, send, recv, **where):
    return pltpu.make_async_remote_copy(
        src_ref=src, dst_ref=dst, send_sem=send, recv_sem=recv, device_id=where, device_id_type=MESH
    )


def greet(place, line=True, plane=True, core=True):
    barrier = pltpu.get_barrier_semaphore()
    count = 0
    if line:
        for k in range(1, 4):
            pl.semaphore_signal(
                barrier, inc=1, device_id={"tensor": (place.t + k) % 4}, device_id_type=MESH
            )
        count += 3
    if plane:
        for peer in (place.dx, place.dy, place.dd):
            pl.semaphore_signal(barrier, inc=1, device_id={"dp": peer}, device_id_type=MESH)
        count += 3
    if core:
        pl.semaphore_signal(barrier, inc=1, device_id={"ctx": 1 - place.c}, device_id_type=MESH)
        count += 1
    pl.semaphore_wait(barrier, count)


def forward_kernel(
    hidden, gain, shift, wqkv_s, cargo_s, bias_s, out_bias, gain_f, shift_f, seg_k, seg_q,
    normed, queries, kv, mixed_in, middle, normed_f, wqkv, wout, weights,
    cargo, hide, v_turn, mix_turn, mixed,
    z_send, z_recv, w_send, w_recv, kv_send, kv_recv, m_send, m_recv,
    cz_send, cp_send, cc_send, c_recv, s_recv, own_sem, out_sem,
):
    at = Place()
    d, c, t = at.d, at.c, at.t
    greet(at)

    planes = (at.dx, at.dy, at.dd)
    w_out = [
        remote(wqkv_s, wqkv.at[d], w_send.at[i], w_recv.at[d], dp=peer)
        for i, peer in enumerate(planes)
    ]
    for copy in w_out:
        copy.start()
    own_w = pltpu.make_async_copy(wqkv_s, wqkv.at[d], own_sem.at[0])
    own_w.start()
    own_c = pltpu.make_async_copy(cargo_s, cargo.at[c, t, d], own_sem.at[1])
    own_c.start()

    def z_copy(s, k, dest):
        return remote(
            normed.at[s, t], normed.at[s, t], z_send.at[s, k], z_recv.at[s, t], tensor=dest
        )

    def z_pass(s, shard, dest):
        return remote(
            normed.at[s, shard], normed.at[s, shard], z_send.at[s, 3], z_recv.at[s, shard], tensor=dest
        )

    for s in range(2):
        scaled, _ = norm_parts(hidden[s])
        normed[s, t] = (scaled * gain[...] + shift[...]).astype(BF)
        z_copy(s, 0, at.order(0)).start()
        z_copy(s, 1, at.order(1)).start()

        @pl.when(at.mid == 1)
        def _():
            z_copy(s, 2, at.order(2)).start()

    own_w.wait()
    own_c.wait()

    def cargo_z(k, dest):
        return remote(
            cargo.at[c, t, d], cargo.at[c, t, d], cz_send.at[k], c_recv.at[t, d], tensor=dest
        )

    def cargo_pass(shard, dest):
        return remote(
            cargo.at[c, shard, d], cargo.at[c, shard, d], cz_send.at[3], c_recv.at[shard, d], tensor=dest
        )

    def cargo_plane(axis, k, shard, owner, dest):
        return remote(
            cargo.at[c, shard, owner], cargo.at[c, shard, owner], cp_send.at[axis, k],
            c_recv.at[shard, owner], dp=dest,
        )

    def cargo_core(shard, owner):
        return remote(
            cargo.at[c, shard, owner], cargo.at[c, shard, owner], cc_send.at[shard, owner],
            s_recv.at[shard, owner], ctx=1 - c,
        )

    def cargo_keep(which, shard, owner):
        return pltpu.make_async_copy(
            cargo.at[which, shard, owner, pl.ds(0, 192)], weights.at[which, shard, owner],
            out_sem.at[which, shard, owner],
        )

    def arrived(shard, owner):
        remote(
            cargo.at[c, shard, owner], cargo.at[c, shard, owner], cz_send.at[0],
            c_recv.at[shard, owner], dp=d,
        ).wait_recv()

    def spread(k, shard):
        cargo_plane(0, k, shard, d, at.dx).start()
        cargo_plane(1, k, shard, d, at.dy).start()
        cargo_core(shard, d).start()
        cargo_keep(c, shard, d).start()

    spread(0, t)

    for i, peer in enumerate(planes):
        remote(wqkv_s, wqkv.at[peer], w_send.at[i], w_recv.at[peer], dp=peer).wait_recv()

    lane_head = lax.broadcasted_iota(jnp.int32, (1, LANES), 1) // HDIM

    def attend(s):
        keys_seg = seg_k[s]
        for b in range(2):
            hide[:, b * 256 : (b + 1) * 256] = jnp.where(
                keys_seg == seg_q[s, :, b * 256 : (b + 1) * 256], 0.0, HIDE
            ).astype(F32)
        all_kv = kv[s].reshape(1024, 2 * LANES)
        v_turn[...] = all_kv[:, LANES:].T
        mix_turn[192:, :] = jnp.zeros((64, 512), F32)

        def step(i, carry):
            h, b = i // 2, i % 2
            block = pl.ds(pl.multiple_of(b * 256, 256), 256)
            q_here = queries[s, block, :]
            q_here = jnp.where(lane_head == h, q_here.astype(F32), 0.0).astype(BF)
            scores = dims(kv[s].reshape(1024, 2 * LANES)[:, :LANES], q_here, 1, 1) + hide[:, block]
            peak = jnp.max(scores, axis=0, keepdims=True)
            expo = jnp.exp(scores - peak)
            total = jnp.sum(expo, axis=0, keepdims=True)
            rows = pl.ds(pl.multiple_of(h * HDIM, HDIM), HDIM)
            turned = jnp.dot(v_turn[rows, :], expo.astype(BF), preferred_element_type=F32)
            mix_turn[rows, block] = turned / total
            return carry

        lax.fori_loop(0, 6, step, 0)
        mixed[s] = mix_turn[...].T.astype(BF).reshape(4, 128, LANES)

    def m_copy(s, k, dest):
        return remote(
            mixed.at[s, dest], mixed_in.at[t, s], m_send.at[s, k], m_recv.at[s, t], tensor=dest
        )

    def kv_copy(s, p):
        return remote(
            kv.at[s, c, p], kv.at[s, c, p], kv_send.at[s, p], kv_recv.at[s, p], ctx=1 - c
        )

    for s in range(2):
        def project(k, carry):
            p = at.order_at(k - 1)

            @pl.when(k > 0)
            def _():
                remote(
                    normed.at[s, p], normed.at[s, p], z_send.at[s, 0], z_recv.at[s, p], tensor=p
                ).wait_recv()

            @pl.when((k == 3) & (at.mid == 1))
            def _():
                z_pass(s, p, at.unmirror(0)).start()

            out = jnp.dot(
                normed[s, p], wqkv[...].reshape(768, 768), preferred_element_type=F32
            ) + bias_s[...]
            out = out.astype(BF)
            queries[s, pl.ds(pl.multiple_of(p * 128, 128), 128), :] = (
                out[:, :LANES] * jnp.asarray(HDIM**-0.5, BF)
            )
            kv[s, c, p] = out[:, LANES:]
            kv_copy(s, p).start()
            return carry

        lax.fori_loop(0, 4, project, 0)
        if s == 0:
            cargo_z(0, at.order(0)).start()
            cargo_z(1, at.order(1)).start()

            @pl.when(at.mid == 1)
            def _():
                cargo_z(2, at.order(2)).start()

        for p in range(4):
            remote(
                kv.at[s, 1 - c, p], kv.at[s, 1 - c, p], kv_send.at[s, p], kv_recv.at[s, p], ctx=1 - c
            ).wait_recv()
        attend(s)
        for k in range(3):
            m_copy(s, k, (t + k + 1) % 4).start()
        mixed_in[t, s] = mixed[s, t]

    def diag(k, shard):
        arrived(shard, at.dx)
        arrived(shard, at.dy)

        @pl.when(shard < 2)
        def _():
            cargo_plane(1, 4 + k, shard, at.dx, at.dy).start()

        @pl.when(shard >= 2)
        def _():
            cargo_plane(0, 4 + k, shard, at.dy, at.dx).start()

        cargo_core(shard, at.dx).start()
        cargo_core(shard, at.dy).start()
        cargo_keep(c, shard, at.dx).start()
        cargo_keep(c, shard, at.dy).start()

    for k in range(3):
        p = at.order(k)
        arrived(p, d)
        if k == 2:

            @pl.when(at.mid == 1)
            def _():
                cargo_pass(p, at.unmirror(0)).start()

        spread(k + 1, p)
        diag(k, t if k == 0 else at.order(k - 1))
    diag(3, at.order(2))
    for p in range(4):
        arrived(p, at.dd)
        cargo_core(p, at.dd).start()
        cargo_keep(c, p, at.dd).start()

    def from_sibling(i, carry):
        shard, owner = i // 4, i % 4
        remote(
            cargo.at[1 - c, shard, owner], cargo.at[1 - c, shard, owner], cc_send.at[shard, owner],
            s_recv.at[shard, owner], ctx=1 - c,
        ).wait_recv()
        cargo_keep(1 - c, shard, owner).start()
        for part in range(2):
            for j in range(3):
                start = pl.multiple_of(owner * 192 + part * 96 + j * 32, 32)
                wout[shard, pl.ds(start, 32), :] = cargo[
                    part, shard, owner, 192:224, j * LANES : (j + 1) * LANES
                ]
        return carry

    lax.fori_loop(0, 16, from_sibling, 0)

    for s in range(2):
        for k in range(3):
            p = (t + k + 1) % 4
            remote(
                mixed.at[s, p], mixed_in.at[p, s], m_send.at[s, k], m_recv.at[s, p], tensor=p
            ).wait_recv()
        total = hidden[s] + out_bias[...]
        for p in range(4):
            total = total + dims(mixed_in[p, s], wout[p], 1, 1)
        middle[s] = total
        scaled, _ = norm_parts(total)
        normed_f[s] = (scaled * gain_f[...] + shift_f[...]).astype(BF)

    for copy in w_out:
        copy.wait_send()
    for s in range(2):
        z_copy(s, 0, at.order(0)).wait_send()
        z_copy(s, 1, at.order(1)).wait_send()

        @pl.when(at.mid == 1)
        def _():
            z_copy(s, 2, at.order(2)).wait_send()
            z_pass(s, at.order(2), at.unmirror(0)).wait_send()

        for p in range(4):
            kv_copy(s, p).wait_send()
        for k in range(3):
            m_copy(s, k, (t + k + 1) % 4).wait_send()
    cargo_z(0, at.order(0)).wait_send()
    cargo_z(1, at.order(1)).wait_send()

    @pl.when(at.mid == 1)
    def _():
        cargo_z(2, at.order(2)).wait_send()
        cargo_pass(at.order(2), at.unmirror(0)).wait_send()

    for k in range(4):
        p = t if k == 0 else at.order(k - 1)
        cargo_plane(0, k, p, d, at.dx).wait_send()
        cargo_plane(1, k, p, d, at.dy).wait_send()

        @pl.when(p < 2)
        def _():
            cargo_plane(1, 4 + k, p, at.dx, at.dy).wait_send()

        @pl.when(p >= 2)
        def _():
            cargo_plane(0, 4 + k, p, at.dy, at.dx).wait_send()

    def finish(i, carry):
        shard, owner = i // 4, i % 4
        cargo_core(shard, owner).wait_send()
        cargo_keep(0, shard, owner).wait()
        cargo_keep(1, shard, owner).wait()
        return carry

    lax.fori_loop(0, 16, finish, 0)


VM = pl.BlockSpec(memory_space=pltpu.VMEM)
ANY = pl.BlockSpec(memory_space=pl.ANY)


def forward_call(*operands):
    struct = jax.ShapeDtypeStruct
    dma = pltpu.SemaphoreType.DMA
    return pl.pallas_call(
        forward_kernel,
        out_shape=(
            struct((2, 4, 128, 768), BF),
            struct((2, 512, LANES), BF),
            struct((2, 2, 4, 128, 2 * LANES), BF),
            struct((4, 2, 128, LANES), BF),
            struct((2, 128, 768), F32),
            struct((2, 128, 768), BF),
            struct((4, 192, 768), BF),
            struct((4, 768, LANES), BF),
            struct((2, 4, 4, 192, 768), BF),
        ),
        in_specs=[VM] * len(operands),
        out_specs=(VM,) * 8 + (ANY,),
        scratch_shapes=[
            pltpu.VMEM((2, 4, 4, 224, 768), BF),
            pltpu.VMEM((1024, 512), F32),
            pltpu.VMEM((LANES, 1024), BF),
            pltpu.VMEM((LANES, 512), F32),
            pltpu.VMEM((2, 4, 128, LANES), BF),
            dma((2, 4)), dma((2, 4)),
            dma((3,)), dma((4,)),
            dma((2, 4)), dma((2, 4)),
            dma((2, 3)), dma((2, 4)),
            dma((4,)), dma((2, 8)), dma((4, 4)), dma((4, 4)), dma((4, 4)),
            dma((2,)), dma((2, 4, 4)),
        ],
        compiler_params=pltpu.CompilerParams(
            collective_id=1, has_side_effects=True, vmem_limit_bytes=56 << 20
        ),
        name="forward",
    )(*operands)


def pad_heads(block):
    return jnp.pad(block, [(0, 0)] * (block.ndim - 1) + [(0, LANES - block.shape[-1])])


def smooth_slope(values, cdf):
    return cdf + values * (jnp.exp(-0.5 * values * values) * INV_ROOT_TWO_PI)


def norm_backward(grad_out, scaled, inverse, gain):
    grad_scaled = grad_out * gain
    plain_mean = jnp.mean(grad_scaled, axis=-1, keepdims=True)
    cross_mean = jnp.mean(grad_scaled * scaled, axis=-1, keepdims=True)
    grad_rows = inverse * (grad_scaled - plain_mean - scaled * cross_mean)
    return (grad_rows, jnp.sum(grad_out * scaled, axis=(0, 1)), jnp.sum(grad_out, axis=(0, 1)))


def place_piece(piece, total, start):
    return lax.dynamic_update_slice(jnp.zeros((total,), F32), piece, (start,))


def body(
    hidden_in, cotangent, segment_ids, attn_gain, attn_shift, query_weight, key_weight,
    value_weight, query_bias, value_bias, output_weight, output_bias, ffn_gain, ffn_shift,
    inner_weight, inner_bias, outer_weight, outer_bias,
):
    part = query_weight.shape[1]
    tensor_at = lax.axis_index("tensor")
    ctx_at = lax.axis_index("ctx")
    wqkv_s = jnp.concatenate(
        [pad_heads(query_weight), pad_heads(key_weight), pad_heads(value_weight)], axis=1
    ).astype(BF)
    wout_s = pad_heads(output_weight.T.astype(BF))
    wout_half = lax.dynamic_slice_in_dim(wout_s, ctx_at * 96, 96)
    wout_half = wout_half.reshape(3, 32, LANES).transpose(1, 0, 2).reshape(32, 768)
    ff_s = jnp.where(ctx_at == 0, inner_weight, outer_weight.T).astype(BF)
    cargo_s = jnp.concatenate([ff_s, wout_half], axis=0)
    q_piece = lax.dynamic_slice_in_dim(query_bias, tensor_at * part, part)
    v_piece = lax.dynamic_slice_in_dim(value_bias, tensor_at * part, part)
    bias_s = jnp.concatenate(
        [pad_heads(q_piece), jnp.zeros((LANES,), F32), pad_heads(v_piece)]
    )[None, :]
    places = jnp.arange(segment_ids.shape[1], dtype=jnp.int32)[None, :]
    seg = jnp.where(segment_ids >= 0, segment_ids, -1 - places)
    seg_q = lax.dynamic_slice_in_dim(seg, ctx_at * 512, 512, axis=1)

    (normed, queries, kv, mixed_in, middle, normed_f, wqkv, wout, weights) = forward_call(
        hidden_in, attn_gain[None], attn_shift[None], wqkv_s, cargo_s, bias_s, output_bias[None],
        ffn_gain[None], ffn_shift[None], seg[:, :, None], seg_q[:, None, :],
    )
    w_in = weights[0].reshape(4, 768, 768)
    w_out = weights[1].reshape(4, 768, 768)

    scaled_a, inverse_a = norm_parts(hidden_in)
    scaled_f, inverse_f = norm_parts(middle)
    nf = normed_f.reshape(256, 768)
    cot = cotangent.reshape(256, 768)
    up = cot.astype(BF)
    inner = jnp.einsum("rd,tdu->rtu", nf, w_in, preferred_element_type=F32) + inner_bias.reshape(4, 768)
    cdf = 0.5 * (1.0 + lax.erf(inner * ROOT_HALF))
    active = (inner * cdf).astype(BF)
    block_out = middle + jnp.einsum(
        "rtu,tdu->rd", active, w_out, preferred_element_type=F32
    ).reshape(2, 128, 768) + outer_bias
    grad_active = jnp.einsum("rd,tdu->rtu", up, w_out, preferred_element_type=F32)
    grad_inner = (grad_active * smooth_slope(inner, cdf)).astype(BF)
    grad_nf = jnp.einsum("rtu,tdu->rd", grad_inner, w_in, preferred_element_type=F32)
    grad_w_in = jnp.einsum("rd,rtu->tdu", nf, grad_inner, preferred_element_type=F32)
    grad_w_out = jnp.einsum("rd,rtu->tdu", up, active, preferred_element_type=F32)
    grad_rows_f, grad_ffn_g, grad_ffn_s = norm_backward(
        grad_nf.reshape(2, 128, 768), scaled_f, inverse_f, ffn_gain
    )
    grad_middle = cotangent + grad_rows_f
    grad_branch = grad_middle.astype(BF)
    gb = grad_branch.reshape(256, 768)
    grad_wout = jnp.einsum(
        "trc,rd->tdc", mixed_in.reshape(4, 256, LANES), gb, preferred_element_type=F32
    )
    grad_mix = jnp.einsum("rd,tdc->trc", gb, wout, preferred_element_type=F32).astype(BF)
    grad_mix = lax.all_to_all(grad_mix.reshape(4, 2, 128, LANES), "tensor", 0, 0, tiled=True)
    grad_mixed = grad_mix.transpose(1, 0, 2, 3).reshape(2, 512, LANES)[..., :part]
    heads = part // HDIM
    q3 = queries[..., :part].reshape(2, 512, heads, HDIM)
    k3 = kv[..., :part].reshape(2, 1024, heads, HDIM)
    v3 = kv[..., LANES : LANES + part].reshape(2, 1024, heads, HDIM)
    g3 = grad_mixed.reshape(2, 512, heads, HDIM)
    scores = jnp.einsum("sqhd,skhd->shqk", q3, k3, preferred_element_type=F32)
    scores = jnp.where((seg_q[:, :, None] == seg[:, None, :])[:, None], scores, HIDE)
    probs = jax.nn.softmax(scores, axis=-1)
    grad_probs = jnp.einsum("sqhd,skhd->shqk", g3, v3, preferred_element_type=F32)
    centre = jnp.sum(probs * grad_probs, axis=-1, keepdims=True)
    grad_scores = (probs * (grad_probs - centre)).astype(BF)
    grad_v = jnp.einsum("shqk,sqhd->skhd", probs.astype(BF), g3, preferred_element_type=F32)
    grad_k = jnp.einsum("shqk,sqhd->skhd", grad_scores, q3, preferred_element_type=F32)
    grad_q = jnp.einsum("shqk,skhd->sqhd", grad_scores, k3, preferred_element_type=F32) * HDIM**-0.5
    grad_q = grad_q.reshape(2, 512, part).astype(BF)
    grad_k = lax.psum_scatter(
        grad_k.reshape(2, 1024, part).astype(BF), "ctx", scatter_dimension=1, tiled=True
    )
    grad_v = lax.psum_scatter(
        grad_v.reshape(2, 1024, part).astype(BF), "ctx", scatter_dimension=1, tiled=True
    )
    grad_qkv = jnp.concatenate([pad_heads(grad_q), pad_heads(grad_k), pad_heads(grad_v)], axis=-1)
    grad_qkv = grad_qkv.reshape(1024, 768)
    grad_wqkv = jnp.einsum(
        "rd,rc->dc", normed.reshape(1024, 768), grad_qkv, preferred_element_type=F32
    )
    grad_na = jnp.einsum("rc,dc->rd", grad_qkv, wqkv.reshape(768, 768), preferred_element_type=F32)
    grad_na = lax.psum_scatter(
        grad_na.astype(BF).reshape(2, 512, 768), "tensor", scatter_dimension=1, tiled=True
    ).astype(F32)
    grad_rows_a, grad_attn_g, grad_attn_s = norm_backward(grad_na, scaled_a, inverse_a, attn_gain)
    grad_input = grad_middle + grad_rows_a

    g_in = lax.psum_scatter(
        grad_w_in.astype(BF).reshape(4, 4, 192, 768), "tensor", scatter_dimension=0, tiled=True
    )
    g_in = lax.psum_scatter(g_in, "dp", scatter_dimension=1, tiled=True).reshape(192, 768)
    g_out = lax.psum_scatter(
        grad_w_out.astype(BF).reshape(4, 4, 192, 768), "tensor", scatter_dimension=0, tiled=True
    )
    g_out = lax.psum_scatter(g_out, "dp", scatter_dimension=1, tiled=True).reshape(192, 768)
    g_wo = lax.psum_scatter(
        grad_wout.astype(BF).reshape(4, 4, 192, LANES), "tensor", scatter_dimension=0, tiled=True
    )
    g_wo = lax.psum_scatter(g_wo, "dp", scatter_dimension=1, tiled=True).reshape(192, LANES)
    g_qkv = lax.psum_scatter(
        grad_wqkv.astype(BF).reshape(4, 192, 768), "dp", scatter_dimension=0, tiled=True
    ).reshape(192, 768)
    g_in, g_out, g_wo, g_qkv = lax.psum((g_in, g_out, g_wo, g_qkv), "ctx")
    g_in, g_out, g_wo, g_qkv = (g.astype(F32) for g in (g_in, g_out, g_wo, g_qkv))
    sums = jnp.sum(grad_qkv.astype(F32), axis=0)
    small = lax.psum(
        jnp.concatenate([
            grad_attn_g, grad_attn_s,
            place_piece(sums[:part], 768, tensor_at * part),
            place_piece(sums[2 * LANES : 2 * LANES + part], 768, tensor_at * part),
            jnp.sum(grad_middle, axis=(0, 1)), grad_ffn_g, grad_ffn_s,
            jnp.sum(cotangent, axis=(0, 1)),
            jnp.sum(grad_inner.astype(F32), axis=0).reshape(3072),
        ]),
        ("dp", "ctx", "tensor"),
    )
    row = lambda i: small[768 * i : 768 * (i + 1)]
    return (
        block_out, grad_input, row(0), row(1),
        g_qkv[:, :part], g_qkv[:, LANES : LANES + part], g_qkv[:, 2 * LANES : 2 * LANES + part],
        row(2), row(3), g_wo[:, :part].T, row(4), row(5), row(6), g_in, small[768 * 8 :],
        g_out.T, row(7),
    )


root_half = 0.7071067811865476
inv_root_two_pi = 0.3989422804014327


def general_gate(values):
    return values * (0.5 * (1.0 + lax.erf(values * root_half)))


def general_slope(values):
    normal_cdf = 0.5 * (1.0 + lax.erf(values * root_half))
    normal_pdf = jnp.exp(-0.5 * values * values) * inv_root_two_pi
    return normal_cdf + values * normal_pdf


def general_norm(rows, gain, shift):
    centred = rows - jnp.mean(rows, axis=-1, keepdims=True)
    inverse = lax.rsqrt(jnp.mean(centred * centred, axis=-1, keepdims=True) + 1e-05)
    scaled = centred * inverse
    return (scaled * gain + shift, scaled, inverse)


def general_norm_backward(grad_out, scaled, inverse, gain):
    grad_scaled = grad_out * gain
    plain_mean = jnp.mean(grad_scaled, axis=-1, keepdims=True)
    cross_mean = jnp.mean(grad_scaled * scaled, axis=-1, keepdims=True)
    grad_rows = inverse * (grad_scaled - plain_mean - scaled * cross_mean)
    return (grad_rows, jnp.sum(grad_out * scaled, axis=0), jnp.sum(grad_out, axis=0))


def tensor_rows(block):
    return lax.all_gather(block, "tensor", axis=0, tiled=True)


def tensor_sums(block):
    return lax.psum_scatter(block, "tensor", scatter_dimension=0, tiled=True)


def fetch_weights(shards):
    return (
        lax.all_gather(shards[0], "dp", axis=0, tiled=True),
        lax.all_gather(shards[1], "dp", axis=0, tiled=True),
        lax.all_gather(shards[2], "dp", axis=0, tiled=True),
        lax.all_gather(shards[3], "dp", axis=0, tiled=True),
        lax.all_gather(shards[4], "dp", axis=1, tiled=True),
        lax.all_gather(shards[5], "dp", axis=1, tiled=True),
    )


def general_piece(piece, total, start):
    return lax.dynamic_update_slice(jnp.zeros((total,), jnp.float32), piece, (start,))


def general_body(
    hidden_in,
    cotangent,
    segment_ids,
    attn_gain,
    attn_shift,
    query_weight,
    key_weight,
    value_weight,
    query_bias,
    value_bias,
    output_weight,
    output_bias,
    ffn_gain,
    ffn_shift,
    inner_weight,
    inner_bias,
    outer_weight,
    outer_bias,
):
    width = hidden_in.shape[2]
    part_width = query_weight.shape[1]
    unit_width = inner_weight.shape[1]
    unit_total = inner_bias.shape[0]
    heads_here = part_width // HDIM
    tensor_at = lax.axis_index("tensor")
    ctx_at = lax.axis_index("ctx")
    half_rows = hidden_in.shape[1] * lax.axis_size("tensor")
    seq_rows = segment_ids.shape[1]
    factor = HDIM ** (-0.5)
    query_piece = lax.dynamic_slice_in_dim(query_bias, tensor_at * part_width, part_width)
    value_piece = lax.dynamic_slice_in_dim(value_bias, tensor_at * part_width, part_width)
    inner_piece = lax.dynamic_slice_in_dim(inner_bias, tensor_at * unit_width, unit_width)
    shards = (
        query_weight.astype(jnp.bfloat16),
        key_weight.astype(jnp.bfloat16),
        value_weight.astype(jnp.bfloat16),
        inner_weight.astype(jnp.bfloat16),
        output_weight.astype(jnp.bfloat16),
        outer_weight.astype(jnp.bfloat16),
    )
    key_index = jnp.arange(seq_rows)
    query_index = ctx_at * half_rows + jnp.arange(half_rows)

    def masked_scores(queries, key_all, allowed):
        scores = (
            jnp.einsum("qhd,khd->hqk", queries, key_all, preferred_element_type=jnp.float32)
            * factor
        )
        return jnp.where(allowed[None, :, :], scores, -1e30)

    def micro(weights_bf, carry, item):
        w_query, w_key, w_value, w_inner, w_output, w_outer = weights_bf
        rows, cot_rows, segment_row = item
        query_seg = lax.dynamic_slice_in_dim(segment_row, ctx_at * half_rows, half_rows)
        allowed = (query_seg[:, None] == segment_row[None, :]) & (
            (segment_row[None, :] >= 0) | (query_index[:, None] == key_index[None, :])
        )
        normed, scaled_a, inverse_a = general_norm(rows, attn_gain, attn_shift)
        normed_all = tensor_rows(normed.astype(jnp.bfloat16))
        queries = (
            jnp.dot(normed_all, w_query, preferred_element_type=jnp.float32) + query_piece
        ).astype(jnp.bfloat16)
        key_half = jnp.dot(normed_all, w_key, preferred_element_type=jnp.float32).astype(
            jnp.bfloat16
        )
        value_half = (
            jnp.dot(normed_all, w_value, preferred_element_type=jnp.float32) + value_piece
        ).astype(jnp.bfloat16)
        key_all, value_all = (
            lax.all_gather(key_half, "ctx", axis=0, tiled=True),
            lax.all_gather(value_half, "ctx", axis=0, tiled=True),
        )
        queries = queries.reshape(half_rows, heads_here, HDIM)
        key_all = key_all.reshape(seq_rows, heads_here, HDIM)
        value_all = value_all.reshape(seq_rows, heads_here, HDIM)
        masked = masked_scores(queries, key_all, allowed)
        peak = jnp.max(masked, axis=-1, keepdims=True)
        expo = jnp.exp(masked - peak)
        total = jnp.sum(expo, axis=-1, keepdims=True)
        log_total = peak + jnp.log(total)
        probs = (expo / total).astype(jnp.bfloat16)
        mixed = jnp.einsum("hqk,khd->qhd", probs, value_all, preferred_element_type=jnp.float32)
        mixed = mixed.reshape(half_rows, part_width).astype(jnp.bfloat16)
        branch_a = tensor_sums(jnp.dot(mixed, w_output, preferred_element_type=jnp.float32))
        middle = rows + branch_a + output_bias
        normed_f, scaled_f, inverse_f = general_norm(middle, ffn_gain, ffn_shift)
        normed_f_all = tensor_rows(normed_f.astype(jnp.bfloat16))
        inner = jnp.dot(normed_f_all, w_inner, preferred_element_type=jnp.float32) + inner_piece
        active = general_gate(inner).astype(jnp.bfloat16)
        branch_f = tensor_sums(jnp.dot(active, w_outer, preferred_element_type=jnp.float32))
        result_rows = middle + branch_f + outer_bias
        grad_up = tensor_rows(cot_rows.astype(jnp.bfloat16))
        grad_outer_w = jnp.einsum("tf,td->fd", active, grad_up, preferred_element_type=jnp.float32)
        grad_active = jnp.einsum("td,fd->tf", grad_up, w_outer, preferred_element_type=jnp.float32)
        grad_inner = (grad_active * general_slope(inner)).astype(jnp.bfloat16)
        grad_inner_w = jnp.einsum(
            "td,tf->df", normed_f_all, grad_inner, preferred_element_type=jnp.float32
        )
        grad_inner_b = jnp.sum(grad_inner.astype(jnp.float32), axis=0)
        grad_normed_f = tensor_sums(
            jnp.einsum("tf,df->td", grad_inner, w_inner, preferred_element_type=jnp.float32)
        )
        grad_rows_f, grad_ffn_g, grad_ffn_s = general_norm_backward(
            grad_normed_f, scaled_f, inverse_f, ffn_gain
        )
        grad_middle = cot_rows + grad_rows_f
        grad_branch = tensor_rows(grad_middle.astype(jnp.bfloat16))
        grad_output_w = jnp.einsum(
            "tc,td->cd", mixed, grad_branch, preferred_element_type=jnp.float32
        )
        grad_mixed = jnp.einsum(
            "td,cd->tc", grad_branch, w_output, preferred_element_type=jnp.float32
        )
        grad_mixed = grad_mixed.astype(jnp.bfloat16).reshape(half_rows, heads_here, HDIM)
        grad_probs = jnp.einsum(
            "qhd,khd->hqk", grad_mixed, value_all, preferred_element_type=jnp.float32
        )
        grad_value_part = jnp.einsum(
            "hqk,qhd->khd", probs, grad_mixed, preferred_element_type=jnp.float32
        )
        again = jnp.exp(masked_scores(queries, key_all, allowed) - log_total)
        centre = jnp.sum(again * grad_probs, axis=-1, keepdims=True)
        grad_scores = (again * (grad_probs - centre)).astype(jnp.bfloat16)
        grad_queries = (
            jnp.einsum("hqk,khd->qhd", grad_scores, key_all, preferred_element_type=jnp.float32)
            * factor
        )
        grad_queries = grad_queries.reshape(half_rows, part_width).astype(jnp.bfloat16)
        grad_key_part = (
            jnp.einsum("hqk,qhd->khd", grad_scores, queries, preferred_element_type=jnp.float32)
            * factor
        )
        grad_key_sum, grad_value_sum = (
            lax.psum_scatter(
                grad_key_part.reshape(seq_rows, part_width).astype(jnp.bfloat16),
                "ctx",
                scatter_dimension=0,
                tiled=True,
            ).astype(jnp.float32),
            lax.psum_scatter(
                grad_value_part.reshape(seq_rows, part_width).astype(jnp.bfloat16),
                "ctx",
                scatter_dimension=0,
                tiled=True,
            ).astype(jnp.float32),
        )
        grad_keys = grad_key_sum.astype(jnp.bfloat16)
        grad_values = grad_value_sum.astype(jnp.bfloat16)
        grad_query_w = jnp.einsum(
            "td,tc->dc", normed_all, grad_queries, preferred_element_type=jnp.float32
        )
        grad_key_w = jnp.einsum(
            "td,tc->dc", normed_all, grad_keys, preferred_element_type=jnp.float32
        )
        grad_value_w = jnp.einsum(
            "td,tc->dc", normed_all, grad_values, preferred_element_type=jnp.float32
        )
        grad_query_b = jnp.sum(grad_queries.astype(jnp.float32), axis=0)
        grad_value_b = jnp.sum(grad_values.astype(jnp.float32), axis=0)
        grad_normed_part = jnp.einsum(
            "tc,dc->td", grad_queries, w_query, preferred_element_type=jnp.float32
        )
        grad_normed_part = grad_normed_part + jnp.einsum(
            "tc,dc->td", grad_keys, w_key, preferred_element_type=jnp.float32
        )
        grad_normed_part = grad_normed_part + jnp.einsum(
            "tc,dc->td", grad_values, w_value, preferred_element_type=jnp.float32
        )
        grad_normed = tensor_sums(grad_normed_part)
        grad_rows_a, grad_attn_g, grad_attn_s = general_norm_backward(
            grad_normed, scaled_a, inverse_a, attn_gain
        )
        grad_rows = grad_middle + grad_rows_a
        big_sums, small_sums = carry
        big_sums = (
            big_sums[0] + grad_query_w,
            big_sums[1] + grad_key_w,
            big_sums[2] + grad_value_w,
            big_sums[3] + grad_inner_w,
            big_sums[4] + grad_output_w,
            big_sums[5] + grad_outer_w,
        )
        small_terms = (
            grad_attn_g,
            grad_attn_s,
            general_piece(grad_query_b, width, tensor_at * part_width),
            general_piece(grad_value_b, width, tensor_at * part_width),
            jnp.sum(grad_middle, axis=0),
            grad_ffn_g,
            grad_ffn_s,
            general_piece(grad_inner_b, unit_total, tensor_at * unit_width),
            jnp.sum(cot_rows, axis=0),
        )
        small_sums = tuple((old + new for old, new in zip(small_sums, small_terms)))
        return ((big_sums, small_sums), (result_rows, grad_rows))

    big_init = (
        jnp.zeros((width, part_width), jnp.float32),
        jnp.zeros((width, part_width), jnp.float32),
        jnp.zeros((width, part_width), jnp.float32),
        jnp.zeros((width, unit_width), jnp.float32),
        jnp.zeros((part_width, width), jnp.float32),
        jnp.zeros((unit_width, width), jnp.float32),
    )
    small_init = tuple((jnp.zeros((width,), jnp.float32) for index_small in range(7))) + (
        jnp.zeros((unit_total,), jnp.float32),
        jnp.zeros((width,), jnp.float32),
    )
    small_init = (
        small_init[0],
        small_init[1],
        small_init[2],
        small_init[3],
        small_init[4],
        small_init[5],
        small_init[6],
        small_init[7],
        small_init[8],
    )
    gathered = fetch_weights(shards)

    def scan_step(carry, item):
        return micro(gathered, carry, item)

    (big_sums, small_sums), (block_out, grad_input) = lax.scan(
        scan_step, (big_init, small_init), (hidden_in, cotangent, segment_ids)
    )
    paired = (
        lax.psum(big_sums[0].astype(jnp.bfloat16), "ctx").astype(jnp.float32),
        lax.psum(big_sums[1].astype(jnp.bfloat16), "ctx").astype(jnp.float32),
        lax.psum(big_sums[2].astype(jnp.bfloat16), "ctx").astype(jnp.float32),
        lax.psum(big_sums[3].astype(jnp.bfloat16), "ctx").astype(jnp.float32),
        lax.psum(big_sums[4].astype(jnp.bfloat16), "ctx").astype(jnp.float32),
        lax.psum(big_sums[5].astype(jnp.bfloat16), "ctx").astype(jnp.float32),
    )
    owned = (
        lax.psum_scatter(
            paired[0].astype(jnp.bfloat16), "dp", scatter_dimension=0, tiled=True
        ).astype(jnp.float32),
        lax.psum_scatter(
            paired[1].astype(jnp.bfloat16), "dp", scatter_dimension=0, tiled=True
        ).astype(jnp.float32),
        lax.psum_scatter(
            paired[2].astype(jnp.bfloat16), "dp", scatter_dimension=0, tiled=True
        ).astype(jnp.float32),
        lax.psum_scatter(
            paired[3].astype(jnp.bfloat16), "dp", scatter_dimension=0, tiled=True
        ).astype(jnp.float32),
        lax.psum_scatter(
            paired[4].astype(jnp.bfloat16), "dp", scatter_dimension=1, tiled=True
        ).astype(jnp.float32),
        lax.psum_scatter(
            paired[5].astype(jnp.bfloat16), "dp", scatter_dimension=1, tiled=True
        ).astype(jnp.float32),
    )
    small = lax.psum(
        (
            small_sums[0],
            small_sums[1],
            small_sums[2],
            small_sums[3],
            small_sums[4],
            small_sums[5],
            small_sums[6],
            small_sums[7],
            small_sums[8],
        ),
        ("dp", "ctx", "tensor"),
    )
    return (
        block_out,
        grad_input,
        small[0],
        small[1],
        owned[0],
        owned[1],
        owned[2],
        small[2],
        small[3],
        owned[4],
        small[4],
        small[5],
        small[6],
        owned[3],
        small[7],
        owned[5],
        small[8],
    )


SPECS = (
    P("dp", ("ctx", "tensor"), None), P("dp", ("ctx", "tensor"), None), P("dp", None), P(), P(),
    P("dp", "tensor"), P("dp", "tensor"), P("dp", "tensor"), P(), P(), P("tensor", "dp"), P(), P(),
    P(), P("dp", "tensor"), P(), P("tensor", "dp"), P(),
)
OUT_SPECS = (
    P("dp", ("ctx", "tensor"), None), P("dp", ("ctx", "tensor"), None), P(), P(),
    P("dp", "tensor"), P("dp", "tensor"), P("dp", "tensor"), P(), P(), P("tensor", "dp"), P(), P(),
    P(), P("dp", "tensor"), P(), P("tensor", "dp"), P(),
)


def solution(mesh):
    lined_up = mesh.shape["dp"] == 4 and mesh.shape["tensor"] == 4 and mesh.shape["ctx"] == 2
    return jax.shard_map(
        body if lined_up else general_body, mesh=mesh, in_specs=SPECS, out_specs=OUT_SPECS, check_vma=False
    )
```

```python
import functools

import jax
import jax.numpy as jnp
from jax import lax
from jax.experimental import pallas as pl
from jax.experimental.pallas import tpu as pltpu
from jax.sharding import PartitionSpec as P

HDIM = 64
LANES = 256
ROOT_HALF = 0.7071067811865476
INV_ROOT_TWO_PI = 0.3989422804014327
MESH = pl.DeviceIdType.MESH
BF = jnp.bfloat16
F32 = jnp.float32
HIDE = -1e30


def dims(left, right, a, b):
    return lax.dot_general(left, right, (((a,), (b,)), ((), ())), preferred_element_type=F32)


def norm_parts(rows):
    centred = rows - jnp.mean(rows, axis=-1, keepdims=True)
    inverse = lax.rsqrt(jnp.mean(centred * centred, axis=-1, keepdims=True) + 1e-05)
    return centred * inverse, inverse


class Place:
    def __init__(self):
        self.d = lax.axis_index("dp")
        self.c = lax.axis_index("ctx")
        self.t = lax.axis_index("tensor")
        col, row = self.d % 2, self.d // 2
        self.dx = row * 2 + (1 - col)
        self.dy = (1 - row) * 2 + col
        self.dd = (1 - row) * 2 + (1 - col)
        self.side = self.t // 2
        self.mid = self.t + self.side * (3 - 2 * self.t)

    def unmirror(self, place):
        return place + self.side * (3 - 2 * place)

    def order(self, k):
        if k == 0:
            return self.unmirror(1 - self.mid)
        return self.unmirror(k + 1)

    def order_at(self, k):
        first = 1 - jnp.minimum(k, 1)
        near = first * (1 - self.mid) + (1 - first) * (k + 1)
        own = jnp.minimum(k, 0)
        return -own * self.t + (1 + own) * self.unmirror(near)


def remote(src, dst, send, recv, **where):
    return pltpu.make_async_remote_copy(
        src_ref=src, dst_ref=dst, send_sem=send, recv_sem=recv, device_id=where, device_id_type=MESH
    )


def greet(place, line=True, plane=True, core=True):
    barrier = pltpu.get_barrier_semaphore()
    count = 0
    if line:
        for k in range(1, 4):
            pl.semaphore_signal(
                barrier, inc=1, device_id={"tensor": (place.t + k) % 4}, device_id_type=MESH
            )
        count += 3
    if plane:
        for peer in (place.dx, place.dy, place.dd):
            pl.semaphore_signal(barrier, inc=1, device_id={"dp": peer}, device_id_type=MESH)
        count += 3
    if core:
        pl.semaphore_signal(barrier, inc=1, device_id={"ctx": 1 - place.c}, device_id_type=MESH)
        count += 1
    pl.semaphore_wait(barrier, count)


def forward_kernel(
    hidden, gain, shift, wqkv_s, cargo_s, bias_s, out_bias, gain_f, shift_f, seg_k, seg_q,
    normed, queries, kv, mixed_in, middle, normed_f, wqkv, wout, weights,
    cargo, hide, v_turn, mix_turn, mixed,
    z_send, z_recv, w_send, w_recv, kv_send, kv_recv, m_send, m_recv,
    cz_send, cp_send, cc_send, c_recv, s_recv, own_sem, out_sem,
):
    at = Place()
    d, c, t = at.d, at.c, at.t
    greet(at)

    planes = (at.dx, at.dy, at.dd)
    w_out = [
        remote(wqkv_s, wqkv.at[d], w_send.at[i], w_recv.at[d], dp=peer)
        for i, peer in enumerate(planes)
    ]
    for copy in w_out:
        copy.start()
    own_w = pltpu.make_async_copy(wqkv_s, wqkv.at[d], own_sem.at[0])
    own_w.start()
    own_c = pltpu.make_async_copy(cargo_s, cargo.at[c, t, d], own_sem.at[1])
    own_c.start()

    def z_copy(s, k, dest):
        return remote(
            normed.at[s, t], normed.at[s, t], z_send.at[s, k], z_recv.at[s, t], tensor=dest
        )

    def z_pass(s, shard, dest):
        return remote(
            normed.at[s, shard], normed.at[s, shard], z_send.at[s, 3], z_recv.at[s, shard], tensor=dest
        )

    for s in range(2):
        scaled, _ = norm_parts(hidden[s])
        normed[s, t] = (scaled * gain[...] + shift[...]).astype(BF)
        z_copy(s, 0, at.order(0)).start()
        z_copy(s, 1, at.order(1)).start()

        @pl.when(at.mid == 1)
        def _():
            z_copy(s, 2, at.order(2)).start()

    own_w.wait()
    own_c.wait()

    def cargo_z(k, dest):
        return remote(
            cargo.at[c, t, d], cargo.at[c, t, d], cz_send.at[k], c_recv.at[t, d], tensor=dest
        )

    def cargo_pass(shard, dest):
        return remote(
            cargo.at[c, shard, d], cargo.at[c, shard, d], cz_send.at[3], c_recv.at[shard, d], tensor=dest
        )

    def cargo_plane(axis, k, shard, owner, dest):
        return remote(
            cargo.at[c, shard, owner], cargo.at[c, shard, owner], cp_send.at[axis, k],
            c_recv.at[shard, owner], dp=dest,
        )

    def cargo_core(shard, owner):
        return remote(
            cargo.at[c, shard, owner], cargo.at[c, shard, owner], cc_send.at[shard, owner],
            s_recv.at[shard, owner], ctx=1 - c,
        )

    def cargo_keep(which, shard, owner):
        return pltpu.make_async_copy(
            cargo.at[which, shard, owner, pl.ds(0, 192)], weights.at[which, shard, owner],
            out_sem.at[which, shard, owner],
        )

    def arrived(shard, owner):
        remote(
            cargo.at[c, shard, owner], cargo.at[c, shard, owner], cz_send.at[0],
            c_recv.at[shard, owner], dp=d,
        ).wait_recv()

    def spread(k, shard):
        cargo_plane(0, k, shard, d, at.dx).start()
        cargo_plane(1, k, shard, d, at.dy).start()
        cargo_core(shard, d).start()
        cargo_keep(c, shard, d).start()

    spread(0, t)

    for i, peer in enumerate(planes):
        remote(wqkv_s, wqkv.at[peer], w_send.at[i], w_recv.at[peer], dp=peer).wait_recv()

    lane_head = lax.broadcasted_iota(jnp.int32, (1, LANES), 1) // HDIM

    def attend(s):
        keys_seg = jnp.broadcast_to(seg_k[s], (128, 1024)).T[:, :1]
        for b in range(2):
            hide[:, b * 256 : (b + 1) * 256] = jnp.where(
                keys_seg == seg_q[s, :, b * 256 : (b + 1) * 256], 0.0, HIDE
            ).astype(F32)
        all_kv = kv[s].reshape(1024, 2 * LANES)
        v_turn[...] = all_kv[:, LANES:].T
        mix_turn[192:, :] = jnp.zeros((64, 512), F32)

        def step(i, carry):
            h, b = i // 2, i % 2
            block = pl.ds(pl.multiple_of(b * 256, 256), 256)
            q_here = queries[s, block, :]
            q_here = jnp.where(lane_head == h, q_here.astype(F32), 0.0).astype(BF)
            scores = dims(kv[s].reshape(1024, 2 * LANES)[:, :LANES], q_here, 1, 1) + hide[:, block]
            peak = jnp.max(scores, axis=0, keepdims=True)
            expo = jnp.exp(scores - peak)
            total = jnp.sum(expo, axis=0, keepdims=True)
            rows = pl.ds(pl.multiple_of(h * HDIM, HDIM), HDIM)
            turned = jnp.dot(v_turn[rows, :], expo.astype(BF), preferred_element_type=F32)
            mix_turn[rows, block] = turned / total
            return carry

        lax.fori_loop(0, 6, step, 0)
        mixed[s] = mix_turn[...].T.astype(BF).reshape(4, 128, LANES)

    def m_copy(s, k, dest):
        return remote(
            mixed.at[s, dest], mixed_in.at[t, s], m_send.at[s, k], m_recv.at[s, t], tensor=dest
        )

    def kv_copy(s, p):
        return remote(
            kv.at[s, c, p], kv.at[s, c, p], kv_send.at[s, p], kv_recv.at[s, p], ctx=1 - c
        )

    for s in range(2):
        def project(k, carry):
            p = at.order_at(k - 1)

            @pl.when(k > 0)
            def _():
                remote(
                    normed.at[s, p], normed.at[s, p], z_send.at[s, 0], z_recv.at[s, p], tensor=p
                ).wait_recv()

            @pl.when((k == 3) & (at.mid == 1))
            def _():
                z_pass(s, p, at.unmirror(0)).start()

            out = jnp.dot(
                normed[s, p], wqkv[...].reshape(768, 768), preferred_element_type=F32
            ) + bias_s[...]
            out = out.astype(BF)
            queries[s, pl.ds(pl.multiple_of(p * 128, 128), 128), :] = (
                out[:, :LANES] * jnp.asarray(HDIM**-0.5, BF)
            )
            kv[s, c, p] = out[:, LANES:]
            kv_copy(s, p).start()
            return carry

        lax.fori_loop(0, 4, project, 0)
        if s == 0:
            cargo_z(0, at.order(0)).start()
            cargo_z(1, at.order(1)).start()

            @pl.when(at.mid == 1)
            def _():
                cargo_z(2, at.order(2)).start()

        for p in range(4):
            remote(
                kv.at[s, 1 - c, p], kv.at[s, 1 - c, p], kv_send.at[s, p], kv_recv.at[s, p], ctx=1 - c
            ).wait_recv()
        attend(s)
        for k in range(3):
            m_copy(s, k, (t + k + 1) % 4).start()
        mixed_in[t, s] = mixed[s, t]

    def diag(k, shard):
        arrived(shard, at.dx)
        arrived(shard, at.dy)

        @pl.when(shard < 2)
        def _():
            cargo_plane(1, 4 + k, shard, at.dx, at.dy).start()

        @pl.when(shard >= 2)
        def _():
            cargo_plane(0, 4 + k, shard, at.dy, at.dx).start()

        cargo_core(shard, at.dx).start()
        cargo_core(shard, at.dy).start()
        cargo_keep(c, shard, at.dx).start()
        cargo_keep(c, shard, at.dy).start()

    for k in range(3):
        p = at.order(k)
        arrived(p, d)
        if k == 2:

            @pl.when(at.mid == 1)
            def _():
                cargo_pass(p, at.unmirror(0)).start()

        spread(k + 1, p)
        diag(k, t if k == 0 else at.order(k - 1))
    diag(3, at.order(2))
    for p in range(4):
        arrived(p, at.dd)
        cargo_core(p, at.dd).start()
        cargo_keep(c, p, at.dd).start()

    def from_sibling(i, carry):
        shard, owner = i // 4, i % 4
        remote(
            cargo.at[1 - c, shard, owner], cargo.at[1 - c, shard, owner], cc_send.at[shard, owner],
            s_recv.at[shard, owner], ctx=1 - c,
        ).wait_recv()
        cargo_keep(1 - c, shard, owner).start()
        for part in range(2):
            for j in range(3):
                start = pl.multiple_of(owner * 192 + part * 96 + j * 32, 32)
                wout[shard, pl.ds(start, 32), :] = cargo[
                    part, shard, owner, 192:224, j * LANES : (j + 1) * LANES
                ]
        return carry

    lax.fori_loop(0, 16, from_sibling, 0)

    for s in range(2):
        for k in range(3):
            p = (t + k + 1) % 4
            remote(
                mixed.at[s, p], mixed_in.at[p, s], m_send.at[s, k], m_recv.at[s, p], tensor=p
            ).wait_recv()
        total = hidden[s] + out_bias[...]
        for p in range(4):
            total = total + dims(mixed_in[p, s], wout[p], 1, 1)
        middle[s] = total
        scaled, _ = norm_parts(total)
        normed_f[s] = (scaled * gain_f[...] + shift_f[...]).astype(BF)

    for copy in w_out:
        copy.wait_send()
    for s in range(2):
        z_copy(s, 0, at.order(0)).wait_send()
        z_copy(s, 1, at.order(1)).wait_send()

        @pl.when(at.mid == 1)
        def _():
            z_copy(s, 2, at.order(2)).wait_send()
            z_pass(s, at.order(2), at.unmirror(0)).wait_send()

        for p in range(4):
            kv_copy(s, p).wait_send()
        for k in range(3):
            m_copy(s, k, (t + k + 1) % 4).wait_send()
    cargo_z(0, at.order(0)).wait_send()
    cargo_z(1, at.order(1)).wait_send()

    @pl.when(at.mid == 1)
    def _():
        cargo_z(2, at.order(2)).wait_send()
        cargo_pass(at.order(2), at.unmirror(0)).wait_send()

    for k in range(4):
        p = t if k == 0 else at.order(k - 1)
        cargo_plane(0, k, p, d, at.dx).wait_send()
        cargo_plane(1, k, p, d, at.dy).wait_send()

        @pl.when(p < 2)
        def _():
            cargo_plane(1, 4 + k, p, at.dx, at.dy).wait_send()

        @pl.when(p >= 2)
        def _():
            cargo_plane(0, 4 + k, p, at.dy, at.dx).wait_send()

    def finish(i, carry):
        shard, owner = i // 4, i % 4
        cargo_core(shard, owner).wait_send()
        cargo_keep(0, shard, owner).wait()
        cargo_keep(1, shard, owner).wait()
        return carry

    lax.fori_loop(0, 16, finish, 0)


def erf_parts(values):
    cdf = 0.5 * (1.0 + lax.erf(values * ROOT_HALF))
    return cdf, cdf + values * (jnp.exp(-0.5 * values * values) * INV_ROOT_TWO_PI)


def backward_kernel(
    hidden, cot, middle, normed_f, normed, queries, kv, mixed_in, wqkv, wout, weights, seg_k, seg_q,
    gain_a, gain_f, inner_bias, outer_bias,
    block_out, grad_input, g_ff, g_wo, g_qkv, small,
    ff, left, right, left_turn, grad_mid, branch, mixed_sib, g_mix_out, g_mix, part, rx1, rx2, rz,
    hide, k_turn, q_turn, acc_k, acc_v, kv_out, kv_in, dqkv, gna, rzn, normed_turn, qkv_sib,
    qkv_in, wide, sums, sums_core, sums_plane, sums_line, gb_turn,
    ff_sem, l_send, l_recv, r_send, r_recv, b_send, b_recv, x_send, x_recv, m_send, m_recv,
    p1_send, p1_recv, p2_send, p2_recv, z_send, z_recv, kv_send, kv_recv, n_send, n_recv,
    qs_send, qs_recv, qp_send, qp_recv, f_send, f_recv, s_send, s_recv,
):
    at = Place()
    d, c, t = at.d, at.c, at.t
    other = 1 - c

    def load(which, i):
        return pltpu.make_async_copy(weights.at[which, i], ff.at[i % 2, which], ff_sem.at[which, i])

    for i in range(2):
        load(0, i).start()
        load(1, i).start()
    greet(at)

    left[0, c] = normed_f[...].reshape(256, 768)
    left[1, c] = cot[...].reshape(256, 768).astype(BF)
    left_copy = remote(left.at[other, c], left.at[other, c], l_send.at[0], l_recv.at[0], ctx=other)
    left_copy.start()
    mixed_copy = remote(mixed_in, mixed_sib, x_send.at[0], x_recv.at[0], ctx=other)
    mixed_copy.start()
    sums[...] = jnp.zeros_like(sums)

    def right_copy(i):
        return remote(
            right.at[other, i, c], right.at[other, i, c], r_send.at[i], r_recv.at[i], ctx=other
        )

    def right_wait(i):
        return remote(right.at[c, i, other], right.at[c, i, other], r_send.at[i], r_recv.at[i], ctx=other)

    wide[...] = jnp.zeros_like(wide)

    def units(i, carry):
        slot = i % 2
        load(0, i).wait()
        load(1, i).wait()
        total = jnp.zeros((1, 768), F32)
        for half in range(2):
            rows = slice(half * 128, half * 128 + 128)
            inner = (
                jnp.dot(left[0, c, rows, :], ff[slot, 0], preferred_element_type=F32) + inner_bias[i]
            )
            cdf, slope = erf_parts(inner)
            active = (inner * cdf).astype(BF)
            right[1, i, c, rows, :] = active
            wide[rows, :] += dims(active, ff[slot, 1], 1, 1)
            grad_inner = (
                jnp.dot(left[1, c, rows, :], ff[slot, 1], preferred_element_type=F32) * slope
            ).astype(BF)
            right[0, i, c, rows, :] = grad_inner
            wide[256 + half * 128 : 384 + half * 128, :] += dims(grad_inner, ff[slot, 0], 1, 1)
            total = total + jnp.sum(grad_inner.astype(F32), axis=0, keepdims=True)
        sums[pl.ds(6 + i, 1), :] = total
        right_copy(i).start()

        @pl.when(i < 2)
        def _():
            load(0, i + 2).start()
            load(1, i + 2).start()

        return carry

    lax.fori_loop(0, 4, units, 0)

    def add_row(i, value):
        sums[i : i + 1, :] += jnp.sum(value, axis=0, keepdims=True)

    def norm_back(s, rows, source, grad_out, gain):
        scaled, inverse = norm_parts(source[s, rows, :])
        grad_scaled = grad_out * gain[...]
        plain = jnp.mean(grad_scaled, axis=-1, keepdims=True)
        cross = jnp.mean(grad_scaled * scaled, axis=-1, keepdims=True)
        return inverse * (grad_scaled - plain - scaled * cross), scaled

    for s in range(2):
        for half in range(2):
            rows = slice(half * 64, half * 64 + 64)
            flat = slice(s * 128 + half * 64, s * 128 + half * 64 + 64)
            block_out[s, rows, :] = middle[s, rows, :] + wide[flat, :] + outer_bias[...]
            grad_out = wide[256 + s * 128 + half * 64 : 320 + s * 128 + half * 64, :]
            grad_rows, scaled = norm_back(s, rows, middle, grad_out, gain_f)
            grad_rows = grad_rows + cot[s, rows, :]
            grad_mid[s, rows, :] = grad_rows
            branch[c, flat, :] = grad_rows.astype(BF)
            add_row(2, grad_out * scaled)
            add_row(3, grad_out)
            add_row(4, grad_rows)
            add_row(5, cot[s, rows, :])
    branch_copy = remote(branch.at[c], branch.at[c], b_send.at[0], b_recv.at[0], ctx=other)
    branch_copy.start()

    def m_copy(s, k, dest):
        return remote(g_mix_out.at[dest, s], g_mix.at[s, t], m_send.at[s, k], m_recv.at[s, t], tensor=dest)

    for p in range(4):
        g_mix_out[p] = jnp.dot(branch[c], wout[p], preferred_element_type=F32).astype(BF).reshape(
            2, 128, LANES
        )
    for s in range(2):
        for k in range(3):
            m_copy(s, k, (t + k + 1) % 4).start()
        g_mix[s, t] = g_mix_out[t, s]

    left_copy.wait_send()
    remote(left.at[c, other], left.at[c, other], l_send.at[0], l_recv.at[0], ctx=other).wait_recv()
    left_turn[...] = left[c].reshape(512, 768).T
    remote(branch.at[other], branch.at[other], b_send.at[0], b_recv.at[0], ctx=other).wait_recv()
    gb_turn[...] = branch[...].reshape(512, 768).T
    mixed_copy.wait_recv()

    def first(i):
        near, far = (at.dx, at.dy) if i < 2 else (at.dy, at.dx)
        return [
            remote(part.at[i, owner], rx1.at[i, j], p1_send.at[i, j], p1_recv.at[i, j], dp=near)
            for j, owner in enumerate((near, at.dd))
        ]

    def second(i):
        far = at.dy if i < 2 else at.dx
        return remote(part.at[i, far], rx2.at[i], p2_send.at[i], p2_recv.at[i], dp=far)

    for i in range(4):
        right_wait(i).wait_recv()
        both = right[c, i].reshape(512, 768)

        def rows_of(q, carry):
            start = pl.multiple_of(q * 192, 192)
            out = jnp.dot(left_turn[pl.ds(start, 192), :], both, preferred_element_type=F32)
            part[i, q, 0:192, :] = out.astype(BF)
            start = pl.multiple_of(q * 192 + c * 96, 96)
            turned = gb_turn[pl.ds(start, 96), :]
            here, there = turned[:, :256], turned[:, 256:]
            mine = mixed_in[i].reshape(256, LANES)
            sib = mixed_sib[i].reshape(256, LANES)
            low = jnp.where(c == 0, mine.astype(F32), sib.astype(F32)).astype(BF)
            high = jnp.where(c == 0, sib.astype(F32), mine.astype(F32)).astype(BF)
            out = jnp.dot(here, low, preferred_element_type=F32) + jnp.dot(
                there, high, preferred_element_type=F32
            )
            for j in range(3):
                part[i, q, 192:224, j * LANES : (j + 1) * LANES] = out[j * 32 : (j + 1) * 32, :].astype(BF)
            return carry

        lax.fori_loop(0, 4, rows_of, 0)
        for copy in first(i):
            copy.start()

    def add_block(ref, index, *others):
        def rows(q, carry):
            block = pl.ds(pl.multiple_of(q * 32, 32), 32)
            total = ref[index + (block, slice(None))].astype(F32)
            for o in others:
                total = total + o[block, :].astype(F32)
            ref[index + (block, slice(None))] = total.astype(BF)
            return carry

        lax.fori_loop(0, 7, rows, 0)

    def to_second(i):
        for copy in first(i):
            copy.wait_recv()
        far = at.dy if i < 2 else at.dx
        add_block(part, (i, far), rx1.at[i, 1])
        second(i).start()
        add_block(part, (i, d), rx1.at[i, 0])

    lane_head = lax.broadcasted_iota(jnp.int32, (1, LANES), 1) // HDIM

    def attend(s):
        keys_seg = jnp.broadcast_to(seg_k[s], (128, 1024)).T[:, :1]
        for b in range(2):
            hide[:, b * 256 : (b + 1) * 256] = jnp.where(
                keys_seg == seg_q[s, :, b * 256 : (b + 1) * 256], 0.0, HIDE
            ).astype(F32)
        k_turn[...] = kv[s].reshape(1024, 2 * LANES)[:, :LANES].T
        q_turn[192:, :] = jnp.zeros((64, 512), F32)
        acc_k[...] = jnp.zeros_like(acc_k)
        acc_v[...] = jnp.zeros_like(acc_v)

        def step(i, carry):
            h, b = i // 2, i % 2
            block = pl.ds(pl.multiple_of(b * 256, 256), 256)
            head = lane_head == h
            q_here = jnp.where(head, queries[s, block, :].astype(F32), 0.0).astype(BF)
            g_here = g_mix[s, pl.ds(b * 2, 2)].reshape(256, LANES)
            g_here = jnp.where(head, g_here.astype(F32), 0.0).astype(BF)
            both = kv[s].reshape(1024, 2 * LANES)
            scores = dims(both[:, :LANES], q_here, 1, 1) + hide[:, block]
            peak = jnp.max(scores, axis=0, keepdims=True)
            expo = jnp.exp(scores - peak)
            probs = expo * (1.0 / jnp.sum(expo, axis=0, keepdims=True))
            grad_probs = dims(both[:, LANES:], g_here, 1, 1)
            centre = jnp.sum(probs * grad_probs, axis=0, keepdims=True)
            acc_v[...] += jnp.dot(probs.astype(BF), g_here, preferred_element_type=F32)
            grad_scores = (probs * (grad_probs - centre)).astype(BF)
            acc_k[...] += jnp.dot(grad_scores, q_here, preferred_element_type=F32)
            rows = pl.ds(pl.multiple_of(h * HDIM, HDIM), HDIM)
            q_turn[rows, block] = jnp.dot(k_turn[rows, :], grad_scores, preferred_element_type=F32)
            return carry

        lax.fori_loop(0, 6, step, 0)
        dqkv[s, :, :LANES] = (q_turn[...].T * HDIM**-0.5).astype(BF)
        theirs = pl.ds(pl.multiple_of(other * 512, 512), 512)
        kv_out[s, :, :LANES] = acc_k[theirs, :].astype(BF)
        kv_out[s, :, LANES:] = acc_v[theirs, :].astype(BF)
        kv_copy(s).start()
        ours = pl.ds(pl.multiple_of(c * 512, 512), 512)
        dqkv[s, :, LANES : 2 * LANES] = acc_k[ours, :].astype(BF)
        dqkv[s, :, 2 * LANES :] = acc_v[ours, :].astype(BF)

    def kv_copy(s):
        return remote(kv_out.at[s], kv_in.at[s], kv_send.at[s], kv_recv.at[s], ctx=other)

    def line_sum(source, landing, send, recv):
        slot = 2 - at.mid
        return dict(
            near=lambda: remote(source(at.order(0)), landing(0), send(0), recv(0), tensor=at.order(0)),
            next=lambda: remote(source(at.order(1)), landing(slot), send(1), recv(slot), tensor=at.order(1)),
            far=lambda: remote(source(at.order(2)), landing(3), send(2), recv(3), tensor=at.order(0)),
            on=lambda: remote(source(at.order(2)), landing(1), send(2), recv(1), tensor=at.order(2)),
            got=lambda k: remote(landing(k), landing(k), send(0), recv(k), tensor=t),
        )

    def line_start(line):
        line["near"]().start()
        line["next"]().start()

        @pl.when(at.mid == 0)
        def _():
            line["far"]().start()

    def line_pass(line, add):
        @pl.when(at.mid == 1)
        def _():
            line["got"](3).wait_recv()
            add()
            line["on"]().start()

    def line_got(line):
        line["got"](0).wait_recv()
        line["got"](1).wait_recv()

        @pl.when(at.mid == 1)
        def _():
            line["got"](2).wait_recv()

    def line_end(line):
        line["near"]().wait_send()
        line["next"]().wait_send()

        @pl.when(at.mid == 0)
        def _():
            line["far"]().wait_send()

        @pl.when(at.mid == 1)
        def _():
            line["on"]().wait_send()

    rows_line = [
        line_sum(
            lambda p, s=s: gna.at[s, p], lambda k, s=s: rzn.at[s, k],
            lambda k, s=s: n_send.at[s, k], lambda k, s=s: n_recv.at[s, k],
        )
        for s in range(2)
    ]
    cargo_line = line_sum(
        lambda p: part.at[p, d], lambda k: rz.at[k], lambda k: z_send.at[k], lambda k: z_recv.at[k]
    )

    for s in range(2):
        for k in range(3):
            p = (t + k + 1) % 4
            remote(g_mix_out.at[p, s], g_mix.at[s, p], m_send.at[s, k], m_recv.at[s, p], tensor=p).wait_recv()
        attend(s)
        to_second(2 * s)

    for s in range(2):
        kv_copy(s).wait_recv()
        dqkv[s, :, LANES:] = (dqkv[s, :, LANES:].astype(F32) + kv_in[s].astype(F32)).astype(BF)
        for p in range(4):
            rows = dqkv[s, p * 128 : (p + 1) * 128, :]
            gna[s, p] = dims(rows, wqkv[...].reshape(768, 768), 1, 1).astype(BF)
            sums[pl.ds(12 + t, 1), :] += jnp.sum(rows.astype(F32), axis=0, keepdims=True)
        line_start(rows_line[s])

    to_second(1)
    to_second(3)

    normed_turn[...] = normed[...].reshape(1024, 768).T

    def qkv_rows(q, carry):
        start = pl.multiple_of(q * 96, 96)
        out = jnp.dot(
            normed_turn[pl.ds(start, 96), :], dqkv[...].reshape(1024, 768), preferred_element_type=F32
        )
        wide[pl.ds(start, 96), :] = out
        return carry

    lax.fori_loop(0, 8, qkv_rows, 0)
    for p in range(4):
        theirs = pl.ds(pl.multiple_of(p * 192 + other * 96, 96), 96)
        qkv_sib[0, p] = wide[theirs, :].astype(BF)
    sib_copy = remote(qkv_sib.at[0], qkv_sib.at[1], qs_send.at[0], qs_recv.at[0], ctx=other)
    sib_copy.start()

    for i in range(4):
        remote(rx2.at[i], rx2.at[i], p2_send.at[i], p2_recv.at[i], dp=d).wait_recv()
        add_block(part, (i, d), rx2.at[i])
    line_start(cargo_line)

    sib_copy.wait_recv()
    for p in range(4):
        ours = pl.ds(pl.multiple_of(p * 192 + c * 96, 96), 96)
        qkv_in[0, p] = (wide[ours, :] + qkv_sib[1, p].astype(F32)).astype(BF)
    planes = (at.dx, at.dy, at.dd)

    def plane_copy(k):
        return remote(qkv_in.at[0, planes[k]], qkv_in.at[1, d], qp_send.at[k], qp_recv.at[d], dp=planes[k])

    for k in range(3):
        plane_copy(k).start()
    qkv_in[1, d] = qkv_in[0, d]

    for s in range(2):
        def add_rows(s=s):
            gna[s, at.order(2)] = (gna[s, at.order(2)].astype(F32) + rzn[s, 3].astype(F32)).astype(BF)

        line_pass(rows_line[s], add_rows)
    line_pass(cargo_line, lambda: add_block(part, (at.order(2), d), rz.at[3]))

    for k in range(3):
        remote(qkv_in.at[0, planes[k]], qkv_in.at[1, planes[k]], qp_send.at[k], qp_recv.at[planes[k]], dp=d).wait_recv()
    total = qkv_in[1, 0].astype(F32)
    for p in range(1, 4):
        total = total + qkv_in[1, p].astype(F32)
    g_qkv[c] = total
    final = [remote(g_qkv.at[c], g_qkv.at[c], f_send.at[0], f_recv.at[0], ctx=other)]
    final[0].start()

    for s in range(2):
        line_got(rows_line[s])
        for half in range(2):
            rows = slice(half * 64, half * 64 + 64)
            grad_out = gna[s, t, rows, :].astype(F32) + rzn[s, 0, rows, :].astype(F32)
            grad_out = grad_out + rzn[s, 1, rows, :].astype(F32)
            third = rzn[s, 2, rows, :].astype(F32)
            grad_out = grad_out + jnp.where(at.mid == 1, third, jnp.zeros_like(third))
            grad_rows, scaled = norm_back(s, rows, hidden, grad_out, gain_a)
            grad_input[s, rows, :] = grad_mid[s, rows, :] + grad_rows
            add_row(0, grad_out * scaled)
            add_row(1, grad_out)

    core_sum = remote(sums, sums_core, s_send.at[0], s_recv.at[0], ctx=other)
    core_sum.start()

    line_got(cargo_line)
    for q in range(7):
        rows = slice(q * 32, q * 32 + 32)
        total = part[t, d, rows, :].astype(F32) + rz[0, rows, :].astype(F32) + rz[1, rows, :].astype(F32)
        third = rz[2, rows, :].astype(F32)
        total = total + jnp.where(at.mid == 1, third, jnp.zeros_like(third))
        if q < 6:
            g_ff[c, rows, :] = total
        else:
            g_wo[c] = total
    final.append(remote(g_ff.at[c], g_ff.at[c], f_send.at[1], f_recv.at[1], ctx=other))
    final.append(remote(g_wo.at[c], g_wo.at[c], f_send.at[2], f_recv.at[2], ctx=other))
    final[1].start()
    final[2].start()

    core_sum.wait()
    sums_plane[d] = sums[...] + sums_core[...]
    for k in range(3):
        remote(sums_plane.at[d], sums_plane.at[d], s_send.at[1 + k], s_recv.at[1 + d], dp=planes[k]).start()
    for k in range(3):
        remote(
            sums_plane.at[planes[k]], sums_plane.at[planes[k]], s_send.at[1 + k], s_recv.at[1 + planes[k]], dp=d
        ).wait_recv()
    sums_line[t] = (sums_plane[0] + sums_plane[1]) + (sums_plane[2] + sums_plane[3])
    for k in range(3):
        p = (t + k + 1) % 4
        remote(sums_line.at[t], sums_line.at[t], s_send.at[4 + k], s_recv.at[5 + t], tensor=p).start()
    for k in range(3):
        p = (t + k + 1) % 4
        remote(sums_line.at[p], sums_line.at[p], s_send.at[4 + k], s_recv.at[5 + p], tensor=p).wait_recv()
    small[...] = (sums_line[0] + sums_line[1]) + (sums_line[2] + sums_line[3])

    for k in range(3):
        remote(sums_plane.at[d], sums_plane.at[d], s_send.at[1 + k], s_recv.at[1 + d], dp=planes[k]).wait_send()
        p = (t + k + 1) % 4
        remote(sums_line.at[t], sums_line.at[t], s_send.at[4 + k], s_recv.at[5 + t], tensor=p).wait_send()
        plane_copy(k).wait_send()
    for i, ref in enumerate((g_qkv, g_ff, g_wo)):
        final[i].wait_send()
        remote(ref.at[other], ref.at[other], f_send.at[i], f_recv.at[i], ctx=other).wait_recv()
    sib_copy.wait_send()
    mixed_copy.wait_send()
    branch_copy.wait_send()
    for s in range(2):
        line_end(rows_line[s])
        kv_copy(s).wait_send()
        for k in range(3):
            m_copy(s, k, (t + k + 1) % 4).wait_send()
    line_end(cargo_line)
    for i in range(4):
        right_copy(i).wait_send()
        for copy in first(i):
            copy.wait_send()
        second(i).wait_send()


VM = pl.BlockSpec(memory_space=pltpu.VMEM)
ANY = pl.BlockSpec(memory_space=pl.ANY)


def forward_call(*operands):
    struct = jax.ShapeDtypeStruct
    dma = pltpu.SemaphoreType.DMA
    return pl.pallas_call(
        forward_kernel,
        out_shape=(
            struct((2, 4, 128, 768), BF),
            struct((2, 512, LANES), BF),
            struct((2, 2, 4, 128, 2 * LANES), BF),
            struct((4, 2, 128, LANES), BF),
            struct((2, 128, 768), F32),
            struct((2, 128, 768), BF),
            struct((4, 192, 768), BF),
            struct((4, 768, LANES), BF),
            struct((2, 4, 4, 192, 768), BF),
        ),
        in_specs=[VM] * len(operands),
        out_specs=(VM,) * 8 + (ANY,),
        scratch_shapes=[
            pltpu.VMEM((2, 4, 4, 224, 768), BF),
            pltpu.VMEM((1024, 512), F32),
            pltpu.VMEM((LANES, 1024), BF),
            pltpu.VMEM((LANES, 512), F32),
            pltpu.VMEM((2, 4, 128, LANES), BF),
            dma((2, 4)), dma((2, 4)),
            dma((3,)), dma((4,)),
            dma((2, 4)), dma((2, 4)),
            dma((2, 3)), dma((2, 4)),
            dma((4,)), dma((2, 8)), dma((4, 4)), dma((4, 4)), dma((4, 4)),
            dma((2,)), dma((2, 4, 4)),
        ],
        compiler_params=pltpu.CompilerParams(
            collective_id=1, has_side_effects=True, vmem_limit_bytes=56 << 20
        ),
        name="forward",
    )(*operands)


def backward_call(*operands):
    struct = jax.ShapeDtypeStruct
    dma = pltpu.SemaphoreType.DMA
    vm = pltpu.VMEM
    return pl.pallas_call(
        backward_kernel,
        out_shape=(
            struct((2, 128, 768), F32),
            struct((2, 128, 768), F32),
            struct((2, 192, 768), F32),
            struct((2, 32, 768), F32),
            struct((2, 96, 768), F32),
            struct((16, 768), F32),
        ),
        in_specs=[VM] * 10 + [ANY] + [VM] * (len(operands) - 11),
        out_specs=(VM,) * 6,
        scratch_shapes=[
            vm((2, 2, 768, 768), BF),
            vm((2, 2, 256, 768), BF),
            vm((2, 4, 2, 256, 768), BF),
            vm((768, 512), BF),
            vm((2, 128, 768), F32),
            vm((2, 256, 768), BF),
            vm((4, 2, 128, LANES), BF),
            vm((4, 2, 128, LANES), BF),
            vm((2, 4, 128, LANES), BF),
            vm((4, 4, 224, 768), BF),
            vm((4, 2, 224, 768), BF),
            vm((4, 224, 768), BF),
            vm((4, 224, 768), BF),
            vm((1024, 512), F32),
            vm((LANES, 1024), BF),
            vm((LANES, 512), F32),
            vm((1024, LANES), F32),
            vm((1024, LANES), F32),
            vm((2, 512, 2 * LANES), BF),
            vm((2, 512, 2 * LANES), BF),
            vm((2, 512, 768), BF),
            vm((2, 4, 128, 768), BF),
            vm((2, 4, 128, 768), BF),
            vm((768, 1024), BF),
            vm((2, 4, 96, 768), BF),
            vm((2, 4, 96, 768), BF),
            vm((768, 768), F32),
            vm((16, 768), F32),
            vm((16, 768), F32),
            vm((4, 16, 768), F32),
            vm((4, 16, 768), F32),
            vm((768, 512), BF),
            dma((2, 4)), dma((1,)), dma((1,)), dma((4,)), dma((4,)), dma((1,)), dma((1,)),
            dma((1,)), dma((1,)), dma((2, 3)), dma((2, 4)),
            dma((4, 2)), dma((4, 2)), dma((4,)), dma((4,)), dma((3,)), dma((4,)),
            dma((2,)), dma((2,)), dma((2, 3)), dma((2, 4)),
            dma((1,)), dma((1,)), dma((3,)), dma((4,)), dma((3,)), dma((3,)), dma((7,)), dma((9,)),
        ],
        compiler_params=pltpu.CompilerParams(
            collective_id=2, has_side_effects=True, vmem_limit_bytes=63 << 20
        ),
        name="backward",
    )(*operands)


def pad_heads(block):
    return jnp.pad(block, [(0, 0)] * (block.ndim - 1) + [(0, LANES - block.shape[-1])])


def body(
    hidden_in, cotangent, segment_ids, attn_gain, attn_shift, query_weight, key_weight,
    value_weight, query_bias, value_bias, output_weight, output_bias, ffn_gain, ffn_shift,
    inner_weight, inner_bias, outer_weight, outer_bias,
):
    part = query_weight.shape[1]
    tensor_at = lax.axis_index("tensor")
    ctx_at = lax.axis_index("ctx")
    wqkv_s = jnp.concatenate(
        [pad_heads(query_weight), pad_heads(key_weight), pad_heads(value_weight)], axis=1
    ).astype(BF)
    wout_s = pad_heads(output_weight.T.astype(BF))
    wout_half = lax.dynamic_slice_in_dim(wout_s, ctx_at * 96, 96)
    wout_half = wout_half.reshape(3, 32, LANES).transpose(1, 0, 2).reshape(32, 768)
    ff_s = jnp.where(ctx_at == 0, inner_weight, outer_weight.T).astype(BF)
    cargo_s = jnp.concatenate([ff_s, wout_half], axis=0)
    q_piece = lax.dynamic_slice_in_dim(query_bias, tensor_at * part, part)
    v_piece = lax.dynamic_slice_in_dim(value_bias, tensor_at * part, part)
    bias_s = jnp.concatenate(
        [pad_heads(q_piece), jnp.zeros((LANES,), F32), pad_heads(v_piece)]
    )[None, :]
    places = jnp.arange(segment_ids.shape[1], dtype=jnp.int32)[None, :]
    seg = jnp.where(segment_ids >= 0, segment_ids, -1 - places).astype(F32)
    seg_q = lax.dynamic_slice_in_dim(seg, ctx_at * 512, 512, axis=1)

    (normed, queries, kv, mixed_in, middle, normed_f, wqkv, wout, weights) = forward_call(
        hidden_in, attn_gain[None], attn_shift[None], wqkv_s, cargo_s, bias_s, output_bias[None],
        ffn_gain[None], ffn_shift[None], seg[:, None, :], seg_q[:, None, :],
    )
    (block_out, grad_input, g_ff, g_wo, g_qkv, small) = backward_call(
        hidden_in, cotangent, middle, normed_f, normed, queries, kv, mixed_in, wqkv, wout,
        weights.reshape(2, 4, 768, 768), seg[:, None, :], seg_q[:, None, :], attn_gain[None],
        ffn_gain[None], inner_bias.reshape(4, 1, 768), outer_bias[None],
    )
    g_qkv = g_qkv.reshape(192, 768)
    g_wo = g_wo.reshape(2, 32, 3, LANES).transpose(0, 2, 1, 3).reshape(192, LANES)
    heads = small[12:, :]
    return (
        block_out, grad_input, small[0], small[1],
        g_qkv[:, :part], g_qkv[:, LANES : LANES + part], g_qkv[:, 2 * LANES : 2 * LANES + part],
        heads[:, :part].reshape(-1), heads[:, 2 * LANES : 2 * LANES + part].reshape(-1),
        g_wo[:, :part].T, small[4], small[2], small[3], g_ff[0], small[6:10].reshape(-1),
        g_ff[1].T, small[5],
    )


root_half = 0.7071067811865476
inv_root_two_pi = 0.3989422804014327


def general_gate(values):
    return values * (0.5 * (1.0 + lax.erf(values * root_half)))


def general_slope(values):
    normal_cdf = 0.5 * (1.0 + lax.erf(values * root_half))
    normal_pdf = jnp.exp(-0.5 * values * values) * inv_root_two_pi
    return normal_cdf + values * normal_pdf


def general_norm(rows, gain, shift):
    centred = rows - jnp.mean(rows, axis=-1, keepdims=True)
    inverse = lax.rsqrt(jnp.mean(centred * centred, axis=-1, keepdims=True) + 1e-05)
    scaled = centred * inverse
    return (scaled * gain + shift, scaled, inverse)


def general_norm_backward(grad_out, scaled, inverse, gain):
    grad_scaled = grad_out * gain
    plain_mean = jnp.mean(grad_scaled, axis=-1, keepdims=True)
    cross_mean = jnp.mean(grad_scaled * scaled, axis=-1, keepdims=True)
    grad_rows = inverse * (grad_scaled - plain_mean - scaled * cross_mean)
    return (grad_rows, jnp.sum(grad_out * scaled, axis=0), jnp.sum(grad_out, axis=0))


def tensor_rows(block):
    return lax.all_gather(block, "tensor", axis=0, tiled=True)


def tensor_sums(block):
    return lax.psum_scatter(block, "tensor", scatter_dimension=0, tiled=True)


def fetch_weights(shards):
    return (
        lax.all_gather(shards[0], "dp", axis=0, tiled=True),
        lax.all_gather(shards[1], "dp", axis=0, tiled=True),
        lax.all_gather(shards[2], "dp", axis=0, tiled=True),
        lax.all_gather(shards[3], "dp", axis=0, tiled=True),
        lax.all_gather(shards[4], "dp", axis=1, tiled=True),
        lax.all_gather(shards[5], "dp", axis=1, tiled=True),
    )


def general_piece(piece, total, start):
    return lax.dynamic_update_slice(jnp.zeros((total,), jnp.float32), piece, (start,))


def general_body(
    hidden_in,
    cotangent,
    segment_ids,
    attn_gain,
    attn_shift,
    query_weight,
    key_weight,
    value_weight,
    query_bias,
    value_bias,
    output_weight,
    output_bias,
    ffn_gain,
    ffn_shift,
    inner_weight,
    inner_bias,
    outer_weight,
    outer_bias,
):
    width = hidden_in.shape[2]
    part_width = query_weight.shape[1]
    unit_width = inner_weight.shape[1]
    unit_total = inner_bias.shape[0]
    heads_here = part_width // HDIM
    tensor_at = lax.axis_index("tensor")
    ctx_at = lax.axis_index("ctx")
    half_rows = hidden_in.shape[1] * lax.axis_size("tensor")
    seq_rows = segment_ids.shape[1]
    factor = HDIM ** (-0.5)
    query_piece = lax.dynamic_slice_in_dim(query_bias, tensor_at * part_width, part_width)
    value_piece = lax.dynamic_slice_in_dim(value_bias, tensor_at * part_width, part_width)
    inner_piece = lax.dynamic_slice_in_dim(inner_bias, tensor_at * unit_width, unit_width)
    shards = (
        query_weight.astype(jnp.bfloat16),
        key_weight.astype(jnp.bfloat16),
        value_weight.astype(jnp.bfloat16),
        inner_weight.astype(jnp.bfloat16),
        output_weight.astype(jnp.bfloat16),
        outer_weight.astype(jnp.bfloat16),
    )
    key_index = jnp.arange(seq_rows)
    query_index = ctx_at * half_rows + jnp.arange(half_rows)

    def masked_scores(queries, key_all, allowed):
        scores = (
            jnp.einsum("qhd,khd->hqk", queries, key_all, preferred_element_type=jnp.float32)
            * factor
        )
        return jnp.where(allowed[None, :, :], scores, -1e30)

    def micro(weights_bf, carry, item):
        w_query, w_key, w_value, w_inner, w_output, w_outer = weights_bf
        rows, cot_rows, segment_row = item
        query_seg = lax.dynamic_slice_in_dim(segment_row, ctx_at * half_rows, half_rows)
        allowed = (query_seg[:, None] == segment_row[None, :]) & (
            (segment_row[None, :] >= 0) | (query_index[:, None] == key_index[None, :])
        )
        normed, scaled_a, inverse_a = general_norm(rows, attn_gain, attn_shift)
        normed_all = tensor_rows(normed.astype(jnp.bfloat16))
        queries = (
            jnp.dot(normed_all, w_query, preferred_element_type=jnp.float32) + query_piece
        ).astype(jnp.bfloat16)
        key_half = jnp.dot(normed_all, w_key, preferred_element_type=jnp.float32).astype(
            jnp.bfloat16
        )
        value_half = (
            jnp.dot(normed_all, w_value, preferred_element_type=jnp.float32) + value_piece
        ).astype(jnp.bfloat16)
        key_all, value_all = (
            lax.all_gather(key_half, "ctx", axis=0, tiled=True),
            lax.all_gather(value_half, "ctx", axis=0, tiled=True),
        )
        queries = queries.reshape(half_rows, heads_here, HDIM)
        key_all = key_all.reshape(seq_rows, heads_here, HDIM)
        value_all = value_all.reshape(seq_rows, heads_here, HDIM)
        masked = masked_scores(queries, key_all, allowed)
        peak = jnp.max(masked, axis=-1, keepdims=True)
        expo = jnp.exp(masked - peak)
        total = jnp.sum(expo, axis=-1, keepdims=True)
        log_total = peak + jnp.log(total)
        probs = (expo / total).astype(jnp.bfloat16)
        mixed = jnp.einsum("hqk,khd->qhd", probs, value_all, preferred_element_type=jnp.float32)
        mixed = mixed.reshape(half_rows, part_width).astype(jnp.bfloat16)
        branch_a = tensor_sums(jnp.dot(mixed, w_output, preferred_element_type=jnp.float32))
        middle = rows + branch_a + output_bias
        normed_f, scaled_f, inverse_f = general_norm(middle, ffn_gain, ffn_shift)
        normed_f_all = tensor_rows(normed_f.astype(jnp.bfloat16))
        inner = jnp.dot(normed_f_all, w_inner, preferred_element_type=jnp.float32) + inner_piece
        active = general_gate(inner).astype(jnp.bfloat16)
        branch_f = tensor_sums(jnp.dot(active, w_outer, preferred_element_type=jnp.float32))
        result_rows = middle + branch_f + outer_bias
        grad_up = tensor_rows(cot_rows.astype(jnp.bfloat16))
        grad_outer_w = jnp.einsum("tf,td->fd", active, grad_up, preferred_element_type=jnp.float32)
        grad_active = jnp.einsum("td,fd->tf", grad_up, w_outer, preferred_element_type=jnp.float32)
        grad_inner = (grad_active * general_slope(inner)).astype(jnp.bfloat16)
        grad_inner_w = jnp.einsum(
            "td,tf->df", normed_f_all, grad_inner, preferred_element_type=jnp.float32
        )
        grad_inner_b = jnp.sum(grad_inner.astype(jnp.float32), axis=0)
        grad_normed_f = tensor_sums(
            jnp.einsum("tf,df->td", grad_inner, w_inner, preferred_element_type=jnp.float32)
        )
        grad_rows_f, grad_ffn_g, grad_ffn_s = general_norm_backward(
            grad_normed_f, scaled_f, inverse_f, ffn_gain
        )
        grad_middle = cot_rows + grad_rows_f
        grad_branch = tensor_rows(grad_middle.astype(jnp.bfloat16))
        grad_output_w = jnp.einsum(
            "tc,td->cd", mixed, grad_branch, preferred_element_type=jnp.float32
        )
        grad_mixed = jnp.einsum(
            "td,cd->tc", grad_branch, w_output, preferred_element_type=jnp.float32
        )
        grad_mixed = grad_mixed.astype(jnp.bfloat16).reshape(half_rows, heads_here, HDIM)
        grad_probs = jnp.einsum(
            "qhd,khd->hqk", grad_mixed, value_all, preferred_element_type=jnp.float32
        )
        grad_value_part = jnp.einsum(
            "hqk,qhd->khd", probs, grad_mixed, preferred_element_type=jnp.float32
        )
        again = jnp.exp(masked_scores(queries, key_all, allowed) - log_total)
        centre = jnp.sum(again * grad_probs, axis=-1, keepdims=True)
        grad_scores = (again * (grad_probs - centre)).astype(jnp.bfloat16)
        grad_queries = (
            jnp.einsum("hqk,khd->qhd", grad_scores, key_all, preferred_element_type=jnp.float32)
            * factor
        )
        grad_queries = grad_queries.reshape(half_rows, part_width).astype(jnp.bfloat16)
        grad_key_part = (
            jnp.einsum("hqk,qhd->khd", grad_scores, queries, preferred_element_type=jnp.float32)
            * factor
        )
        grad_key_sum, grad_value_sum = (
            lax.psum_scatter(
                grad_key_part.reshape(seq_rows, part_width).astype(jnp.bfloat16),
                "ctx",
                scatter_dimension=0,
                tiled=True,
            ).astype(jnp.float32),
            lax.psum_scatter(
                grad_value_part.reshape(seq_rows, part_width).astype(jnp.bfloat16),
                "ctx",
                scatter_dimension=0,
                tiled=True,
            ).astype(jnp.float32),
        )
        grad_keys = grad_key_sum.astype(jnp.bfloat16)
        grad_values = grad_value_sum.astype(jnp.bfloat16)
        grad_query_w = jnp.einsum(
            "td,tc->dc", normed_all, grad_queries, preferred_element_type=jnp.float32
        )
        grad_key_w = jnp.einsum(
            "td,tc->dc", normed_all, grad_keys, preferred_element_type=jnp.float32
        )
        grad_value_w = jnp.einsum(
            "td,tc->dc", normed_all, grad_values, preferred_element_type=jnp.float32
        )
        grad_query_b = jnp.sum(grad_queries.astype(jnp.float32), axis=0)
        grad_value_b = jnp.sum(grad_values.astype(jnp.float32), axis=0)
        grad_normed_part = jnp.einsum(
            "tc,dc->td", grad_queries, w_query, preferred_element_type=jnp.float32
        )
        grad_normed_part = grad_normed_part + jnp.einsum(
            "tc,dc->td", grad_keys, w_key, preferred_element_type=jnp.float32
        )
        grad_normed_part = grad_normed_part + jnp.einsum(
            "tc,dc->td", grad_values, w_value, preferred_element_type=jnp.float32
        )
        grad_normed = tensor_sums(grad_normed_part)
        grad_rows_a, grad_attn_g, grad_attn_s = general_norm_backward(
            grad_normed, scaled_a, inverse_a, attn_gain
        )
        grad_rows = grad_middle + grad_rows_a
        big_sums, small_sums = carry
        big_sums = (
            big_sums[0] + grad_query_w,
            big_sums[1] + grad_key_w,
            big_sums[2] + grad_value_w,
            big_sums[3] + grad_inner_w,
            big_sums[4] + grad_output_w,
            big_sums[5] + grad_outer_w,
        )
        small_terms = (
            grad_attn_g,
            grad_attn_s,
            general_piece(grad_query_b, width, tensor_at * part_width),
            general_piece(grad_value_b, width, tensor_at * part_width),
            jnp.sum(grad_middle, axis=0),
            grad_ffn_g,
            grad_ffn_s,
            general_piece(grad_inner_b, unit_total, tensor_at * unit_width),
            jnp.sum(cot_rows, axis=0),
        )
        small_sums = tuple((old + new for old, new in zip(small_sums, small_terms)))
        return ((big_sums, small_sums), (result_rows, grad_rows))

    big_init = (
        jnp.zeros((width, part_width), jnp.float32),
        jnp.zeros((width, part_width), jnp.float32),
        jnp.zeros((width, part_width), jnp.float32),
        jnp.zeros((width, unit_width), jnp.float32),
        jnp.zeros((part_width, width), jnp.float32),
        jnp.zeros((unit_width, width), jnp.float32),
    )
    small_init = tuple((jnp.zeros((width,), jnp.float32) for index_small in range(7))) + (
        jnp.zeros((unit_total,), jnp.float32),
        jnp.zeros((width,), jnp.float32),
    )
    small_init = (
        small_init[0],
        small_init[1],
        small_init[2],
        small_init[3],
        small_init[4],
        small_init[5],
        small_init[6],
        small_init[7],
        small_init[8],
    )
    gathered = fetch_weights(shards)

    def scan_step(carry, item):
        return micro(gathered, carry, item)

    (big_sums, small_sums), (block_out, grad_input) = lax.scan(
        scan_step, (big_init, small_init), (hidden_in, cotangent, segment_ids)
    )
    paired = (
        lax.psum(big_sums[0].astype(jnp.bfloat16), "ctx").astype(jnp.float32),
        lax.psum(big_sums[1].astype(jnp.bfloat16), "ctx").astype(jnp.float32),
        lax.psum(big_sums[2].astype(jnp.bfloat16), "ctx").astype(jnp.float32),
        lax.psum(big_sums[3].astype(jnp.bfloat16), "ctx").astype(jnp.float32),
        lax.psum(big_sums[4].astype(jnp.bfloat16), "ctx").astype(jnp.float32),
        lax.psum(big_sums[5].astype(jnp.bfloat16), "ctx").astype(jnp.float32),
    )
    owned = (
        lax.psum_scatter(
            paired[0].astype(jnp.bfloat16), "dp", scatter_dimension=0, tiled=True
        ).astype(jnp.float32),
        lax.psum_scatter(
            paired[1].astype(jnp.bfloat16), "dp", scatter_dimension=0, tiled=True
        ).astype(jnp.float32),
        lax.psum_scatter(
            paired[2].astype(jnp.bfloat16), "dp", scatter_dimension=0, tiled=True
        ).astype(jnp.float32),
        lax.psum_scatter(
            paired[3].astype(jnp.bfloat16), "dp", scatter_dimension=0, tiled=True
        ).astype(jnp.float32),
        lax.psum_scatter(
            paired[4].astype(jnp.bfloat16), "dp", scatter_dimension=1, tiled=True
        ).astype(jnp.float32),
        lax.psum_scatter(
            paired[5].astype(jnp.bfloat16), "dp", scatter_dimension=1, tiled=True
        ).astype(jnp.float32),
    )
    small = lax.psum(
        (
            small_sums[0],
            small_sums[1],
            small_sums[2],
            small_sums[3],
            small_sums[4],
            small_sums[5],
            small_sums[6],
            small_sums[7],
            small_sums[8],
        ),
        ("dp", "ctx", "tensor"),
    )
    return (
        block_out,
        grad_input,
        small[0],
        small[1],
        owned[0],
        owned[1],
        owned[2],
        small[2],
        small[3],
        owned[4],
        small[4],
        small[5],
        small[6],
        owned[3],
        small[7],
        owned[5],
        small[8],
    )


SPECS = (
    P("dp", ("ctx", "tensor"), None), P("dp", ("ctx", "tensor"), None), P("dp", None), P(), P(),
    P("dp", "tensor"), P("dp", "tensor"), P("dp", "tensor"), P(), P(), P("tensor", "dp"), P(), P(),
    P(), P("dp", "tensor"), P(), P("tensor", "dp"), P(),
)
OUT_SPECS = (
    P("dp", ("ctx", "tensor"), None), P("dp", ("ctx", "tensor"), None), P(), P(),
    P("dp", "tensor"), P("dp", "tensor"), P("dp", "tensor"), P(), P(), P("tensor", "dp"), P(), P(),
    P(), P("dp", "tensor"), P(), P("tensor", "dp"), P(),
)


def solution(mesh):
    lined_up = mesh.shape["dp"] == 4 and mesh.shape["tensor"] == 4 and mesh.shape["ctx"] == 2
    return jax.shard_map(
        body if lined_up else general_body, mesh=mesh, in_specs=SPECS, out_specs=OUT_SPECS, check_vma=False
    )
```

```python
import functools

import jax
import jax.numpy as jnp
from jax import lax
from jax.experimental import pallas as pl
from jax.experimental.pallas import tpu as pltpu
from jax.sharding import PartitionSpec as P

HDIM = 64
LANES = 256
ROOT_HALF = 0.7071067811865476
INV_ROOT_TWO_PI = 0.3989422804014327
MESH = pl.DeviceIdType.MESH
BF = jnp.bfloat16
F32 = jnp.float32
HIDE = -1e30


def dims(left, right, a, b):
    return lax.dot_general(left, right, (((a,), (b,)), ((), ())), preferred_element_type=F32)


def norm_parts(rows):
    centred = rows - jnp.mean(rows, axis=-1, keepdims=True)
    inverse = lax.rsqrt(jnp.mean(centred * centred, axis=-1, keepdims=True) + 1e-05)
    return centred * inverse, inverse


class Place:
    def __init__(self):
        self.d = lax.axis_index("dp")
        self.c = lax.axis_index("ctx")
        self.t = lax.axis_index("tensor")
        col, row = self.d % 2, self.d // 2
        self.dx = row * 2 + (1 - col)
        self.dy = (1 - row) * 2 + col
        self.dd = (1 - row) * 2 + (1 - col)
        self.side = self.t // 2
        self.mid = self.t + self.side * (3 - 2 * self.t)

    def unmirror(self, place):
        return place + self.side * (3 - 2 * place)

    def order(self, k):
        if k == 0:
            return self.unmirror(1 - self.mid)
        return self.unmirror(k + 1)

    def order_at(self, k):
        first = 1 - jnp.minimum(k, 1)
        near = first * (1 - self.mid) + (1 - first) * (k + 1)
        own = jnp.minimum(k, 0)
        return -own * self.t + (1 + own) * self.unmirror(near)


def remote(src, dst, send, recv, **where):
    return pltpu.make_async_remote_copy(
        src_ref=src, dst_ref=dst, send_sem=send, recv_sem=recv, device_id=where, device_id_type=MESH
    )


def greet(place):
    barrier = pltpu.get_barrier_semaphore()
    for k in range(1, 4):
        pl.semaphore_signal(
            barrier, inc=1, device_id={"tensor": (place.t + k) % 4}, device_id_type=MESH
        )
    for peer in (place.dx, place.dy, place.dd):
        pl.semaphore_signal(barrier, inc=1, device_id={"dp": peer}, device_id_type=MESH)
    pl.semaphore_signal(barrier, inc=1, device_id={"ctx": 1 - place.c}, device_id_type=MESH)
    return lambda: pl.semaphore_wait(barrier, 7)


class Several:
    def __init__(self, *copies):
        self.copies = copies

    def start(self):
        for copy in self.copies:
            copy.start()

    def wait_send(self):
        for copy in self.copies:
            copy.wait_send()

    def wait_recv(self):
        for copy in self.copies:
            copy.wait_recv()


def rows_at(start, size, step):
    return pl.ds(pl.multiple_of(start, step), size)


def erf_parts(values):
    cdf = 0.5 * (1.0 + lax.erf(values * ROOT_HALF))
    return cdf, cdf + values * (jnp.exp(-0.5 * values * values) * INV_ROOT_TWO_PI)


def layer_kernel(
    hidden, cot, seg, gain_a, shift_a, wq_s, wk_s, wv_s, bias_q, bias_v, wo_s, bias_o, gain_f, shift_f,
    win_s, bias_in, wout_s, bias_out,
    block_out, grad_input, g_gain_a, g_shift_a, g_wq, g_wk, g_wv, g_bias_q, g_bias_v, g_wo, g_bias_o,
    g_gain_f, g_shift_f, g_win, g_bias_in, g_wout, g_bias_out,
    normed, normed_turn, queries, kv, mixed_in, mixed_sib, wqkv, wout, ffw, turn, q_turn, mixed, g_mix,
    keys_seg, left, left_in, left_turn, right, right_in, branch, branch_turn, part_wo, rx1, rx2, rz,
    rx1w, rx2w, rzw, wide, kv_out, kv_in, dqkv, gna, rzn, qkv_sib, qkv_in, sums, sums_core, sums_plane,
    sums_line, res_ff, res_wo, res_qkv, bias_row, inner_rows,
    q_send, q_recv, qc_send, qc_recv, z_send, z_recv, kvf_send, kvf_recv, mf_send, mf_recv,
    cz_send, cp_send, cc_send, c_recv, s_recv,
    l_send, l_recv, r_send, r_recv, b_send, b_recv, x_send, x_recv, m_send, m_recv,
    p1_send, p1_recv, p2_send, p2_recv, w1_send, w1_recv, zz_send, zz_recv, kv_send, kv_recv,
    n_send, n_recv, qs_send, qs_recv, qp_send, qp_recv, f_send, f_recv, s_send, sum_recv,
):
    at = Place()
    d, c, t = at.d, at.c, at.t
    other = 1 - c
    planes = (at.dx, at.dy, at.dd)
    others = [(t + k + 1) % 4 for k in range(3)]
    arrive = greet(at)

    for ref, start in ((wq_s, 0), (wk_s, LANES), (wv_s, 2 * LANES)):
        wqkv[d, :, start + 128 : start + 256] = jnp.zeros((192, 128), BF)
        wqkv[d, :, start : start + 192] = ref[...].astype(BF)
    arrive()

    def q_copy(i):
        half = wqkv.at[d, rows_at(c * 96, 96, 96)]
        return remote(half, half, q_send.at[i], q_recv.at[d], dp=planes[i])

    for i in range(3):
        q_copy(i).start()

    scaled, _ = norm_parts(hidden[0])
    normed[0, t] = (scaled * gain_a[...].reshape(1, 768) + shift_a[...].reshape(1, 768)).astype(BF)

    def z_copy(s, k):
        return remote(normed.at[s, t], normed.at[s, t], z_send.at[s, k], z_recv.at[s, t], tensor=at.order(k))

    def z_pass(s, shard):
        block = normed.at[s, shard]
        return remote(block, block, z_send.at[s, 3], z_recv.at[s, shard], tensor=at.unmirror(0))

    def z_start(s):
        z_copy(s, 0).start()
        z_copy(s, 1).start()

        @pl.when(at.mid == 1)
        def _():
            z_copy(s, 2).start()

    z_start(0)

    here = rows_at(d * 192, 192, 192)

    @pl.when(c == 0)
    def _():
        ffw[0, t, here, :] = win_s[...].astype(BF)

    @pl.when(c == 1)
    def _():
        ffw[1, t, here, :] = wout_s[...].astype(BF)

    turned = wo_s[...].T
    turned = jnp.where(c == 0, turned[:96], turned[96:]).astype(BF)
    here = rows_at(d * 192 + c * 96, 96, 96)
    wout[t, here, 128:256] = jnp.zeros((96, 128), BF)
    wout[t, here, 0:192] = turned

    def ff_block(which, shard, owner):
        return ffw.at[which, shard, rows_at(owner * 192, 192, 192)]

    def wo_block(which, shard, owner):
        return wout.at[shard, rows_at(owner * 192 + which * 96, 96, 96)]

    def carry_to(shard, owner, send, **where):
        f, w = ff_block(c, shard, owner), wo_block(c, shard, owner)
        return Several(
            remote(w, w, send.at[1], c_recv.at[shard, owner, 1], **where),
            remote(f, f, send.at[0], c_recv.at[shard, owner, 0], **where),
        )

    def cargo_z(k):
        return carry_to(t, d, cz_send.at[k], tensor=at.order(k))

    def cargo_pass(shard):
        return carry_to(shard, d, cz_send.at[3], tensor=at.unmirror(0))

    def cargo_plane(axis, k, shard, owner, dest):
        return carry_to(shard, owner, cp_send.at[axis, k], dp=dest)

    def cargo_core(shard, owner):
        f, w = ff_block(c, shard, owner), wo_block(c, shard, owner)
        return Several(
            remote(w, w, cc_send.at[shard, owner, 1], s_recv.at[shard, owner, 1], ctx=other),
            remote(f, f, cc_send.at[shard, owner, 0], s_recv.at[shard, owner, 0], ctx=other),
        )

    def arrived(shard, owner):
        carry_to(shard, owner, cz_send.at[0], dp=d).wait_recv()

    def from_sibling(shard, owner):
        f, w = ff_block(other, shard, owner), wo_block(other, shard, owner)
        Several(
            remote(w, w, cc_send.at[shard, owner, 1], s_recv.at[shard, owner, 1], ctx=other),
            remote(f, f, cc_send.at[shard, owner, 0], s_recv.at[shard, owner, 0], ctx=other),
        ).wait_recv()

    def spread(k, shard):
        cargo_plane(0, k, shard, d, at.dx).start()
        cargo_plane(1, k, shard, d, at.dy).start()
        cargo_core(shard, d).start()

    def diag_of(k, shard, act):
        @pl.when(shard < 2)
        def _():
            act(cargo_plane(1, 4 + k, shard, at.dx, at.dy))

        @pl.when(shard >= 2)
        def _():
            act(cargo_plane(0, 4 + k, shard, at.dy, at.dx))

    def diag(k, shard):
        arrived(shard, at.dx)
        arrived(shard, at.dy)
        diag_of(k, shard, lambda copy: copy.start())
        cargo_core(shard, at.dx).start()
        cargo_core(shard, at.dy).start()

    spread(0, t)
    cargo_z(0).start()
    cargo_z(1).start()

    @pl.when(at.mid == 1)
    def _():
        cargo_z(2).start()

    scaled, _ = norm_parts(hidden[1])
    normed[1, t] = (scaled * gain_a[...].reshape(1, 768) + shift_a[...].reshape(1, 768)).astype(BF)
    left[1] = cot[...].reshape(256, 768).astype(BF)
    sums[...] = jnp.zeros_like(sums)
    wide[...] = jnp.zeros_like(wide)
    bias_row[...] = jnp.zeros_like(bias_row)
    for p in range(4):

        @pl.when(t == p)
        def _(p=p):
            bias_row[:, 0:192] = bias_q[...].reshape(1, 768)[:, p * 192 : (p + 1) * 192]
            bias_row[:, 512:704] = bias_v[...].reshape(1, 768)[:, p * 192 : (p + 1) * 192]

        inner_rows[p] = bias_in[...].reshape(1, 3072)[:, p * 768 : (p + 1) * 768]

    def seg_rows(s):
        row = seg[s : s + 1, :]
        places = lax.broadcasted_iota(jnp.int32, (1, 1024), 1)
        return jnp.where(row >= 0, row, -1 - places).astype(F32)

    def seg_query(s):
        row = seg_rows(s)
        return jnp.where(c == 0, row[:, :512], row[:, 512:])

    def q_core(i):
        half = wqkv.at[planes[i], rows_at(c * 96, 96, 96)]
        return remote(half, half, qc_send.at[i], qc_recv.at[i], ctx=other)

    for i in range(3):
        half = wqkv.at[planes[i], rows_at(c * 96, 96, 96)]
        remote(half, half, q_send.at[i], q_recv.at[planes[i]], dp=d).wait_recv()
        q_core(i).start()
    for i in range(3):
        half = wqkv.at[planes[i], rows_at(other * 96, 96, 96)]
        remote(half, half, qc_send.at[i], qc_recv.at[i], ctx=other).wait_recv()

    def kvf_copy(s, p):
        return remote(kv.at[s, c, p], kv.at[s, c, p], kvf_send.at[s, p], kvf_recv.at[s, p], ctx=other)

    def project(s):
        def step(k, carry):
            p = at.order_at(k - 1)

            @pl.when(k > 0)
            def _():
                block = normed.at[s, p]
                remote(block, block, z_send.at[s, 0], z_recv.at[s, p], tensor=p).wait_recv()

            @pl.when((k == 3) & (at.mid == 1))
            def _():
                z_pass(s, p).start()

            out = jnp.dot(normed[s, p], wqkv[...].reshape(768, 768), preferred_element_type=F32)
            out = (out + bias_row[...]).astype(BF)
            queries[s, rows_at(p * 128, 128, 128), :] = out[:, :LANES] * jnp.asarray(HDIM**-0.5, BF)
            kv[s, c, p] = out[:, LANES:]
            kvf_copy(s, p).start()
            return carry

        lax.fori_loop(0, 4, step, 0)

    lane_head = lax.broadcasted_iota(jnp.int32, (1, LANES), 1) // HDIM

    def masked_scores(s, b, q_here):
        seg_here = seg_query(s)
        seg_here = jnp.where(b == 0, seg_here[:, :256], seg_here[:, 256:])
        keys = kv[s].reshape(1024, 2 * LANES)[:, :LANES]
        scores = dims(keys, q_here, 1, 1)
        column = keys_seg[...]
        visible = jnp.concatenate([column, column], axis=1) == seg_here
        return jnp.where(visible, scores, HIDE)

    def one_head(h, block):
        return jnp.where(lane_head == h, block.astype(F32), 0.0).astype(BF)

    def attend(s):
        for p in range(4):
            block = kv.at[s, other, p]
            remote(block, block, kvf_send.at[s, p], kvf_recv.at[s, p], ctx=other).wait_recv()
        keys_seg[...] = jnp.broadcast_to(seg_rows(s), (128, 1024)).T
        turn[...] = kv[s].reshape(1024, 2 * LANES)[:, LANES:].T
        q_turn[192:, :] = jnp.zeros((64, 512), F32)

        def step(i, carry):
            h, b = i // 2, i % 2
            block = rows_at(b * 256, 256, 256)
            scores = masked_scores(s, b, one_head(h, queries[s, block, :]))
            peak = jnp.max(scores, axis=0, keepdims=True)
            expo = jnp.exp(scores - peak)
            total = jnp.sum(expo, axis=0, keepdims=True)
            rows = rows_at(h * HDIM, HDIM, HDIM)
            turned = jnp.dot(turn[rows, :], expo.astype(BF), preferred_element_type=F32)
            q_turn[rows, block] = turned / total
            return carry

        lax.fori_loop(0, 6, step, 0)
        mixed[:, s] = q_turn[...].T.astype(BF).reshape(4, 128, LANES)
        for k in range(3):
            mf_copy(s, k).start()
        mixed_in[t, s] = mixed[t, s]

    def mf_copy(s, k):
        dest = others[k]
        return remote(mixed.at[dest, s], mixed_in.at[t, s], mf_send.at[s, k], mf_recv.at[s, t], tensor=dest)

    project(0)
    z_start(1)
    arrived(at.order(0), d)
    spread(1, at.order(0))
    diag(0, t)
    attend(0)
    arrived(at.order(1), d)
    spread(2, at.order(1))
    diag(1, at.order(0))
    arrived(at.order(2), d)

    @pl.when(at.mid == 1)
    def _():
        cargo_pass(at.order(2)).start()

    spread(3, at.order(2))
    diag(2, at.order(1))
    project(1)
    attend(1)
    diag(3, at.order(2))
    normed_turn[...] = normed[...].reshape(1024, 768).T
    for k in range(4):
        p = t if k == 0 else at.order(k - 1)
        arrived(p, at.dd)
        cargo_core(p, at.dd).start()

    def all_from_sibling(i, carry):
        from_sibling(i // 4, i % 4)
        return carry

    lax.fori_loop(0, 16, all_from_sibling, 0)
    for s in range(2):
        for k in range(3):
            p = others[k]
            block = mixed_in.at[p, s]
            remote(block, block, mf_send.at[s, k], mf_recv.at[s, p], tensor=p).wait_recv()
        total = hidden[s] + bias_o[...].reshape(1, 768)
        for p in range(4):
            total = total + dims(mixed_in[p, s], wout[p], 1, 1)
        block_out[s] = total
        scaled, _ = norm_parts(total)
        left[0, s * 128 : (s + 1) * 128, :] = (
            scaled * gain_f[...].reshape(1, 768) + shift_f[...].reshape(1, 768)
        ).astype(BF)

    left_copy = remote(left.at[other], left_in, l_send.at[0], l_recv.at[0], ctx=other)
    left_copy.start()
    mixed_copy = remote(mixed_in, mixed_sib, x_send.at[0], x_recv.at[0], ctx=other)
    mixed_copy.start()

    for i in range(3):
        q_copy(i).wait_send()
        q_core(i).wait_send()
    for s in range(2):
        z_copy(s, 0).wait_send()
        z_copy(s, 1).wait_send()

        @pl.when(at.mid == 1)
        def _(s=s):
            z_copy(s, 2).wait_send()
            z_pass(s, at.order(2)).wait_send()

        for p in range(4):
            kvf_copy(s, p).wait_send()
        for k in range(3):
            mf_copy(s, k).wait_send()
    cargo_z(0).wait_send()
    cargo_z(1).wait_send()

    @pl.when(at.mid == 1)
    def _():
        cargo_z(2).wait_send()
        cargo_pass(at.order(2)).wait_send()

    for k in range(4):
        p = t if k == 0 else at.order(k - 1)
        cargo_plane(0, k, p, d, at.dx).wait_send()
        cargo_plane(1, k, p, d, at.dy).wait_send()
        diag_of(k, p, lambda copy: copy.wait_send())

    def handed_over(i, carry):
        cargo_core(i // 4, i % 4).wait_send()
        return carry

    lax.fori_loop(0, 16, handed_over, 0)

    left_turn[0] = left[c].T
    left_copy.wait_recv()
    left_turn[1] = left_in[...].T

    def right_copy(i):
        return remote(right.at[other, i % 2], right_in.at[i], r_send.at[i], r_recv.at[i], ctx=other)

    def near_far(i):
        near = at.dx + (i // 2) * (at.dy - at.dx)
        return near, at.dx + at.dy - near

    def first_ff(i, j):
        near, _ = near_far(i)
        owner = near if j == 0 else at.dd
        return remote(ff_block(0, i, owner), rx1.at[i, j], p1_send.at[i, j], p1_recv.at[i, j], dp=near)

    def first_wo(i, j):
        near, _ = near_far(i)
        owner = near if j == 0 else at.dd
        block = part_wo.at[i, rows_at(owner * 192 + c * 96, 96, 96)]
        return remote(block, rx1w.at[i, j], w1_send.at[i, j], w1_recv.at[i, j], dp=near)

    def weight_gradient(i):
        right_copy(i).wait_recv()

        def rows_of(q, carry):
            rows = rows_at(q * 192, 192, 192)
            out = jnp.dot(left_turn[0, rows, :], right[c, i % 2], preferred_element_type=F32)
            out = out + jnp.dot(left_turn[1, rows, :], right_in[i], preferred_element_type=F32)
            ffw[0, i, rows, :] = out.astype(BF)
            return carry

        lax.fori_loop(0, 4, rows_of, 0)
        first_ff(i, 0).start()
        first_ff(i, 1).start()

    def units(i, carry):
        @pl.when(i >= 2)
        def _():
            right_copy(i - 2).wait_send()

        for j in range(3):
            cols = slice(j * 256, (j + 1) * 256)
            w_in, w_out = ffw[0, i, :, cols], ffw[1, i, :, cols]
            inner = jnp.dot(left[0], w_in, preferred_element_type=F32) + inner_rows[i, :, cols]
            cdf, slope = erf_parts(inner)
            active = (inner * cdf).astype(BF)
            right[1, i % 2, :, cols] = active
            grad_inner = jnp.dot(left[1], w_out, preferred_element_type=F32) * slope
            grad_inner = grad_inner.astype(BF)
            right[0, i % 2, :, cols] = grad_inner
            sums[pl.ds(6 + i, 1), cols] = jnp.sum(grad_inner.astype(F32), axis=0, keepdims=True)
            up, down = dims(active, w_out, 1, 1), dims(grad_inner, w_in, 1, 1)
            for k in range(3):
                wide[k, 0:256, :] += up[:, k * 256 : (k + 1) * 256]
                wide[k, 256:512, :] += down[:, k * 256 : (k + 1) * 256]
        right_copy(i).start()

        @pl.when(i > 0)
        def _():
            weight_gradient(i - 1)

        return carry

    lax.fori_loop(0, 4, units, 0)

    def add_row(i, value):
        sums[i : i + 1, :] += jnp.sum(value, axis=0, keepdims=True)

    def norm_back(source, grad_out, gain):
        scaled, inverse = norm_parts(source)
        grad_scaled = grad_out * gain[...].reshape(1, 768)
        plain = jnp.mean(grad_scaled, axis=-1, keepdims=True)
        cross = jnp.mean(grad_scaled * scaled, axis=-1, keepdims=True)
        return inverse * (grad_scaled - plain - scaled * cross), scaled

    def wide_rows(start):
        return jnp.concatenate([wide[k, start : start + 64, :] for k in range(3)], axis=1)

    for s in range(2):
        for half in range(2):
            rows = slice(half * 64, half * 64 + 64)
            start = s * 128 + half * 64
            middle = block_out[s, rows, :]
            cot_here = cot[s, rows, :]
            grad_out = wide_rows(256 + start)
            grad_rows, scaled = norm_back(middle, grad_out, gain_f)
            grad_rows = grad_rows + cot_here
            grad_input[s, rows, :] = grad_rows
            branch[0, start : start + 64, :] = grad_rows.astype(BF)
            block_out[s, rows, :] = middle + wide_rows(start) + bias_out[...].reshape(1, 768)
            add_row(2, grad_out * scaled)
            add_row(3, grad_out)
            add_row(4, grad_rows)
            add_row(5, cot_here)
    branch_copy = remote(branch.at[0], branch.at[1], b_send.at[0], b_recv.at[0], ctx=other)
    branch_copy.start()

    def m_copy(s, k):
        dest = others[k]
        return remote(mixed.at[dest, s], g_mix.at[s, t], m_send.at[s, k], m_recv.at[s, t], tensor=dest)

    for p in range(4):
        mixed[p] = jnp.dot(branch[0], wout[p], preferred_element_type=F32).astype(BF).reshape(2, 128, LANES)
    for s in range(2):
        for k in range(3):
            m_copy(s, k).start()
        g_mix[s, t] = mixed[t, s]
    weight_gradient(3)

    branch_turn[0] = branch[0].T
    branch_copy.wait_recv()
    branch_turn[1] = branch[1].T
    mixed_copy.wait_recv()

    def wo_gradient(i, carry):
        out = jnp.dot(branch_turn[0], mixed_in[i].reshape(256, LANES), preferred_element_type=F32)
        out = out + jnp.dot(branch_turn[1], mixed_sib[i].reshape(256, LANES), preferred_element_type=F32)
        part_wo[i] = out.astype(BF)
        first_wo(i, 0).start()
        first_wo(i, 1).start()
        return carry

    lax.fori_loop(0, 4, wo_gradient, 0)

    def add_to(target, *terms):
        total = target[...].astype(F32)
        for term in terms:
            total = total + term[...].astype(F32)
        target[...] = total.astype(BF)

    def wo_part(i, owner):
        return part_wo.at[i, rows_at(owner * 192 + c * 96, 96, 96)]

    def second(i):
        _, far = near_far(i)
        return Several(
            remote(ff_block(0, i, far), rx2.at[i], p2_send.at[i, 0], p2_recv.at[i, 0], dp=far),
            remote(wo_part(i, far), rx2w.at[i], p2_send.at[i, 1], p2_recv.at[i, 1], dp=far),
        )

    def to_second(i):
        for j in range(2):
            first_ff(i, j).wait_recv()
            first_wo(i, j).wait_recv()
        _, far = near_far(i)
        add_to(ff_block(0, i, far), rx1.at[i, 1])
        add_to(wo_part(i, far), rx1w.at[i, 1])
        second(i).start()
        add_to(ff_block(0, i, d), rx1.at[i, 0])
        add_to(wo_part(i, d), rx1w.at[i, 0])

    acc_k, acc_v = wide.at[0], wide.at[1]

    def attend_back(s):
        for k in range(3):
            p = others[k]
            block = g_mix.at[s, p]
            remote(block, block, m_send.at[s, k], m_recv.at[s, p], tensor=p).wait_recv()
        keys_seg[...] = jnp.broadcast_to(seg_rows(s), (128, 1024)).T
        turn[...] = kv[s].reshape(1024, 2 * LANES)[:, :LANES].T
        q_turn[192:, :] = jnp.zeros((64, 512), F32)
        acc_k[...] = jnp.zeros((1024, LANES), F32)
        acc_v[...] = jnp.zeros((1024, LANES), F32)

        def step(i, carry):
            h, b = i // 2, i % 2
            block = rows_at(b * 256, 256, 256)
            q_here = one_head(h, queries[s, block, :])
            g_here = one_head(h, g_mix[s, pl.ds(b * 2, 2)].reshape(256, LANES))
            scores = masked_scores(s, b, q_here)
            peak = jnp.max(scores, axis=0, keepdims=True)
            expo = jnp.exp(scores - peak)
            probs = expo * (1.0 / jnp.sum(expo, axis=0, keepdims=True))
            grad_probs = dims(kv[s].reshape(1024, 2 * LANES)[:, LANES:], g_here, 1, 1)
            centre = jnp.sum(probs * grad_probs, axis=0, keepdims=True)
            acc_v[...] += jnp.dot(probs.astype(BF), g_here, preferred_element_type=F32)
            grad_scores = (probs * (grad_probs - centre)).astype(BF)
            acc_k[...] += jnp.dot(grad_scores, q_here, preferred_element_type=F32)
            rows = rows_at(h * HDIM, HDIM, HDIM)
            q_turn[rows, block] = jnp.dot(turn[rows, :], grad_scores, preferred_element_type=F32)
            return carry

        lax.fori_loop(0, 6, step, 0)
        theirs = rows_at(other * 512, 512, 512)
        kv_out[s, :, :LANES] = acc_k[theirs, :].astype(BF)
        kv_out[s, :, LANES:] = acc_v[theirs, :].astype(BF)
        kv_copy(s).start()
        dqkv[s, :, :LANES] = (q_turn[...].T * HDIM**-0.5).astype(BF)
        ours = rows_at(c * 512, 512, 512)
        dqkv[s, :, LANES : 2 * LANES] = acc_k[ours, :].astype(BF)
        dqkv[s, :, 2 * LANES :] = acc_v[ours, :].astype(BF)

    def kv_copy(s):
        return remote(kv_out.at[s], kv_in.at[s], kv_send.at[s], kv_recv.at[s], ctx=other)

    class LineSum:
        def __init__(self, *parts):
            self.parts = parts

        def copies(self, owner, slot, k, dest):
            return Several(*[
                remote(source(owner), landing.at[slot], send.at[k], recv.at[slot], tensor=dest)
                for source, landing, send, recv in self.parts
            ])

        def near(self):
            return self.copies(at.order(0), 0, 0, at.order(0))

        def next(self):
            return self.copies(at.order(1), 2 - at.mid, 1, at.order(1))

        def far(self):
            return self.copies(at.order(2), 3, 2, at.order(0))

        def on(self):
            return self.copies(at.order(2), 1, 2, at.order(2))

        def got(self, slot):
            self.copies(t, slot, 0, t).wait_recv()

        def start(self):
            @pl.when(at.mid == 0)
            def _():
                self.far().start()

            self.near().start()
            self.next().start()

        def pass_on(self):
            @pl.when(at.mid == 1)
            def _():
                self.got(3)
                for source, landing, _, _ in self.parts:
                    add_to(source(at.order(2)), landing.at[3])
                self.on().start()

        def collect(self):
            self.got(0)
            self.got(1)

            @pl.when(at.mid == 1)
            def _():
                self.got(2)

        def end(self):
            self.near().wait_send()
            self.next().wait_send()

            @pl.when(at.mid == 0)
            def _():
                self.far().wait_send()

            @pl.when(at.mid == 1)
            def _():
                self.on().wait_send()

    rows_line = [
        LineSum((lambda p, s=s: gna.at[s, p], rzn.at[s], n_send.at[s], n_recv.at[s])) for s in range(2)
    ]
    cargo_line = LineSum(
        (lambda p: ff_block(0, p, d), rz, zz_send.at[0], zz_recv.at[0]),
        (lambda p: wo_part(p, d), rzw, zz_send.at[1], zz_recv.at[1]),
    )

    def rows_back(s):
        kv_copy(s).wait_recv()
        dqkv[s, :, LANES:] = (dqkv[s, :, LANES:].astype(F32) + kv_in[s].astype(F32)).astype(BF)
        for p in range(4):
            rows = dqkv[s, p * 128 : (p + 1) * 128, :]
            gna[s, p] = dims(rows, wqkv[...].reshape(768, 768), 1, 1).astype(BF)
            sums[pl.ds(12 + t, 1), :] += jnp.sum(rows.astype(F32), axis=0, keepdims=True)
        rows_line[s].start()

    attend_back(0)
    to_second(0)
    to_second(2)
    rows_back(0)
    attend_back(1)
    to_second(1)
    to_second(3)
    rows_back(1)
    rows_line[0].pass_on()

    def qkv_rows(q, carry):
        rows = rows_at(q * 192, 192, 192)
        out = jnp.dot(normed_turn[rows, :], dqkv[...].reshape(1024, 768), preferred_element_type=F32)
        for k in range(3):
            wide[k, rows, :] = out[:, k * 256 : (k + 1) * 256]
        return carry

    lax.fori_loop(0, 4, qkv_rows, 0)
    for p in range(4):
        theirs = rows_at(p * 192 + other * 96, 96, 96)
        for k in range(3):
            qkv_sib[0, p, :, k * 256 : (k + 1) * 256] = wide[k, theirs, :].astype(BF)
    sib_copy = remote(qkv_sib.at[0], qkv_sib.at[1], qs_send.at[0], qs_recv.at[0], ctx=other)
    sib_copy.start()

    for i in range(4):
        second(i).wait_recv()
        add_to(ff_block(0, i, d), rx2.at[i])
        add_to(wo_part(i, d), rx2w.at[i])
    cargo_line.start()

    sib_copy.wait_recv()
    for p in range(4):
        ours = rows_at(p * 192 + c * 96, 96, 96)
        for k in range(3):
            cols = slice(k * 256, (k + 1) * 256)
            qkv_in[0, p, :, cols] = (wide[k, ours, :] + qkv_sib[1, p, :, cols].astype(F32)).astype(BF)

    def plane_copy(k):
        return remote(qkv_in.at[0, planes[k]], qkv_in.at[1, d], qp_send.at[k], qp_recv.at[d], dp=planes[k])

    for k in range(3):
        plane_copy(k).start()
    qkv_in[1, d] = qkv_in[0, d]
    rows_line[1].pass_on()
    cargo_line.pass_on()

    for k in range(3):
        block = qkv_in.at[1, planes[k]]
        remote(block, block, qp_send.at[k], qp_recv.at[planes[k]], dp=d).wait_recv()
    total = qkv_in[1, 0].astype(F32)
    for p in range(1, 4):
        total = total + qkv_in[1, p].astype(F32)
    res_qkv[c] = total

    def result_copy(i, ref):
        return remote(ref.at[c], ref.at[c], f_send.at[i], f_recv.at[i], ctx=other)

    result_copy(0, res_qkv).start()

    for s in range(2):
        rows_line[s].collect()
        for half in range(2):
            rows = slice(half * 64, half * 64 + 64)
            grad_out = gna[s, t, rows, :].astype(F32) + rzn[s, 0, rows, :].astype(F32)
            grad_out = grad_out + rzn[s, 1, rows, :].astype(F32)
            third = rzn[s, 2, rows, :].astype(F32)
            grad_out = grad_out + jnp.where(at.mid == 1, third, jnp.zeros_like(third))
            grad_rows, scaled = norm_back(hidden[s, rows, :], grad_out, gain_a)
            grad_input[s, rows, :] += grad_rows
            add_row(0, grad_out * scaled)
            add_row(1, grad_out)

    core_sum = remote(sums, sums_core, s_send.at[0], sum_recv.at[0], ctx=other)
    core_sum.start()

    cargo_line.collect()
    total = ffw[0, t, rows_at(d * 192, 192, 192), :].astype(F32) + rz[0].astype(F32) + rz[1].astype(F32)
    third = rz[2].astype(F32)
    res_ff[c] = total + jnp.where(at.mid == 1, third, jnp.zeros_like(third))
    total = part_wo[t, rows_at(d * 192 + c * 96, 96, 96), :].astype(F32) + rzw[0].astype(F32)
    total = total + rzw[1].astype(F32)
    third = rzw[2].astype(F32)
    res_wo[c] = total + jnp.where(at.mid == 1, third, jnp.zeros_like(third))
    result_copy(1, res_ff).start()
    result_copy(2, res_wo).start()

    core_sum.wait_recv()
    sums_plane[d] = sums[...] + sums_core[...]

    def plane_sum(k, owner):
        block = sums_plane.at[owner]
        return remote(block, block, s_send.at[1 + k], sum_recv.at[1 + owner], dp=planes[k])

    def line_copy(k, owner):
        block = sums_line.at[owner]
        return remote(block, block, s_send.at[4 + k], sum_recv.at[5 + owner], tensor=others[k])

    for k in range(3):
        plane_sum(k, d).start()
    for k in range(3):
        plane_sum(k, planes[k]).wait_recv()
    sums_line[t] = (sums_plane[0] + sums_plane[1]) + (sums_plane[2] + sums_plane[3])
    for k in range(3):
        line_copy(k, t).start()

    for i, ref in enumerate((res_qkv, res_ff, res_wo)):
        result_copy(i, ref).wait_send()
        block = ref.at[other]
        remote(block, block, f_send.at[i], f_recv.at[i], ctx=other).wait_recv()
    for which in range(2):
        rows = slice(which * 96, (which + 1) * 96)
        for ref, start in ((g_wq, 0), (g_wk, LANES), (g_wv, 2 * LANES)):
            ref[rows, :] = res_qkv[which, :, start : start + 192]
    g_win[...] = res_ff[0]
    g_wout[...] = res_ff[1]
    g_wo[...] = res_wo[...].reshape(192, LANES).T[:192, :]

    for k in range(3):
        line_copy(k, others[k]).wait_recv()
    total = (sums_line[0] + sums_line[1]) + (sums_line[2] + sums_line[3])
    for i, ref in enumerate((g_gain_a, g_shift_a, g_gain_f, g_shift_f, g_bias_o, g_bias_out)):
        ref[...] = total[i]
    g_bias_in[...] = jnp.concatenate([total[6 + i : 7 + i, :] for i in range(4)], axis=1).reshape(3072)
    g_bias_q[...] = jnp.concatenate([total[12 + i : 13 + i, :192] for i in range(4)], axis=1).reshape(768)
    g_bias_v[...] = jnp.concatenate(
        [total[12 + i : 13 + i, 2 * LANES : 2 * LANES + 192] for i in range(4)], axis=1
    ).reshape(768)

    core_sum.wait_send()
    for k in range(3):
        plane_sum(k, d).wait_send()
        line_copy(k, t).wait_send()
        plane_copy(k).wait_send()
    sib_copy.wait_send()
    left_copy.wait_send()
    mixed_copy.wait_send()
    branch_copy.wait_send()
    for s in range(2):
        rows_line[s].end()
        kv_copy(s).wait_send()
        for k in range(3):
            m_copy(s, k).wait_send()
    cargo_line.end()
    for i in range(4):
        for j in range(2):
            first_ff(i, j).wait_send()
            first_wo(i, j).wait_send()
        second(i).wait_send()
    right_copy(2).wait_send()
    right_copy(3).wait_send()


def deliver_kernel(*refs):
    sems = refs[-1]
    count = (len(refs) - 1) // 2
    copies = [pltpu.make_async_copy(refs[i], refs[count + i], sems.at[i]) for i in range(count)]
    for copy in copies:
        copy.start()
    for copy in copies:
        copy.wait()


VM = pl.BlockSpec(memory_space=pltpu.VMEM)
ANY = pl.BlockSpec(memory_space=pl.ANY)


def body(*operands):
    struct = jax.ShapeDtypeStruct
    dma = pltpu.SemaphoreType.DMA
    vm = pltpu.VMEM
    operands = operands[:16] + (operands[16].T, operands[17])
    hidden, cotangent, _, gain, _, wq, wk, wv, bq, bv, wo, bo, gf, sf, win, bin_, wout, bout = operands
    results = (hidden, hidden, gain, gain, wq, wk, wv, bq, bv, wo, bo, gf, sf, win, bin_, wout, bout)
    shapes = tuple(struct(r.shape, F32) for r in results)
    made = pl.pallas_call(
        layer_kernel,
        out_shape=shapes,
        in_specs=[VM] * len(operands),
        out_specs=(VM,) * len(results),
        scratch_shapes=[
            vm((2, 4, 128, 768), BF),
            vm((768, 1024), BF),
            vm((2, 512, LANES), BF),
            vm((2, 2, 4, 128, 2 * LANES), BF),
            vm((4, 2, 128, LANES), BF),
            vm((4, 2, 128, LANES), BF),
            vm((4, 192, 768), BF),
            vm((4, 768, LANES), BF),
            vm((2, 4, 768, 768), BF),
            vm((LANES, 1024), BF),
            vm((LANES, 512), F32),
            vm((4, 2, 128, LANES), BF),
            vm((2, 4, 128, LANES), BF),
            vm((1024, 128), F32),
            vm((2, 256, 768), BF),
            vm((256, 768), BF),
            vm((2, 768, 256), BF),
            vm((2, 2, 256, 768), BF),
            vm((4, 256, 768), BF),
            vm((2, 256, 768), BF),
            vm((2, 768, 256), BF),
            vm((4, 768, LANES), BF),
            vm((4, 2, 192, 768), BF),
            vm((4, 192, 768), BF),
            vm((4, 192, 768), BF),
            vm((4, 2, 96, LANES), BF),
            vm((4, 96, LANES), BF),
            vm((4, 96, LANES), BF),
            vm((3, 1024, LANES), F32),
            vm((2, 512, 2 * LANES), BF),
            vm((2, 512, 2 * LANES), BF),
            vm((2, 512, 768), BF),
            vm((2, 4, 128, 768), BF),
            vm((2, 4, 128, 768), BF),
            vm((2, 4, 96, 768), BF),
            vm((2, 4, 96, 768), BF),
            vm((16, 768), F32),
            vm((16, 768), F32),
            vm((4, 16, 768), F32),
            vm((4, 16, 768), F32),
            vm((2, 192, 768), F32),
            vm((2, 96, LANES), F32),
            vm((2, 96, 768), F32),
            vm((1, 768), F32),
            vm((4, 1, 768), F32),
            dma((3,)), dma((4,)), dma((3,)), dma((3,)), dma((2, 4)), dma((2, 4)),
            dma((2, 4)), dma((2, 4)), dma((2, 3)), dma((2, 4)),
            dma((4, 2)), dma((2, 8, 2)), dma((4, 4, 2)), dma((4, 4, 2)), dma((4, 4, 2)),
            dma((1,)), dma((1,)), dma((4,)), dma((4,)), dma((1,)), dma((1,)), dma((1,)), dma((1,)),
            dma((2, 3)), dma((2, 4)),
            dma((4, 2)), dma((4, 2)), dma((4, 2)), dma((4, 2)), dma((4, 2)), dma((4, 2)),
            dma((2, 3)), dma((2, 4)), dma((2,)), dma((2,)), dma((2, 3)), dma((2, 4)),
            dma((1,)), dma((1,)), dma((3,)), dma((4,)), dma((3,)), dma((3,)), dma((7,)), dma((9,)),
        ],
        compiler_params=pltpu.CompilerParams(
            collective_id=1, has_side_effects=True, vmem_limit_bytes=63 << 20
        ),
        name="layer",
    )(*operands)
    made = pl.pallas_call(
        deliver_kernel,
        out_shape=shapes,
        in_specs=[VM] * len(shapes),
        out_specs=(ANY,) * len(shapes),
        scratch_shapes=[dma((len(shapes),))],
        name="deliver",
    )(*made)
    return tuple(made[:15]) + (made[15].T, made[16])


root_half = 0.7071067811865476
inv_root_two_pi = 0.3989422804014327


def general_gate(values):
    return values * (0.5 * (1.0 + lax.erf(values * root_half)))


def general_slope(values):
    normal_cdf = 0.5 * (1.0 + lax.erf(values * root_half))
    normal_pdf = jnp.exp(-0.5 * values * values) * inv_root_two_pi
    return normal_cdf + values * normal_pdf


def general_norm(rows, gain, shift):
    centred = rows - jnp.mean(rows, axis=-1, keepdims=True)
    inverse = lax.rsqrt(jnp.mean(centred * centred, axis=-1, keepdims=True) + 1e-05)
    scaled = centred * inverse
    return (scaled * gain + shift, scaled, inverse)


def general_norm_backward(grad_out, scaled, inverse, gain):
    grad_scaled = grad_out * gain
    plain_mean = jnp.mean(grad_scaled, axis=-1, keepdims=True)
    cross_mean = jnp.mean(grad_scaled * scaled, axis=-1, keepdims=True)
    grad_rows = inverse * (grad_scaled - plain_mean - scaled * cross_mean)
    return (grad_rows, jnp.sum(grad_out * scaled, axis=0), jnp.sum(grad_out, axis=0))


def tensor_rows(block):
    return lax.all_gather(block, "tensor", axis=0, tiled=True)


def tensor_sums(block):
    return lax.psum_scatter(block, "tensor", scatter_dimension=0, tiled=True)


def fetch_weights(shards):
    return (
        lax.all_gather(shards[0], "dp", axis=0, tiled=True),
        lax.all_gather(shards[1], "dp", axis=0, tiled=True),
        lax.all_gather(shards[2], "dp", axis=0, tiled=True),
        lax.all_gather(shards[3], "dp", axis=0, tiled=True),
        lax.all_gather(shards[4], "dp", axis=1, tiled=True),
        lax.all_gather(shards[5], "dp", axis=1, tiled=True),
    )


def general_piece(piece, total, start):
    return lax.dynamic_update_slice(jnp.zeros((total,), jnp.float32), piece, (start,))


def general_body(
    hidden_in,
    cotangent,
    segment_ids,
    attn_gain,
    attn_shift,
    query_weight,
    key_weight,
    value_weight,
    query_bias,
    value_bias,
    output_weight,
    output_bias,
    ffn_gain,
    ffn_shift,
    inner_weight,
    inner_bias,
    outer_weight,
    outer_bias,
):
    width = hidden_in.shape[2]
    part_width = query_weight.shape[1]
    unit_width = inner_weight.shape[1]
    unit_total = inner_bias.shape[0]
    heads_here = part_width // HDIM
    tensor_at = lax.axis_index("tensor")
    ctx_at = lax.axis_index("ctx")
    half_rows = hidden_in.shape[1] * lax.axis_size("tensor")
    seq_rows = segment_ids.shape[1]
    factor = HDIM ** (-0.5)
    query_piece = lax.dynamic_slice_in_dim(query_bias, tensor_at * part_width, part_width)
    value_piece = lax.dynamic_slice_in_dim(value_bias, tensor_at * part_width, part_width)
    inner_piece = lax.dynamic_slice_in_dim(inner_bias, tensor_at * unit_width, unit_width)
    shards = (
        query_weight.astype(jnp.bfloat16),
        key_weight.astype(jnp.bfloat16),
        value_weight.astype(jnp.bfloat16),
        inner_weight.astype(jnp.bfloat16),
        output_weight.astype(jnp.bfloat16),
        outer_weight.astype(jnp.bfloat16),
    )
    key_index = jnp.arange(seq_rows)
    query_index = ctx_at * half_rows + jnp.arange(half_rows)

    def masked_scores(queries, key_all, allowed):
        scores = (
            jnp.einsum("qhd,khd->hqk", queries, key_all, preferred_element_type=jnp.float32)
            * factor
        )
        return jnp.where(allowed[None, :, :], scores, -1e30)

    def micro(weights_bf, carry, item):
        w_query, w_key, w_value, w_inner, w_output, w_outer = weights_bf
        rows, cot_rows, segment_row = item
        query_seg = lax.dynamic_slice_in_dim(segment_row, ctx_at * half_rows, half_rows)
        allowed = (query_seg[:, None] == segment_row[None, :]) & (
            (segment_row[None, :] >= 0) | (query_index[:, None] == key_index[None, :])
        )
        normed, scaled_a, inverse_a = general_norm(rows, attn_gain, attn_shift)
        normed_all = tensor_rows(normed.astype(jnp.bfloat16))
        queries = (
            jnp.dot(normed_all, w_query, preferred_element_type=jnp.float32) + query_piece
        ).astype(jnp.bfloat16)
        key_half = jnp.dot(normed_all, w_key, preferred_element_type=jnp.float32).astype(
            jnp.bfloat16
        )
        value_half = (
            jnp.dot(normed_all, w_value, preferred_element_type=jnp.float32) + value_piece
        ).astype(jnp.bfloat16)
        key_all, value_all = (
            lax.all_gather(key_half, "ctx", axis=0, tiled=True),
            lax.all_gather(value_half, "ctx", axis=0, tiled=True),
        )
        queries = queries.reshape(half_rows, heads_here, HDIM)
        key_all = key_all.reshape(seq_rows, heads_here, HDIM)
        value_all = value_all.reshape(seq_rows, heads_here, HDIM)
        masked = masked_scores(queries, key_all, allowed)
        peak = jnp.max(masked, axis=-1, keepdims=True)
        expo = jnp.exp(masked - peak)
        total = jnp.sum(expo, axis=-1, keepdims=True)
        log_total = peak + jnp.log(total)
        probs = (expo / total).astype(jnp.bfloat16)
        mixed = jnp.einsum("hqk,khd->qhd", probs, value_all, preferred_element_type=jnp.float32)
        mixed = mixed.reshape(half_rows, part_width).astype(jnp.bfloat16)
        branch_a = tensor_sums(jnp.dot(mixed, w_output, preferred_element_type=jnp.float32))
        middle = rows + branch_a + output_bias
        normed_f, scaled_f, inverse_f = general_norm(middle, ffn_gain, ffn_shift)
        normed_f_all = tensor_rows(normed_f.astype(jnp.bfloat16))
        inner = jnp.dot(normed_f_all, w_inner, preferred_element_type=jnp.float32) + inner_piece
        active = general_gate(inner).astype(jnp.bfloat16)
        branch_f = tensor_sums(jnp.dot(active, w_outer, preferred_element_type=jnp.float32))
        result_rows = middle + branch_f + outer_bias
        grad_up = tensor_rows(cot_rows.astype(jnp.bfloat16))
        grad_outer_w = jnp.einsum("tf,td->fd", active, grad_up, preferred_element_type=jnp.float32)
        grad_active = jnp.einsum("td,fd->tf", grad_up, w_outer, preferred_element_type=jnp.float32)
        grad_inner = (grad_active * general_slope(inner)).astype(jnp.bfloat16)
        grad_inner_w = jnp.einsum(
            "td,tf->df", normed_f_all, grad_inner, preferred_element_type=jnp.float32
        )
        grad_inner_b = jnp.sum(grad_inner.astype(jnp.float32), axis=0)
        grad_normed_f = tensor_sums(
            jnp.einsum("tf,df->td", grad_inner, w_inner, preferred_element_type=jnp.float32)
        )
        grad_rows_f, grad_ffn_g, grad_ffn_s = general_norm_backward(
            grad_normed_f, scaled_f, inverse_f, ffn_gain
        )
        grad_middle = cot_rows + grad_rows_f
        grad_branch = tensor_rows(grad_middle.astype(jnp.bfloat16))
        grad_output_w = jnp.einsum(
            "tc,td->cd", mixed, grad_branch, preferred_element_type=jnp.float32
        )
        grad_mixed = jnp.einsum(
            "td,cd->tc", grad_branch, w_output, preferred_element_type=jnp.float32
        )
        grad_mixed = grad_mixed.astype(jnp.bfloat16).reshape(half_rows, heads_here, HDIM)
        grad_probs = jnp.einsum(
            "qhd,khd->hqk", grad_mixed, value_all, preferred_element_type=jnp.float32
        )
        grad_value_part = jnp.einsum(
            "hqk,qhd->khd", probs, grad_mixed, preferred_element_type=jnp.float32
        )
        again = jnp.exp(masked_scores(queries, key_all, allowed) - log_total)
        centre = jnp.sum(again * grad_probs, axis=-1, keepdims=True)
        grad_scores = (again * (grad_probs - centre)).astype(jnp.bfloat16)
        grad_queries = (
            jnp.einsum("hqk,khd->qhd", grad_scores, key_all, preferred_element_type=jnp.float32)
            * factor
        )
        grad_queries = grad_queries.reshape(half_rows, part_width).astype(jnp.bfloat16)
        grad_key_part = (
            jnp.einsum("hqk,qhd->khd", grad_scores, queries, preferred_element_type=jnp.float32)
            * factor
        )
        grad_key_sum, grad_value_sum = (
            lax.psum_scatter(
                grad_key_part.reshape(seq_rows, part_width).astype(jnp.bfloat16),
                "ctx",
                scatter_dimension=0,
                tiled=True,
            ).astype(jnp.float32),
            lax.psum_scatter(
                grad_value_part.reshape(seq_rows, part_width).astype(jnp.bfloat16),
                "ctx",
                scatter_dimension=0,
                tiled=True,
            ).astype(jnp.float32),
        )
        grad_keys = grad_key_sum.astype(jnp.bfloat16)
        grad_values = grad_value_sum.astype(jnp.bfloat16)
        grad_query_w = jnp.einsum(
            "td,tc->dc", normed_all, grad_queries, preferred_element_type=jnp.float32
        )
        grad_key_w = jnp.einsum(
            "td,tc->dc", normed_all, grad_keys, preferred_element_type=jnp.float32
        )
        grad_value_w = jnp.einsum(
            "td,tc->dc", normed_all, grad_values, preferred_element_type=jnp.float32
        )
        grad_query_b = jnp.sum(grad_queries.astype(jnp.float32), axis=0)
        grad_value_b = jnp.sum(grad_values.astype(jnp.float32), axis=0)
        grad_normed_part = jnp.einsum(
            "tc,dc->td", grad_queries, w_query, preferred_element_type=jnp.float32
        )
        grad_normed_part = grad_normed_part + jnp.einsum(
            "tc,dc->td", grad_keys, w_key, preferred_element_type=jnp.float32
        )
        grad_normed_part = grad_normed_part + jnp.einsum(
            "tc,dc->td", grad_values, w_value, preferred_element_type=jnp.float32
        )
        grad_normed = tensor_sums(grad_normed_part)
        grad_rows_a, grad_attn_g, grad_attn_s = general_norm_backward(
            grad_normed, scaled_a, inverse_a, attn_gain
        )
        grad_rows = grad_middle + grad_rows_a
        big_sums, small_sums = carry
        big_sums = (
            big_sums[0] + grad_query_w,
            big_sums[1] + grad_key_w,
            big_sums[2] + grad_value_w,
            big_sums[3] + grad_inner_w,
            big_sums[4] + grad_output_w,
            big_sums[5] + grad_outer_w,
        )
        small_terms = (
            grad_attn_g,
            grad_attn_s,
            general_piece(grad_query_b, width, tensor_at * part_width),
            general_piece(grad_value_b, width, tensor_at * part_width),
            jnp.sum(grad_middle, axis=0),
            grad_ffn_g,
            grad_ffn_s,
            general_piece(grad_inner_b, unit_total, tensor_at * unit_width),
            jnp.sum(cot_rows, axis=0),
        )
        small_sums = tuple((old + new for old, new in zip(small_sums, small_terms)))
        return ((big_sums, small_sums), (result_rows, grad_rows))

    big_init = (
        jnp.zeros((width, part_width), jnp.float32),
        jnp.zeros((width, part_width), jnp.float32),
        jnp.zeros((width, part_width), jnp.float32),
        jnp.zeros((width, unit_width), jnp.float32),
        jnp.zeros((part_width, width), jnp.float32),
        jnp.zeros((unit_width, width), jnp.float32),
    )
    small_init = tuple((jnp.zeros((width,), jnp.float32) for index_small in range(7))) + (
        jnp.zeros((unit_total,), jnp.float32),
        jnp.zeros((width,), jnp.float32),
    )
    small_init = (
        small_init[0],
        small_init[1],
        small_init[2],
        small_init[3],
        small_init[4],
        small_init[5],
        small_init[6],
        small_init[7],
        small_init[8],
    )
    gathered = fetch_weights(shards)

    def scan_step(carry, item):
        return micro(gathered, carry, item)

    (big_sums, small_sums), (block_out, grad_input) = lax.scan(
        scan_step, (big_init, small_init), (hidden_in, cotangent, segment_ids)
    )
    paired = (
        lax.psum(big_sums[0].astype(jnp.bfloat16), "ctx").astype(jnp.float32),
        lax.psum(big_sums[1].astype(jnp.bfloat16), "ctx").astype(jnp.float32),
        lax.psum(big_sums[2].astype(jnp.bfloat16), "ctx").astype(jnp.float32),
        lax.psum(big_sums[3].astype(jnp.bfloat16), "ctx").astype(jnp.float32),
        lax.psum(big_sums[4].astype(jnp.bfloat16), "ctx").astype(jnp.float32),
        lax.psum(big_sums[5].astype(jnp.bfloat16), "ctx").astype(jnp.float32),
    )
    owned = (
        lax.psum_scatter(
            paired[0].astype(jnp.bfloat16), "dp", scatter_dimension=0, tiled=True
        ).astype(jnp.float32),
        lax.psum_scatter(
            paired[1].astype(jnp.bfloat16), "dp", scatter_dimension=0, tiled=True
        ).astype(jnp.float32),
        lax.psum_scatter(
            paired[2].astype(jnp.bfloat16), "dp", scatter_dimension=0, tiled=True
        ).astype(jnp.float32),
        lax.psum_scatter(
            paired[3].astype(jnp.bfloat16), "dp", scatter_dimension=0, tiled=True
        ).astype(jnp.float32),
        lax.psum_scatter(
            paired[4].astype(jnp.bfloat16), "dp", scatter_dimension=1, tiled=True
        ).astype(jnp.float32),
        lax.psum_scatter(
            paired[5].astype(jnp.bfloat16), "dp", scatter_dimension=1, tiled=True
        ).astype(jnp.float32),
    )
    small = lax.psum(
        (
            small_sums[0],
            small_sums[1],
            small_sums[2],
            small_sums[3],
            small_sums[4],
            small_sums[5],
            small_sums[6],
            small_sums[7],
            small_sums[8],
        ),
        ("dp", "ctx", "tensor"),
    )
    return (
        block_out,
        grad_input,
        small[0],
        small[1],
        owned[0],
        owned[1],
        owned[2],
        small[2],
        small[3],
        owned[4],
        small[4],
        small[5],
        small[6],
        owned[3],
        small[7],
        owned[5],
        small[8],
    )


SPECS = (
    P("dp", ("ctx", "tensor"), None), P("dp", ("ctx", "tensor"), None), P("dp", None), P(), P(),
    P("dp", "tensor"), P("dp", "tensor"), P("dp", "tensor"), P(), P(), P("tensor", "dp"), P(), P(),
    P(), P("dp", "tensor"), P(), P("tensor", "dp"), P(),
)
OUT_SPECS = (
    P("dp", ("ctx", "tensor"), None), P("dp", ("ctx", "tensor"), None), P(), P(),
    P("dp", "tensor"), P("dp", "tensor"), P("dp", "tensor"), P(), P(), P("tensor", "dp"), P(), P(),
    P(), P("dp", "tensor"), P(), P("tensor", "dp"), P(),
)


def solution(mesh):
    lined_up = mesh.shape["dp"] == 4 and mesh.shape["tensor"] == 4 and mesh.shape["ctx"] == 2
    return jax.shard_map(
        body if lined_up else general_body, mesh=mesh, in_specs=SPECS, out_specs=OUT_SPECS, check_vma=False
    )
```

```python
import functools

import jax
import jax.numpy as jnp
from jax import lax
from jax.experimental import pallas as pl
from jax.experimental.pallas import tpu as pltpu
from jax.sharding import PartitionSpec as P

HDIM = 64
LANES = 256
ROOT_HALF = 0.7071067811865476
INV_ROOT_TWO_PI = 0.3989422804014327
MESH = pl.DeviceIdType.MESH
BF = jnp.bfloat16
F32 = jnp.float32
HIDE = -1e30


def dims(left, right, a, b):
    return lax.dot_general(left, right, (((a,), (b,)), ((), ())), preferred_element_type=F32)


def norm_parts(rows):
    centred = rows - jnp.mean(rows, axis=-1, keepdims=True)
    inverse = lax.rsqrt(jnp.mean(centred * centred, axis=-1, keepdims=True) + 1e-05)
    return centred * inverse, inverse


class Place:
    def __init__(self):
        self.d = lax.axis_index("dp")
        self.c = lax.axis_index("ctx")
        self.t = lax.axis_index("tensor")
        col, row = self.d % 2, self.d // 2
        self.dx = row * 2 + (1 - col)
        self.dy = (1 - row) * 2 + col
        self.dd = (1 - row) * 2 + (1 - col)
        self.h = self.t // 2
        self.g = self.t % 2
        self.mid = self.g + self.h * (1 - 2 * self.g)
        self.mate = 2 * self.h + 1 - self.g
        self.twin = (self.t + 2) % 4
        self.far_mid = 2 - self.h
        self.far_end = 3 * (1 - self.h)

    def source(self, k):
        first = 1 - jnp.minimum(k, 1)
        second = jnp.minimum(k, 1) * (1 - jnp.minimum(jnp.maximum(k - 1, 0), 1))
        third = jnp.minimum(jnp.maximum(k - 1, 0), 1) * (1 - jnp.maximum(k - 2, 0))
        fourth = jnp.maximum(k - 2, 0)
        return first * self.t + second * self.mate + third * self.far_mid + fourth * self.far_end


def remote(src, dst, send, recv, **where):
    return pltpu.make_async_remote_copy(
        src_ref=src, dst_ref=dst, send_sem=send, recv_sem=recv, device_id=where, device_id_type=MESH
    )


def greet(place):
    barrier = pltpu.get_barrier_semaphore()
    for k in range(1, 4):
        pl.semaphore_signal(
            barrier, inc=1, device_id={"tensor": (place.t + k) % 4}, device_id_type=MESH
        )
    for peer in (place.dx, place.dy, place.dd):
        pl.semaphore_signal(barrier, inc=1, device_id={"dp": peer}, device_id_type=MESH)
    pl.semaphore_signal(barrier, inc=1, device_id={"ctx": 1 - place.c}, device_id_type=MESH)
    for k in range(1, 4):
        where = {"ctx": 1 - place.c, "tensor": (place.t + k) % 4}
        pl.semaphore_signal(barrier, inc=1, device_id=where, device_id_type=MESH)
    return lambda: pl.semaphore_wait(barrier, 10)


class Several:
    def __init__(self, *copies):
        self.copies = copies

    def start(self):
        for copy in self.copies:
            copy.start()

    def wait_send(self):
        for copy in self.copies:
            copy.wait_send()

    def wait_recv(self):
        for copy in self.copies:
            copy.wait_recv()


def rows_at(start, size, step):
    return pl.ds(pl.multiple_of(start, step), size)


def erf_parts(values):
    cdf = 0.5 * (1.0 + lax.erf(values * ROOT_HALF))
    return cdf, cdf + values * (jnp.exp(-0.5 * values * values) * INV_ROOT_TWO_PI)


def add_to(target, *terms):
    total = target[...].astype(F32)
    for term in terms:
        total = total + term[...].astype(F32)
    target[...] = total.astype(BF)


def layer_kernel(
    hidden, cot, seg, gain_a, shift_a, wq_s, wk_s, wv_s, bias_q, bias_v, wo_s, bias_o, gain_f, shift_f,
    win_s, bias_in, wout_s, bias_out,
    block_out, grad_input, g_gain_a, g_shift_a, g_wq, g_wk, g_wv, g_bias_q, g_bias_v, g_wo, g_bias_o,
    g_gain_f, g_shift_f, g_win, g_bias_in, g_wout, g_bias_out,
    normed, far_rows, normed_turn, queries, kv, mixed_in, mixed_sib, q_land, wqkv, wo_land, wout, ffw,
    turn, q_turn, mixed, g_mix, keys_seg, left, left_in, left_turn, right, right_in, nf_out, nf_in,
    bf_out, bf_in, branch, branch_turn, part_wo, rxw, sumw, rzw, rx1, rx2, rz, wide, kv_out, kv_in, dqkv,
    gna, rzn, qkv_own, qkv_sib, qkv_in, qkv_sum, qkv_twin, sums, sums_core, sums_plane, sums_line,
    late, late_line, late_plane, res_ff, res_wo, res_qkv, bias_row, inner_rows,
    qt_send, q_send, q_recv, qc_send, qc_recv, z_send, z_recv, kvf_send, kvf_recv, mf_send, mf_recv,
    ct_send, cp_send, c_recv, cc_send, s_recv, wz_send, wz_recv, wp_send, wp_recv, wc_send, wc_recv,
    u_send, u_recv, l_send, l_recv, r_send, r_recv, n_send, n_recv, b_send, b_recv, x_send, x_recv,
    m_send, m_recv, p1_send, p1_recv, p2_send, p2_recv, zz_send, zz_recv, gp_send, gp_recv, gz_send, gz_recv,
    kv_send, kv_recv, rn_send, rn_recv, qs_send, qs_recv, qp_send, qp_recv, qz_send, qz_recv,
    f_send, f_recv, t_send, t_recv, ta_send, ta_recv, tb_send, tb_recv,
):
    at = Place()
    d, c, t, h, g = at.d, at.c, at.t, at.h, at.g
    other, away = 1 - c, 1 - h
    planes = (at.dx, at.dy, at.dd)
    others = [(t + k + 1) % 4 for k in range(3)]
    waits = []

    def begin(*copies):
        for copy in copies:
            copy.start()
            waits.append(copy)

    arrive = greet(at)

    for ref, start in ((wq_s, 0), (wk_s, LANES), (wv_s, 2 * LANES)):
        q_land[h, d, :, start + 128 : start + 256] = jnp.zeros((192, 128), BF)
        q_land[h, d, :, start : start + 192] = ref[...].astype(BF)
    arrive()

    def q_half(a, owner, which):
        return q_land.at[a, owner, rows_at(which * 96, 96, 96)]

    def q_plane(a, i, owner):
        half = q_half(a, owner, c)
        return remote(half, half, q_send.at[a, i], q_recv.at[a, owner], dp=planes[i])

    def q_core(a, owner):
        half = q_half(a, owner, c)
        return remote(half, half, qc_send.at[a, owner], qc_recv.at[a, owner], ctx=other)

    def q_core_wait(a, owner):
        half = q_half(a, owner, other)
        remote(half, half, qc_send.at[a, owner], qc_recv.at[a, owner], ctx=other).wait_recv()

    def q_wait(a, owner):
        half = q_half(a, owner, c)
        remote(half, half, qt_send.at[0], q_recv.at[a, owner], tensor=t).wait_recv()

    begin(remote(q_half(h, d, c), q_half(h, d, c), qt_send.at[0], q_recv.at[h, d], tensor=at.twin))
    for i in range(3):
        begin(q_plane(h, i, d))

    turned = wo_s[...].T
    turned = jnp.where(c == 0, turned[:96], turned[96:]).astype(BF)
    mine = rows_at(d * 192 + c * 96, 96, 96)
    wo_land[t, mine, 128:256] = jnp.zeros((96, 128), BF)
    wo_land[t, mine, 0:192] = turned

    def wo_rows(owner, which):
        return wo_land.at[:, rows_at(owner * 192 + which * 96, 96, 96)]

    def wo_line(k, owner):
        block = wo_land.at[owner, mine]
        return remote(block, block, wz_send.at[k], wz_recv.at[owner], tensor=others[k])

    for k in range(3):
        begin(wo_line(k, t))

    def normed_rows(s):
        scaled, _ = norm_parts(hidden[s])
        return (scaled * gain_a[...].reshape(1, 768) + shift_a[...].reshape(1, 768)).astype(BF)

    def row_copy(src, owner, k, dest):
        return remote(src, normed.at[owner], z_send.at[k], z_recv.at[owner], tensor=dest)

    def row_wait(p):
        row_copy(normed.at[p], p, 0, t).wait_recv()

    pass_end = row_copy(normed.at[at.far_end], at.far_end, 2, at.mate)
    pass_mid = row_copy(normed.at[at.far_mid], at.far_mid, 3, at.mate)
    far_rows[...] = normed_rows(away)
    begin(row_copy(far_rows, t, 1, at.far_mid))
    normed[t] = normed_rows(h)
    begin(row_copy(normed.at[t], t, 0, at.mate))

    here = rows_at(d * 192, 192, 192)

    @pl.when(c == 0)
    def _():
        ffw[0, h, here, :] = win_s[...].astype(BF)

    @pl.when(c == 1)
    def _():
        ffw[1, h, here, :] = wout_s[...].astype(BF)

    def ff_block(which, a, owner):
        return ffw.at[which, a, rows_at(owner * 192, 192, 192)]

    def ff_half(which, a, owner, n):
        return ffw.at[which, a, rows_at(owner * 192 + n * 96, 96, 96)]

    def ff_twin(n):
        block = ff_half(c, h, d, n)
        return remote(block, block, ct_send.at[n], c_recv.at[h, d, n], tensor=at.twin)

    def ff_plane(axis, a, owner, n, dest):
        block = ff_half(c, a, owner, n)
        return remote(block, block, cp_send.at[axis, a, n], c_recv.at[a, owner, n], dp=dest)

    def ff_core(a, owner, n):
        block = ff_half(c, a, owner, n)
        return remote(block, block, cc_send.at[a, owner, n], s_recv.at[a, owner, n], ctx=other)

    def ff_wait(a, owner, n):
        block = ff_half(c, a, owner, n)
        remote(block, block, ct_send.at[n], c_recv.at[a, owner, n], dp=d).wait_recv()

    def ff_core_wait(a, owner, n):
        block = ff_half(other, a, owner, n)
        remote(block, block, cc_send.at[a, owner, n], s_recv.at[a, owner, n], ctx=other).wait_recv()

    ff_sends = []

    def ff_begin(*copies):
        for copy in copies:
            copy.start()
            ff_sends.append(copy)

    def spread(a, n):
        ff_begin(ff_plane(0, a, d, n, at.dx), ff_plane(1, a, d, n, at.dy), ff_core(a, d, n))

    def near_far(a):
        near = at.dx + a * (at.dy - at.dx)
        return near, at.dx + at.dy - near

    def diag(a, n):
        near, far = near_far(a)
        ff_wait(a, near, n)
        ff_begin(ff_plane(2, a, near, n, far), ff_core(a, near, n))
        ff_wait(a, far, n)
        ff_begin(ff_core(a, far, n))

    def last(a, n):
        ff_wait(a, at.dd, n)
        ff_begin(ff_core(a, at.dd, n))

    left[1, 0] = cot[...].reshape(256, 768).astype(BF)
    sums[...] = jnp.zeros_like(sums)
    late[...] = jnp.zeros_like(late)
    wide[...] = jnp.zeros_like(wide)
    part_wo[...] = jnp.zeros_like(part_wo)
    for p in range(2):

        @pl.when(g == p)
        def _(p=p):
            for a in range(2):
                cols = slice((p + 2 * a) * 192, (p + 2 * a) * 192 + 192)
                bias_row[:, a * 192 : a * 192 + 192] = bias_q[...].reshape(1, 768)[:, cols]
                bias_row[:, 768 + a * 192 : 960 + a * 192] = bias_v[...].reshape(1, 768)[:, cols]

    bias_row[:, 384:768] = jnp.zeros((1, 384), F32)
    for p in range(4):
        inner_rows[p] = bias_in[...].reshape(1, 3072)[:, p * 768 : (p + 1) * 768]

    row = jnp.where(h == 0, seg[0:1, :], seg[1:2, :])
    places = lax.broadcasted_iota(jnp.int32, (1, 1024), 1)
    row = jnp.where(row >= 0, row, -1 - places).astype(F32)
    seg_query = jnp.where(c == 0, row[:, :512], row[:, 512:])
    keys_seg[...] = jnp.broadcast_to(row, (128, 1024)).T

    for i in range(3):
        q_wait(h, planes[i])
        begin(q_core(h, planes[i]))
    q_wait(away, d)
    for i in range(3):
        begin(q_plane(away, i, d))
    begin(q_core(away, d))

    @pl.when(at.mid == 1)
    def _():
        row_wait(at.far_end)
        pass_end.start()
        row_wait(at.far_mid)
        pass_mid.start()

    for i in range(3):
        q_wait(away, planes[i])
        begin(q_core(away, planes[i]))
    for k in range(3):
        p = others[k]
        block = wo_land.at[p, mine]
        remote(block, block, wz_send.at[k], wz_recv.at[p], tensor=p).wait_recv()
    for i in range(3):
        begin(remote(wo_rows(d, c), wo_rows(d, c), wp_send.at[i], wp_recv.at[d], dp=planes[i]))
    begin(remote(wo_rows(d, c), wo_rows(d, c), wc_send.at[d], wc_recv.at[d], ctx=other))
    for n in range(2):
        spread(h, n)
    for i in range(3):
        q_core_wait(h, planes[i])
        q_core_wait(away, planes[i])
    q_core_wait(away, d)

    def gather_columns(i, carry):
        rows = rows_at(i * 192, 192, 192)
        for k in range(3):
            pair = [q_land[a, i, :, k * LANES : k * LANES + 192] for a in range(2)]
            wqkv[rows, k * 384 : (k + 1) * 384] = jnp.concatenate(pair, axis=1)
        return carry

    lax.fori_loop(0, 4, gather_columns, 0)

    def kvf_copy(p):
        block = kv.at[:, c, p]
        return remote(block, block, kvf_send.at[p], kvf_recv.at[p], ctx=other)

    def project(k, carry):
        p = at.source(k)

        @pl.when((k == 1) | ((k > 1) & (at.mid == 0)))
        def _():
            row_wait(p)

        out = jnp.dot(normed[p], wqkv[...], preferred_element_type=F32)
        out = (out + bias_row[...]).astype(BF)
        for u in range(3):
            cols = out[:, u * 128 : (u + 1) * 128]
            queries[u, rows_at(p * 128, 128, 128), :] = cols * jnp.asarray(HDIM**-0.5, BF)
        for u in range(6):
            kv[u, c, p] = out[:, 384 + u * 128 : 512 + u * 128]
        kvf_copy(p).start()
        return carry

    for n in range(2):
        ff_begin(ff_twin(n))
    lax.fori_loop(0, 4, project, 0)

    lane_head = lax.broadcasted_iota(jnp.int32, (1, 128), 1) // HDIM

    def head_pair(ref, u):
        return ref[u].reshape(1024, 128)

    def masked_scores(u, b, q_here):
        seg_here = jnp.where(b == 0, seg_query[:, :256], seg_query[:, 256:])
        scores = dims(head_pair(kv, u), q_here, 1, 1)
        column = keys_seg[...]
        visible = jnp.concatenate([column, column], axis=1) == seg_here
        return jnp.where(visible, scores, HIDE)

    def one_head(w, block):
        return jnp.where(lane_head == w, block.astype(F32), 0.0).astype(BF)

    def mf_copy(k, p):
        return remote(mixed.at[p], mixed_in.at[g, h], mf_send.at[k], mf_recv.at[t], tensor=p)

    for p in range(4):
        block = kv.at[:, other, p]
        remote(block, block, kvf_send.at[p], kvf_recv.at[p], ctx=other).wait_recv()
    for u in range(3):
        turn[u * 128 : (u + 1) * 128, :] = head_pair(kv, 3 + u).T

    def attend(b):
        block = rows_at(b * 256, 256, 256)

        def step(i, carry):
            u, w = i // 2, i % 2
            scores = masked_scores(u, b, one_head(w, queries[u, block, :]))
            peak = jnp.max(scores, axis=0, keepdims=True)
            expo = jnp.exp(scores - peak)
            total = jnp.sum(expo, axis=0, keepdims=True)
            rows = rows_at(i * HDIM, HDIM, HDIM)
            turned = jnp.dot(turn[rows, :], expo.astype(BF), preferred_element_type=F32)
            q_turn[rows, :] = turned / total
            return carry

        lax.fori_loop(0, 6, step, 0)
        mixed[pl.ds(2 * b, 2)] = q_turn[...].T.astype(BF).reshape(2, 128, 384)

    attend(away)
    mf_copy(0, 2 * away).start()
    mf_copy(1, 2 * away + 1).start()
    begin(remote(left.at[1, 0], left.at[1, 1], u_send.at[1], u_recv.at[1], tensor=at.mate))
    for n in range(2):
        diag(h, n)
    attend(h)
    mf_copy(2, at.mate).start()
    mixed_in[g, h] = mixed[t]
    ff_wait(away, d, 0)
    spread(away, 0)
    for n in range(2):
        last(h, n)
    for i in range(3):
        p = planes[i]
        remote(wo_rows(p, c), wo_rows(p, c), wp_send.at[i], wp_recv.at[p], dp=p).wait_recv()
        begin(remote(wo_rows(p, c), wo_rows(p, c), wc_send.at[p], wc_recv.at[p], ctx=other))
    normed_turn[...] = normed[...].reshape(512, 768).T
    for p in range(4):
        remote(wo_rows(p, other), wo_rows(p, other), wc_send.at[p], wc_recv.at[p], ctx=other).wait_recv()
    for p in range(2):
        for i in range(4):
            rows = slice(i * 192, (i + 1) * 192)
            pair = [wo_land[p + 2 * a, rows, :192] for a in range(2)]
            wout[p, rows, :] = jnp.concatenate(pair, axis=1)
    ff_wait(away, d, 1)
    spread(away, 1)
    diag(away, 0)

    for k in range(3):
        p = others[k]
        block = mixed_in.at[p % 2, p // 2]
        remote(block, block, mf_send.at[k], mf_recv.at[p], tensor=p).wait_recv()
    for s in range(2):
        total = hidden[s] + bias_o[...].reshape(1, 768)
        for p in range(2):
            total = total + dims(mixed_in[p, s], wout[p], 1, 1)
        block_out[s] = total
        scaled, _ = norm_parts(total)
        left[0, 0, s * 128 : (s + 1) * 128, :] = (
            scaled * gain_f[...].reshape(1, 768) + shift_f[...].reshape(1, 768)
        ).astype(BF)
    begin(remote(left.at[0, 0], left.at[0, 1], u_send.at[0], u_recv.at[0], tensor=at.mate))
    begin(remote(mixed_in, mixed_sib, x_send.at[0], x_recv.at[0], ctx=other))

    diag(away, 1)
    for p in range(4):
        for n in range(2):
            ff_core_wait(h, p, n)

    def right_copy(a, r):
        return remote(
            right.at[other, a, r], right_in.at[a, r], r_send.at[a, r], r_recv.at[a, r], ctx=other
        )

    def units(a, r):
        unit = g + 2 * a
        top = pl.multiple_of(r * 512, 512)
        for j in range(3):
            cols = slice(j * 256, (j + 1) * 256)
            w_in, w_out = ffw[0, a, :, cols], ffw[1, a, :, cols]
            inner = jnp.dot(left[0, r], w_in, preferred_element_type=F32) + inner_rows[unit, :, cols]
            cdf, slope = erf_parts(inner)
            active = (inner * cdf).astype(BF)
            right[1, a, r, :, cols] = active
            grad_inner = jnp.dot(left[1, r], w_out, preferred_element_type=F32) * slope
            grad_inner = grad_inner.astype(BF)
            right[0, a, r, :, cols] = grad_inner
            sums[pl.ds(6 + unit, 1), cols] += jnp.sum(grad_inner.astype(F32), axis=0, keepdims=True)
            up, down = dims(active, w_out, 1, 1), dims(grad_inner, w_in, 1, 1)
            for k in range(6):
                wide[k, pl.ds(top, 256), :] += up[:, k * 128 : (k + 1) * 128]
                wide[k, pl.ds(top + 256, 256), :] += down[:, k * 128 : (k + 1) * 128]
        right_copy(a, r).start()

    def wide_rows(start, size=64):
        return jnp.concatenate([wide[k, start : start + size, :] for k in range(6)], axis=1)

    def own_slot(r, carry):
        @pl.when(r == 1)
        def _():
            for which in range(2):
                block = left.at[which, 1]
                remote(block, block, u_send.at[which], u_recv.at[which], tensor=at.mate).wait_recv()
            left_copy.start()

        units(h, r)
        return carry

    left_copy = remote(left.at[other], left_in, l_send.at[0], l_recv.at[0], ctx=other)
    waits.append(left_copy)
    lax.fori_loop(0, 2, own_slot, 0)
    for n in range(2):
        last(away, n)
    for p in range(4):
        for n in range(2):
            ff_core_wait(away, p, n)

    def twin_slot(i, carry):
        @pl.when(i == 1)
        def _():
            for q in range(4):
                rows = slice(q * 64, (q + 1) * 64)
                nf_out[rows, :] = wide_rows(768 + q * 64).astype(BF)
            nf_copy.start()

        units(away, 1 - i)
        return carry

    nf_copy = remote(nf_out, nf_in, n_send.at[0], n_recv.at[0], tensor=at.mate)
    waits.append(nf_copy)
    lax.fori_loop(0, 2, twin_slot, 0)
    for q in range(4):
        rows = slice(q * 64, (q + 1) * 64)
        bf_out[rows, :] = wide_rows(512 + q * 64).astype(BF)

    for copy in ff_sends:
        copy.wait_send()
    left_turn[0] = left[c, 0].T
    left_turn[1] = left[c, 1].T
    remote(left.at[c], left_in, l_send.at[0], l_recv.at[0], ctx=other).wait_recv()
    left_turn[2] = left_in[0].T
    left_turn[3] = left_in[1].T

    def first(a, j):
        near, _ = near_far(a)
        owner = near if j == 0 else at.dd
        return remote(ff_block(0, a, owner), rx1.at[a, j], p1_send.at[a, j], p1_recv.at[a, j], dp=near)

    def second(a):
        _, far = near_far(a)
        return remote(ff_block(0, a, far), rx2.at[a], p2_send.at[a], p2_recv.at[a], dp=far)

    def weight_gradient(a):
        for r in range(2):
            right_copy(a, r).wait_recv()

        def rows_of(q, carry):
            rows = rows_at(q * 192, 192, 192)
            out = jnp.dot(left_turn[0, rows, :], right[c, a, 0], preferred_element_type=F32)
            out = out + jnp.dot(left_turn[1, rows, :], right[c, a, 1], preferred_element_type=F32)
            out = out + jnp.dot(left_turn[2, rows, :], right_in[a, 0], preferred_element_type=F32)
            out = out + jnp.dot(left_turn[3, rows, :], right_in[a, 1], preferred_element_type=F32)
            ffw[0, a, rows, :] = out.astype(BF)
            return carry

        lax.fori_loop(0, 4, rows_of, 0)
        first(a, 1).start()
        first(a, 0).start()

    def both_slots(a, carry):
        weight_gradient(a)
        return carry

    lax.fori_loop(0, 2, both_slots, 0)

    def add_row(i, value):
        sums[i : i + 1, :] += jnp.sum(value, axis=0, keepdims=True)

    def norm_back(source, grad_out, gain):
        scaled, inverse = norm_parts(source)
        grad_scaled = grad_out * gain[...].reshape(1, 768)
        plain = jnp.mean(grad_scaled, axis=-1, keepdims=True)
        cross = jnp.mean(grad_scaled * scaled, axis=-1, keepdims=True)
        return inverse * (grad_scaled - plain - scaled * cross), scaled

    remote(nf_out, nf_in, n_send.at[0], n_recv.at[0], tensor=at.mate).wait_recv()
    for s in range(2):
        for half in range(2):
            rows = slice(half * 64, half * 64 + 64)
            start = s * 128 + half * 64
            cot_here = cot[s, rows, :]
            grad_out = wide_rows(256 + start) + nf_in[start : start + 64, :].astype(F32)
            middle = block_out[s, rows, :]
            grad_rows, scaled = norm_back(middle, grad_out, gain_f)
            block_out[s, rows, :] = middle + wide_rows(start) + bias_out[...].reshape(1, 768)
            grad_rows = grad_rows + cot_here
            grad_input[s, rows, :] = grad_rows
            branch[0, start : start + 64, :] = grad_rows.astype(BF)
            add_row(2, grad_out * scaled)
            add_row(3, grad_out)
            add_row(4, grad_rows)
            add_row(5, cot_here)
    begin(remote(branch.at[0], branch.at[1], b_send.at[0], b_recv.at[0], ctx=other))

    def m_copy(k):
        p = others[k]
        return remote(mixed.at[p], g_mix.at[t], m_send.at[k], m_recv.at[t], tensor=p)

    mf_copy(0, 2 * away).wait_send()
    mf_copy(1, 2 * away + 1).wait_send()
    mf_copy(2, at.mate).wait_send()
    for p in range(2):
        out = jnp.dot(branch[0], wout[p], preferred_element_type=F32).astype(BF)
        for s in range(2):
            mixed[2 * s + p] = out[s * 128 : (s + 1) * 128, :]
    for k in range(3):
        begin(m_copy(k))
    g_mix[t] = mixed[t]

    branch_turn[0] = branch[0].T
    remote(branch.at[0], branch.at[1], b_send.at[0], b_recv.at[0], ctx=other).wait_recv()
    branch_turn[1] = branch[1].T
    remote(mixed_in, mixed_sib, x_send.at[0], x_recv.at[0], ctx=other).wait_recv()
    for p in range(2):
        for q in range(4):
            rows = slice(q * 192, (q + 1) * 192)
            out = jnp.dot(branch_turn[0, rows, :], mixed_in[p].reshape(256, 384), preferred_element_type=F32)
            out = out + jnp.dot(
                branch_turn[1, rows, :], mixed_sib[p].reshape(256, 384), preferred_element_type=F32
            )
            for a in range(2):
                part_wo[p + 2 * a, rows, :192] = out[:, a * 192 : (a + 1) * 192].astype(BF)

    def wo_part(owner):
        return part_wo.at[:, rows_at(owner * 192 + c * 96, 96, 96)]

    for i in range(3):
        begin(remote(wo_part(planes[i]), rxw.at[d], gp_send.at[i], gp_recv.at[d], dp=planes[i]))

    def to_second(a):
        _, far = near_far(a)
        first(a, 1).wait_recv()
        add_to(ff_block(0, a, far), rx1.at[a, 1])
        second(a).start()
        first(a, 0).wait_recv()
        add_to(ff_block(0, a, d), rx1.at[a, 0])

    def plane_done(a):
        second(a).wait_recv()
        add_to(ff_block(0, a, d), rx2.at[a])

    zz_copy = remote(ff_block(0, away, d), rz, zz_send.at[0], zz_recv.at[0], tensor=at.twin)
    waits.append(zz_copy)

    for u in range(3):
        turn[u * 128 : (u + 1) * 128, :] = head_pair(kv, u).T
    wide[...] = jnp.zeros_like(wide)

    def m_wait(p):
        block = g_mix.at[p]
        remote(block, block, m_send.at[0], m_recv.at[p], tensor=p).wait_recv()

    theirs = rows_at(other * 512, 512, 512)
    ours = rows_at(c * 512, 512, 512)

    def kv_copy(u):
        return remote(kv_out.at[u], kv_in.at[u], kv_send.at[u], kv_recv.at[u], ctx=other)

    def attend_back(b, last):
        block = rows_at(b * 256, 256, 256)

        def step(u, carry):
            cols = pl.ds(pl.multiple_of(u * 128, 128), 128)
            g_pair = g_mix[pl.ds(2 * b, 2), :, cols].reshape(256, 128)
            for w in range(2):
                q_here = one_head(w, queries[u, block, :])
                g_here = one_head(w, g_pair)
                scores = masked_scores(u, b, q_here)
                peak = jnp.max(scores, axis=0, keepdims=True)
                expo = jnp.exp(scores - peak)
                probs = expo * (1.0 / jnp.sum(expo, axis=0, keepdims=True))
                grad_probs = dims(head_pair(kv, 3 + u), g_here, 1, 1)
                centre = jnp.sum(probs * grad_probs, axis=0, keepdims=True)
                wide[3 + u] += jnp.dot(probs.astype(BF), g_here, preferred_element_type=F32)
                grad_scores = (probs * (grad_probs - centre)).astype(BF)
                wide[u] += jnp.dot(grad_scores, q_here, preferred_element_type=F32)
                rows = rows_at(u * 128 + w * HDIM, HDIM, HDIM)
                q_turn[rows, :] = jnp.dot(turn[rows, :], grad_scores, preferred_element_type=F32)
            if not last:

                @pl.when(u > 0)
                def _():
                    to_second(u - 1)

            if last:
                @pl.when(u == 1)
                def _():
                    plane_done(away)
                    zz_copy.start()

                kv_out[u, :, :128] = wide[u, theirs, :].astype(BF)
                kv_out[u, :, 128:] = wide[3 + u, theirs, :].astype(BF)
                kv_copy(u).start()
            return carry

        lax.fori_loop(0, 3, step, 0)
        dqkv[block, :384] = (q_turn[...].T * HDIM**-0.5).astype(BF)

    m_wait(at.mate)
    begin(remote(bf_out, bf_in, n_send.at[1], n_recv.at[1], tensor=at.mate))
    attend_back(h, False)
    m_wait(at.far_mid)
    m_wait(at.far_end)
    attend_back(away, True)

    for i in range(3):
        p = planes[i]
        remote(wo_part(p), rxw.at[p], gp_send.at[i], gp_recv.at[p], dp=p).wait_recv()
    total = part_wo[:, mine, :].astype(F32)
    for i in range(3):
        total = total + rxw[planes[i]].astype(F32)
    sumw[...] = total.astype(BF)

    for u in range(3):
        kv_copy(u).wait_recv()
        for k in range(2):
            cols = slice(384 * (k + 1) + u * 128, 384 * (k + 1) + (u + 1) * 128)
            theirs_here = kv_in[u, :, k * 128 : (k + 1) * 128].astype(F32)
            dqkv[:, cols] = (wide[3 * k + u, ours, :] + theirs_here).astype(BF)

    def line_copy(owner, slot, k, dest):
        return remote(gna.at[owner], rzn.at[slot], rn_send.at[k], rn_recv.at[slot], tensor=dest)

    def line_wait(slot):
        line_copy(t, slot, 0, t).wait_recv()

    far_sum = line_copy(at.far_end, 3, 2, at.mate)
    on_sum = line_copy(at.far_end, 1, 2, at.far_end)

    def rows_back(p):
        rows = dqkv[rows_at(p * 128, 128, 128), :]
        gna[p] = dims(rows, wqkv[...], 1, 1).astype(BF)

    rows_back(at.far_end)

    @pl.when(at.mid == 0)
    def _():
        far_sum.start()

    rows_back(at.far_mid)
    begin(line_copy(at.far_mid, 2 - at.mid, 1, at.far_mid))
    rows_back(at.mate)
    begin(line_copy(at.mate, 0, 0, at.mate))
    rows_back(t)
    total = jnp.sum(dqkv[...].astype(F32), axis=0, keepdims=True)
    sums[pl.ds(10 + g, 1), :384] = total[:, :384]
    sums[pl.ds(10 + g, 1), 384:] = total[:, 768:]

    core_sum = remote(sums, sums_core, t_send.at[0], t_recv.at[0], ctx=other)
    begin(core_sum)

    def plane_sum(k, owner):
        block = sums_plane.at[owner]
        return remote(block, block, t_send.at[1 + k], t_recv.at[1 + owner], dp=planes[k])

    def line_sum(k, owner):
        block = sums_line.at[owner]
        return remote(block, block, t_send.at[4 + k], t_recv.at[5 + owner], tensor=others[k])

    def qkv_rows(i, carry):
        rows = rows_at(i * 192, 192, 192)
        out = jnp.dot(normed_turn[rows, :], dqkv[...], preferred_element_type=F32)
        qkv_own[i] = jnp.where(c == 0, out[:96], out[96:])
        qkv_sib[0, i] = jnp.where(c == 0, out[96:], out[:96]).astype(BF)
        return carry

    lax.fori_loop(0, 4, qkv_rows, 0)
    sib_copy = remote(qkv_sib.at[0], qkv_sib.at[1], qs_send.at[0], qs_recv.at[0], ctx=other)
    begin(sib_copy)
    for k in range(3):
        begin(remote(sumw.at[others[k]], rzw.at[t], gz_send.at[k], gz_recv.at[t], tensor=others[k]))

    @pl.when(at.mid == 1)
    def _():
        line_wait(3)
        add_to(gna.at[at.far_end], rzn.at[3])
        on_sum.start()

    core_sum.wait_recv()
    sums_plane[d] = sums[...] + sums_core[...]
    for k in range(3):
        begin(plane_sum(k, d))
    sib_copy.wait_recv()
    for p in range(4):
        qkv_in[0, p] = (qkv_own[p] + qkv_sib[1, p].astype(F32)).astype(BF)
    for k in range(3):
        begin(remote(qkv_in.at[0, planes[k]], qkv_in.at[1, d], qp_send.at[k], qp_recv.at[d], dp=planes[k]))
    qkv_in[1, d] = qkv_in[0, d]

    def result_copy(i, ref):
        return remote(ref.at[c], ref.at[c], f_send.at[i], f_recv.at[i], ctx=other)

    plane_done(h)
    remote(rz, rz, zz_send.at[0], zz_recv.at[0], tensor=t).wait_recv()
    res_ff[c] = ffw[0, h, here, :].astype(F32) + rz[...].astype(F32)
    begin(result_copy(1, res_ff))
    rzw[t] = sumw[t]
    for k in range(3):
        p = others[k]
        remote(rzw.at[p], rzw.at[p], gz_send.at[k], gz_recv.at[p], tensor=p).wait_recv()
    total = rzw[0].astype(F32)
    for p in range(1, 4):
        total = total + rzw[p].astype(F32)
    res_wo[c] = total
    begin(result_copy(2, res_wo))

    for k in range(3):
        plane_sum(k, planes[k]).wait_recv()
    sums_line[t] = (sums_plane[0] + sums_plane[1]) + (sums_plane[2] + sums_plane[3])
    for k in range(3):
        begin(line_sum(k, t))

    for k in range(3):
        block = qkv_in.at[1, planes[k]]
        remote(block, block, qp_send.at[k], qp_recv.at[planes[k]], dp=d).wait_recv()
    total = qkv_in[1, 0].astype(F32)
    for p in range(1, 4):
        total = total + qkv_in[1, p].astype(F32)
    for k in range(3):
        low, high = total[:, k * 384 : k * 384 + 192], total[:, k * 384 + 192 : (k + 1) * 384]
        qkv_sum[0, :, k * LANES : k * LANES + 192] = jnp.where(h == 0, low, high)
        qkv_twin[0, :, k * LANES : k * LANES + 192] = jnp.where(h == 0, high, low).astype(BF)
    begin(remote(qkv_twin.at[0], qkv_twin.at[1], qz_send.at[0], qz_recv.at[0], tensor=at.twin))

    remote(bf_out, bf_in, n_send.at[1], n_recv.at[1], tensor=at.mate).wait_recv()
    for s in range(2):
        block_out[s] += bf_in[s * 128 : (s + 1) * 128, :].astype(F32)

    for slot in range(2):
        line_wait(slot)

    @pl.when(at.mid == 1)
    def _():
        line_wait(2)

    for s in range(2):
        for half in range(2):
            rows = slice(half * 64, half * 64 + 64)
            near = gna[t, rows, :].astype(F32) + rzn[0, rows, :].astype(F32)
            third = rzn[2, rows, :].astype(F32)
            far = rzn[1, rows, :].astype(F32) + jnp.where(at.mid == 1, third, jnp.zeros_like(third))
            grad_out = jnp.where(h == s, near, far)
            grad_rows, scaled = norm_back(hidden[s, rows, :], grad_out, gain_a)
            grad_input[s, rows, :] += grad_rows
            late[0:1, :] += jnp.sum(grad_out * scaled, axis=0, keepdims=True)
            late[1:2, :] += jnp.sum(grad_out, axis=0, keepdims=True)

    late_line[c, t] = late[...]
    peers = [(c, p) for p in others] + [(other, p) for p in others] + [(other, t)]
    for k, (core, p) in enumerate(peers):
        block = late_line.at[c, t]
        begin(remote(block, block, ta_send.at[k], ta_recv.at[c, t], ctx=core, tensor=p))
    block = qkv_twin.at[1]
    remote(block, block, qz_send.at[0], qz_recv.at[0], tensor=t).wait_recv()
    res_qkv[c] = qkv_sum[0] + qkv_twin[1].astype(F32)
    begin(result_copy(0, res_qkv))
    for k, (core, p) in enumerate(peers):
        block = late_line.at[core, p]
        remote(block, block, ta_send.at[k], ta_recv.at[core, p], ctx=core, tensor=p).wait_recv()
    total = late_line[0, 0]
    for k in range(1, 8):
        total = total + late_line[k // 4, k % 4]
    late_plane[d] = total
    for k in range(3):
        block = late_plane.at[d]
        begin(remote(block, block, tb_send.at[k], tb_recv.at[d], dp=planes[k]))

    for i, ref in enumerate((res_qkv, res_ff, res_wo)):
        block = ref.at[other]
        remote(block, block, f_send.at[i], f_recv.at[i], ctx=other).wait_recv()
    for which in range(2):
        rows = slice(which * 96, (which + 1) * 96)
        for ref, start in ((g_wq, 0), (g_wk, LANES), (g_wv, 2 * LANES)):
            ref[rows, :] = res_qkv[which, :, start : start + 192]
    g_win[...] = res_ff[0]
    g_wout[...] = res_ff[1]
    g_wo[...] = res_wo[...].reshape(192, LANES).T[:192, :]

    for k in range(3):
        line_sum(k, others[k]).wait_recv()
    total = (sums_line[0] + sums_line[1]) + (sums_line[2] + sums_line[3])
    for i, ref in enumerate((g_gain_f, g_shift_f, g_bias_o, g_bias_out)):
        ref[...] = total[2 + i]
    g_bias_in[...] = jnp.concatenate([total[6 + i : 7 + i, :] for i in range(4)], axis=1).reshape(3072)
    for ref, start in ((g_bias_q, 0), (g_bias_v, 384)):
        pieces = []
        for p in range(4):
            first_lane = start + (p // 2) * 192
            pieces.append(total[10 + p % 2 : 11 + p % 2, first_lane : first_lane + 192])
        ref[...] = jnp.concatenate(pieces, axis=1).reshape(768)
    for k in range(3):
        block = late_plane.at[planes[k]]
        remote(block, block, tb_send.at[k], tb_recv.at[planes[k]], dp=d).wait_recv()
    total = (late_plane[0] + late_plane[1]) + (late_plane[2] + late_plane[3])
    g_gain_a[...] = total[0]
    g_shift_a[...] = total[1]

    for copy in waits:
        copy.wait_send()
    for p in range(4):
        kvf_copy(p).wait_send()
    for u in range(3):
        kv_copy(u).wait_send()
    for a in range(2):
        first(a, 0).wait_send()
        first(a, 1).wait_send()
        second(a).wait_send()
        for r in range(2):
            right_copy(a, r).wait_send()

    @pl.when(at.mid == 1)
    def _():
        pass_end.wait_send()
        pass_mid.wait_send()
        on_sum.wait_send()

    @pl.when(at.mid == 0)
    def _():
        far_sum.wait_send()


def deliver_kernel(*refs):
    sems = refs[-1]
    count = (len(refs) - 1) // 2
    copies = [pltpu.make_async_copy(refs[i], refs[count + i], sems.at[i]) for i in range(count)]
    for copy in copies:
        copy.start()
    for copy in copies:
        copy.wait()


VM = pl.BlockSpec(memory_space=pltpu.VMEM)
ANY = pl.BlockSpec(memory_space=pl.ANY)


def body(*operands):
    struct = jax.ShapeDtypeStruct
    dma = pltpu.SemaphoreType.DMA
    vm = pltpu.VMEM
    operands = operands[:16] + (operands[16].T, operands[17])
    hidden, cotangent, _, gain, _, wq, wk, wv, bq, bv, wo, bo, gf, sf, win, bin_, wout, bout = operands
    results = (hidden, hidden, gain, gain, wq, wk, wv, bq, bv, wo, bo, gf, sf, win, bin_, wout, bout)
    shapes = tuple(struct(r.shape, F32) for r in results)
    made = pl.pallas_call(
        layer_kernel,
        out_shape=shapes,
        in_specs=[VM] * len(operands),
        out_specs=(VM,) * len(results),
        scratch_shapes=[
            vm((4, 128, 768), BF),
            vm((128, 768), BF),
            vm((768, 512), BF),
            vm((3, 512, 128), BF),
            vm((6, 2, 4, 128, 128), BF),
            vm((2, 2, 128, 384), BF),
            vm((2, 2, 128, 384), BF),
            vm((2, 4, 192, 768), BF),
            vm((768, 1152), BF),
            vm((4, 768, LANES), BF),
            vm((2, 768, 384), BF),
            vm((2, 2, 768, 768), BF),
            vm((384, 1024), BF),
            vm((384, 256), F32),
            vm((4, 128, 384), BF),
            vm((4, 128, 384), BF),
            vm((1024, 128), F32),
            vm((2, 2, 256, 768), BF),
            vm((2, 256, 768), BF),
            vm((4, 768, 256), BF),
            vm((2, 2, 2, 256, 768), BF),
            vm((2, 2, 256, 768), BF),
            vm((256, 768), BF),
            vm((256, 768), BF),
            vm((256, 768), BF),
            vm((256, 768), BF),
            vm((2, 256, 768), BF),
            vm((2, 768, 256), BF),
            vm((4, 768, LANES), BF),
            vm((4, 4, 96, LANES), BF),
            vm((4, 96, LANES), BF),
            vm((4, 96, LANES), BF),
            vm((2, 2, 192, 768), BF),
            vm((2, 192, 768), BF),
            vm((192, 768), BF),
            vm((6, 1024, 128), F32),
            vm((3, 512, 256), BF),
            vm((3, 512, 256), BF),
            vm((512, 1152), BF),
            vm((4, 128, 768), BF),
            vm((4, 128, 768), BF),
            vm((4, 96, 1152), F32),
            vm((2, 4, 96, 1152), BF),
            vm((2, 4, 96, 1152), BF),
            vm((1, 96, 768), F32),
            vm((2, 96, 768), BF),
            vm((16, 768), F32),
            vm((16, 768), F32),
            vm((4, 16, 768), F32),
            vm((4, 16, 768), F32),
            vm((2, 768), F32),
            vm((2, 4, 2, 768), F32),
            vm((4, 2, 768), F32),
            vm((2, 192, 768), F32),
            vm((2, 96, LANES), F32),
            vm((2, 96, 768), F32),
            vm((1, 1152), F32),
            vm((4, 1, 768), F32),
            dma((1,)), dma((2, 3)), dma((2, 4)), dma((2, 4)), dma((2, 4)),
            dma((4,)), dma((4,)), dma((4,)), dma((4,)), dma((3,)), dma((4,)),
            dma((2,)), dma((3, 2, 2)), dma((2, 4, 2)), dma((2, 4, 2)), dma((2, 4, 2)),
            dma((3,)), dma((4,)), dma((3,)), dma((4,)), dma((4,)), dma((4,)),
            dma((2,)), dma((2,)), dma((1,)), dma((1,)), dma((2, 2)), dma((2, 2)),
            dma((2,)), dma((2,)), dma((1,)), dma((1,)), dma((1,)), dma((1,)),
            dma((3,)), dma((4,)),
            dma((2, 2)), dma((2, 2)), dma((2,)), dma((2,)), dma((1,)), dma((1,)),
            dma((3,)), dma((4,)), dma((3,)), dma((4,)),
            dma((3,)), dma((3,)), dma((3,)), dma((4,)),
            dma((1,)), dma((1,)), dma((3,)), dma((4,)), dma((1,)), dma((1,)),
            dma((3,)), dma((3,)), dma((7,)), dma((9,)),
            dma((7,)), dma((2, 4)), dma((3,)), dma((4,)),
        ],
        compiler_params=pltpu.CompilerParams(
            collective_id=1, has_side_effects=True, vmem_limit_bytes=63 << 20
        ),
        name="layer",
    )(*operands)
    made = pl.pallas_call(
        deliver_kernel,
        out_shape=shapes,
        in_specs=[VM] * len(shapes),
        out_specs=(ANY,) * len(shapes),
        scratch_shapes=[dma((len(shapes),))],
        name="deliver",
    )(*made)
    return tuple(made[:15]) + (made[15].T, made[16])


root_half = 0.7071067811865476
inv_root_two_pi = 0.3989422804014327


def general_gate(values):
    return values * (0.5 * (1.0 + lax.erf(values * root_half)))


def general_slope(values):
    normal_cdf = 0.5 * (1.0 + lax.erf(values * root_half))
    normal_pdf = jnp.exp(-0.5 * values * values) * inv_root_two_pi
    return normal_cdf + values * normal_pdf


def general_norm(rows, gain, shift):
    centred = rows - jnp.mean(rows, axis=-1, keepdims=True)
    inverse = lax.rsqrt(jnp.mean(centred * centred, axis=-1, keepdims=True) + 1e-05)
    scaled = centred * inverse
    return (scaled * gain + shift, scaled, inverse)


def general_norm_backward(grad_out, scaled, inverse, gain):
    grad_scaled = grad_out * gain
    plain_mean = jnp.mean(grad_scaled, axis=-1, keepdims=True)
    cross_mean = jnp.mean(grad_scaled * scaled, axis=-1, keepdims=True)
    grad_rows = inverse * (grad_scaled - plain_mean - scaled * cross_mean)
    return (grad_rows, jnp.sum(grad_out * scaled, axis=0), jnp.sum(grad_out, axis=0))


def tensor_rows(block):
    return lax.all_gather(block, "tensor", axis=0, tiled=True)


def tensor_sums(block):
    return lax.psum_scatter(block, "tensor", scatter_dimension=0, tiled=True)


def fetch_weights(shards):
    return (
        lax.all_gather(shards[0], "dp", axis=0, tiled=True),
        lax.all_gather(shards[1], "dp", axis=0, tiled=True),
        lax.all_gather(shards[2], "dp", axis=0, tiled=True),
        lax.all_gather(shards[3], "dp", axis=0, tiled=True),
        lax.all_gather(shards[4], "dp", axis=1, tiled=True),
        lax.all_gather(shards[5], "dp", axis=1, tiled=True),
    )


def general_piece(piece, total, start):
    return lax.dynamic_update_slice(jnp.zeros((total,), jnp.float32), piece, (start,))


def general_body(
    hidden_in,
    cotangent,
    segment_ids,
    attn_gain,
    attn_shift,
    query_weight,
    key_weight,
    value_weight,
    query_bias,
    value_bias,
    output_weight,
    output_bias,
    ffn_gain,
    ffn_shift,
    inner_weight,
    inner_bias,
    outer_weight,
    outer_bias,
):
    width = hidden_in.shape[2]
    part_width = query_weight.shape[1]
    unit_width = inner_weight.shape[1]
    unit_total = inner_bias.shape[0]
    heads_here = part_width // HDIM
    tensor_at = lax.axis_index("tensor")
    ctx_at = lax.axis_index("ctx")
    half_rows = hidden_in.shape[1] * lax.axis_size("tensor")
    seq_rows = segment_ids.shape[1]
    factor = HDIM ** (-0.5)
    query_piece = lax.dynamic_slice_in_dim(query_bias, tensor_at * part_width, part_width)
    value_piece = lax.dynamic_slice_in_dim(value_bias, tensor_at * part_width, part_width)
    inner_piece = lax.dynamic_slice_in_dim(inner_bias, tensor_at * unit_width, unit_width)
    shards = (
        query_weight.astype(jnp.bfloat16),
        key_weight.astype(jnp.bfloat16),
        value_weight.astype(jnp.bfloat16),
        inner_weight.astype(jnp.bfloat16),
        output_weight.astype(jnp.bfloat16),
        outer_weight.astype(jnp.bfloat16),
    )
    key_index = jnp.arange(seq_rows)
    query_index = ctx_at * half_rows + jnp.arange(half_rows)

    def masked_scores(queries, key_all, allowed):
        scores = (
            jnp.einsum("qhd,khd->hqk", queries, key_all, preferred_element_type=jnp.float32)
            * factor
        )
        return jnp.where(allowed[None, :, :], scores, -1e30)

    def micro(weights_bf, carry, item):
        w_query, w_key, w_value, w_inner, w_output, w_outer = weights_bf
        rows, cot_rows, segment_row = item
        query_seg = lax.dynamic_slice_in_dim(segment_row, ctx_at * half_rows, half_rows)
        allowed = (query_seg[:, None] == segment_row[None, :]) & (
            (segment_row[None, :] >= 0) | (query_index[:, None] == key_index[None, :])
        )
        normed, scaled_a, inverse_a = general_norm(rows, attn_gain, attn_shift)
        normed_all = tensor_rows(normed.astype(jnp.bfloat16))
        queries = (
            jnp.dot(normed_all, w_query, preferred_element_type=jnp.float32) + query_piece
        ).astype(jnp.bfloat16)
        key_half = jnp.dot(normed_all, w_key, preferred_element_type=jnp.float32).astype(
            jnp.bfloat16
        )
        value_half = (
            jnp.dot(normed_all, w_value, preferred_element_type=jnp.float32) + value_piece
        ).astype(jnp.bfloat16)
        key_all, value_all = (
            lax.all_gather(key_half, "ctx", axis=0, tiled=True),
            lax.all_gather(value_half, "ctx", axis=0, tiled=True),
        )
        queries = queries.reshape(half_rows, heads_here, HDIM)
        key_all = key_all.reshape(seq_rows, heads_here, HDIM)
        value_all = value_all.reshape(seq_rows, heads_here, HDIM)
        masked = masked_scores(queries, key_all, allowed)
        peak = jnp.max(masked, axis=-1, keepdims=True)
        expo = jnp.exp(masked - peak)
        total = jnp.sum(expo, axis=-1, keepdims=True)
        log_total = peak + jnp.log(total)
        probs = (expo / total).astype(jnp.bfloat16)
        mixed = jnp.einsum("hqk,khd->qhd", probs, value_all, preferred_element_type=jnp.float32)
        mixed = mixed.reshape(half_rows, part_width).astype(jnp.bfloat16)
        branch_a = tensor_sums(jnp.dot(mixed, w_output, preferred_element_type=jnp.float32))
        middle = rows + branch_a + output_bias
        normed_f, scaled_f, inverse_f = general_norm(middle, ffn_gain, ffn_shift)
        normed_f_all = tensor_rows(normed_f.astype(jnp.bfloat16))
        inner = jnp.dot(normed_f_all, w_inner, preferred_element_type=jnp.float32) + inner_piece
        active = general_gate(inner).astype(jnp.bfloat16)
        branch_f = tensor_sums(jnp.dot(active, w_outer, preferred_element_type=jnp.float32))
        result_rows = middle + branch_f + outer_bias
        grad_up = tensor_rows(cot_rows.astype(jnp.bfloat16))
        grad_outer_w = jnp.einsum("tf,td->fd", active, grad_up, preferred_element_type=jnp.float32)
        grad_active = jnp.einsum("td,fd->tf", grad_up, w_outer, preferred_element_type=jnp.float32)
        grad_inner = (grad_active * general_slope(inner)).astype(jnp.bfloat16)
        grad_inner_w = jnp.einsum(
            "td,tf->df", normed_f_all, grad_inner, preferred_element_type=jnp.float32
        )
        grad_inner_b = jnp.sum(grad_inner.astype(jnp.float32), axis=0)
        grad_normed_f = tensor_sums(
            jnp.einsum("tf,df->td", grad_inner, w_inner, preferred_element_type=jnp.float32)
        )
        grad_rows_f, grad_ffn_g, grad_ffn_s = general_norm_backward(
            grad_normed_f, scaled_f, inverse_f, ffn_gain
        )
        grad_middle = cot_rows + grad_rows_f
        grad_branch = tensor_rows(grad_middle.astype(jnp.bfloat16))
        grad_output_w = jnp.einsum(
            "tc,td->cd", mixed, grad_branch, preferred_element_type=jnp.float32
        )
        grad_mixed = jnp.einsum(
            "td,cd->tc", grad_branch, w_output, preferred_element_type=jnp.float32
        )
        grad_mixed = grad_mixed.astype(jnp.bfloat16).reshape(half_rows, heads_here, HDIM)
        grad_probs = jnp.einsum(
            "qhd,khd->hqk", grad_mixed, value_all, preferred_element_type=jnp.float32
        )
        grad_value_part = jnp.einsum(
            "hqk,qhd->khd", probs, grad_mixed, preferred_element_type=jnp.float32
        )
        again = jnp.exp(masked_scores(queries, key_all, allowed) - log_total)
        centre = jnp.sum(again * grad_probs, axis=-1, keepdims=True)
        grad_scores = (again * (grad_probs - centre)).astype(jnp.bfloat16)
        grad_queries = (
            jnp.einsum("hqk,khd->qhd", grad_scores, key_all, preferred_element_type=jnp.float32)
            * factor
        )
        grad_queries = grad_queries.reshape(half_rows, part_width).astype(jnp.bfloat16)
        grad_key_part = (
            jnp.einsum("hqk,qhd->khd", grad_scores, queries, preferred_element_type=jnp.float32)
            * factor
        )
        grad_key_sum, grad_value_sum = (
            lax.psum_scatter(
                grad_key_part.reshape(seq_rows, part_width).astype(jnp.bfloat16),
                "ctx",
                scatter_dimension=0,
                tiled=True,
            ).astype(jnp.float32),
            lax.psum_scatter(
                grad_value_part.reshape(seq_rows, part_width).astype(jnp.bfloat16),
                "ctx",
                scatter_dimension=0,
                tiled=True,
            ).astype(jnp.float32),
        )
        grad_keys = grad_key_sum.astype(jnp.bfloat16)
        grad_values = grad_value_sum.astype(jnp.bfloat16)
        grad_query_w = jnp.einsum(
            "td,tc->dc", normed_all, grad_queries, preferred_element_type=jnp.float32
        )
        grad_key_w = jnp.einsum(
            "td,tc->dc", normed_all, grad_keys, preferred_element_type=jnp.float32
        )
        grad_value_w = jnp.einsum(
            "td,tc->dc", normed_all, grad_values, preferred_element_type=jnp.float32
        )
        grad_query_b = jnp.sum(grad_queries.astype(jnp.float32), axis=0)
        grad_value_b = jnp.sum(grad_values.astype(jnp.float32), axis=0)
        grad_normed_part = jnp.einsum(
            "tc,dc->td", grad_queries, w_query, preferred_element_type=jnp.float32
        )
        grad_normed_part = grad_normed_part + jnp.einsum(
            "tc,dc->td", grad_keys, w_key, preferred_element_type=jnp.float32
        )
        grad_normed_part = grad_normed_part + jnp.einsum(
            "tc,dc->td", grad_values, w_value, preferred_element_type=jnp.float32
        )
        grad_normed = tensor_sums(grad_normed_part)
        grad_rows_a, grad_attn_g, grad_attn_s = general_norm_backward(
            grad_normed, scaled_a, inverse_a, attn_gain
        )
        grad_rows = grad_middle + grad_rows_a
        big_sums, small_sums = carry
        big_sums = (
            big_sums[0] + grad_query_w,
            big_sums[1] + grad_key_w,
            big_sums[2] + grad_value_w,
            big_sums[3] + grad_inner_w,
            big_sums[4] + grad_output_w,
            big_sums[5] + grad_outer_w,
        )
        small_terms = (
            grad_attn_g,
            grad_attn_s,
            general_piece(grad_query_b, width, tensor_at * part_width),
            general_piece(grad_value_b, width, tensor_at * part_width),
            jnp.sum(grad_middle, axis=0),
            grad_ffn_g,
            grad_ffn_s,
            general_piece(grad_inner_b, unit_total, tensor_at * unit_width),
            jnp.sum(cot_rows, axis=0),
        )
        small_sums = tuple((old + new for old, new in zip(small_sums, small_terms)))
        return ((big_sums, small_sums), (result_rows, grad_rows))

    big_init = (
        jnp.zeros((width, part_width), jnp.float32),
        jnp.zeros((width, part_width), jnp.float32),
        jnp.zeros((width, part_width), jnp.float32),
        jnp.zeros((width, unit_width), jnp.float32),
        jnp.zeros((part_width, width), jnp.float32),
        jnp.zeros((unit_width, width), jnp.float32),
    )
    small_init = tuple((jnp.zeros((width,), jnp.float32) for index_small in range(7))) + (
        jnp.zeros((unit_total,), jnp.float32),
        jnp.zeros((width,), jnp.float32),
    )
    small_init = (
        small_init[0],
        small_init[1],
        small_init[2],
        small_init[3],
        small_init[4],
        small_init[5],
        small_init[6],
        small_init[7],
        small_init[8],
    )
    gathered = fetch_weights(shards)

    def scan_step(carry, item):
        return micro(gathered, carry, item)

    (big_sums, small_sums), (block_out, grad_input) = lax.scan(
        scan_step, (big_init, small_init), (hidden_in, cotangent, segment_ids)
    )
    paired = (
        lax.psum(big_sums[0].astype(jnp.bfloat16), "ctx").astype(jnp.float32),
        lax.psum(big_sums[1].astype(jnp.bfloat16), "ctx").astype(jnp.float32),
        lax.psum(big_sums[2].astype(jnp.bfloat16), "ctx").astype(jnp.float32),
        lax.psum(big_sums[3].astype(jnp.bfloat16), "ctx").astype(jnp.float32),
        lax.psum(big_sums[4].astype(jnp.bfloat16), "ctx").astype(jnp.float32),
        lax.psum(big_sums[5].astype(jnp.bfloat16), "ctx").astype(jnp.float32),
    )
    owned = (
        lax.psum_scatter(
            paired[0].astype(jnp.bfloat16), "dp", scatter_dimension=0, tiled=True
        ).astype(jnp.float32),
        lax.psum_scatter(
            paired[1].astype(jnp.bfloat16), "dp", scatter_dimension=0, tiled=True
        ).astype(jnp.float32),
        lax.psum_scatter(
            paired[2].astype(jnp.bfloat16), "dp", scatter_dimension=0, tiled=True
        ).astype(jnp.float32),
        lax.psum_scatter(
            paired[3].astype(jnp.bfloat16), "dp", scatter_dimension=0, tiled=True
        ).astype(jnp.float32),
        lax.psum_scatter(
            paired[4].astype(jnp.bfloat16), "dp", scatter_dimension=1, tiled=True
        ).astype(jnp.float32),
        lax.psum_scatter(
            paired[5].astype(jnp.bfloat16), "dp", scatter_dimension=1, tiled=True
        ).astype(jnp.float32),
    )
    small = lax.psum(
        (
            small_sums[0],
            small_sums[1],
            small_sums[2],
            small_sums[3],
            small_sums[4],
            small_sums[5],
            small_sums[6],
            small_sums[7],
            small_sums[8],
        ),
        ("dp", "ctx", "tensor"),
    )
    return (
        block_out,
        grad_input,
        small[0],
        small[1],
        owned[0],
        owned[1],
        owned[2],
        small[2],
        small[3],
        owned[4],
        small[4],
        small[5],
        small[6],
        owned[3],
        small[7],
        owned[5],
        small[8],
    )


SPECS = (
    P("dp", ("ctx", "tensor"), None), P("dp", ("ctx", "tensor"), None), P("dp", None), P(), P(),
    P("dp", "tensor"), P("dp", "tensor"), P("dp", "tensor"), P(), P(), P("tensor", "dp"), P(), P(),
    P(), P("dp", "tensor"), P(), P("tensor", "dp"), P(),
)
OUT_SPECS = (
    P("dp", ("ctx", "tensor"), None), P("dp", ("ctx", "tensor"), None), P(), P(),
    P("dp", "tensor"), P("dp", "tensor"), P("dp", "tensor"), P(), P(), P("tensor", "dp"), P(), P(),
    P(), P("dp", "tensor"), P(), P("tensor", "dp"), P(),
)


def solution(mesh):
    lined_up = mesh.shape["dp"] == 4 and mesh.shape["tensor"] == 4 and mesh.shape["ctx"] == 2
    return jax.shard_map(
        body if lined_up else general_body, mesh=mesh, in_specs=SPECS, out_specs=OUT_SPECS, check_vma=False
    )
```

```python
import functools

import jax
import jax.numpy as jnp
from jax import lax
from jax.experimental import pallas as pl
from jax.experimental.pallas import tpu as pltpu
from jax.sharding import PartitionSpec as P

HDIM = 64
LANES = 256
ROOT_HALF = 0.7071067811865476
INV_ROOT_TWO_PI = 0.3989422804014327
MESH = pl.DeviceIdType.MESH
BF = jnp.bfloat16
F32 = jnp.float32
HIDE = -1e30


def dims(left, right, a, b):
    return lax.dot_general(left, right, (((a,), (b,)), ((), ())), preferred_element_type=F32)


def norm_parts(rows):
    centred = rows - jnp.mean(rows, axis=-1, keepdims=True)
    inverse = lax.rsqrt(jnp.mean(centred * centred, axis=-1, keepdims=True) + 1e-05)
    return centred * inverse, inverse


class Place:
    def __init__(self):
        self.d = lax.axis_index("dp")
        self.c = lax.axis_index("ctx")
        self.t = lax.axis_index("tensor")
        col, row = self.d % 2, self.d // 2
        self.dx = row * 2 + (1 - col)
        self.dy = (1 - row) * 2 + col
        self.dd = (1 - row) * 2 + (1 - col)
        self.h = self.t // 2
        self.g = self.t % 2
        self.mid = self.g + self.h * (1 - 2 * self.g)
        self.mate = 2 * self.h + 1 - self.g
        self.twin = (self.t + 2) % 4
        self.far_mid = 2 - self.h
        self.far_end = 3 * (1 - self.h)

    def source(self, k):
        first = 1 - jnp.minimum(k, 1)
        second = jnp.minimum(k, 1) * (1 - jnp.minimum(jnp.maximum(k - 1, 0), 1))
        third = jnp.minimum(jnp.maximum(k - 1, 0), 1) * (1 - jnp.maximum(k - 2, 0))
        fourth = jnp.maximum(k - 2, 0)
        return first * self.t + second * self.mate + third * self.far_mid + fourth * self.far_end


def remote(src, dst, send, recv, **where):
    return pltpu.make_async_remote_copy(
        src_ref=src, dst_ref=dst, send_sem=send, recv_sem=recv, device_id=where, device_id_type=MESH
    )


def greet(place):
    barrier = pltpu.get_barrier_semaphore()
    for k in range(1, 4):
        pl.semaphore_signal(
            barrier, inc=1, device_id={"tensor": (place.t + k) % 4}, device_id_type=MESH
        )
    for peer in (place.dx, place.dy, place.dd):
        pl.semaphore_signal(barrier, inc=1, device_id={"dp": peer}, device_id_type=MESH)
    pl.semaphore_signal(barrier, inc=1, device_id={"ctx": 1 - place.c}, device_id_type=MESH)
    for k in range(1, 4):
        where = {"ctx": 1 - place.c, "tensor": (place.t + k) % 4}
        pl.semaphore_signal(barrier, inc=1, device_id=where, device_id_type=MESH)
    return lambda: pl.semaphore_wait(barrier, 10)


class Several:
    def __init__(self, *copies):
        self.copies = copies

    def start(self):
        for copy in self.copies:
            copy.start()

    def wait_send(self):
        for copy in self.copies:
            copy.wait_send()

    def wait_recv(self):
        for copy in self.copies:
            copy.wait_recv()


def rows_at(start, size, step):
    return pl.ds(pl.multiple_of(start, step), size)


def erf_parts(values):
    cdf = 0.5 * (1.0 + lax.erf(values * ROOT_HALF))
    return cdf, cdf + values * (jnp.exp(-0.5 * values * values) * INV_ROOT_TWO_PI)


def add_to(target, *terms):
    total = target[...].astype(F32)
    for term in terms:
        total = total + term[...].astype(F32)
    target[...] = total.astype(BF)


def layer_kernel(
    hidden, cot, seg, gain_a, shift_a, wq_s, wk_s, wv_s, bias_q, bias_v, wo_s, bias_o, gain_f, shift_f,
    win_s, bias_in, wout_s, bias_out,
    block_out, grad_input, g_gain_a, g_shift_a, g_wq, g_wk, g_wv, g_bias_q, g_bias_v, g_wo, g_bias_o,
    g_gain_f, g_shift_f, g_win, g_bias_in, g_wout, g_bias_out,
    normed, far_rows, normed_turn, queries, kv, mixed_in, mixed_sib, q_land, wqkv, wo_land, wout, ffw,
    turn, q_turn, mixed, g_mix, keys_seg, left, left_in, left_turn, right, right_in, nf_out, nf_in,
    bf_out, bf_in, branch, branch_turn, part_wo, rxw, sumw, rzw, rx1, rx2, rz, wide, kv_out, kv_in, dqkv,
    gna, rzn, qkv_own, qkv_sib, qkv_in, qkv_sum, qkv_twin, sums, sums_core, sums_plane, sums_line,
    late, late_line, late_plane, res_ff, res_wo, res_qkv, bias_row, inner_rows,
    qt_send, q_send, q_recv, qc_send, qc_recv, z_send, z_recv, kvf_send, kvf_recv, mf_send, mf_recv,
    ct_send, cp_send, c_recv, cc_send, s_recv, wz_send, wz_recv, wp_send, wp_recv, wc_send, wc_recv,
    u_send, u_recv, l_send, l_recv, r_send, r_recv, n_send, n_recv, b_send, b_recv, x_send, x_recv,
    m_send, m_recv, p1_send, p1_recv, p2_send, p2_recv, zz_send, zz_recv, gp_send, gp_recv, gz_send, gz_recv,
    kv_send, kv_recv, rn_send, rn_recv, qs_send, qs_recv, qp_send, qp_recv, qz_send, qz_recv,
    f_send, f_recv, t_send, t_recv, ta_send, ta_recv, tb_send, tb_recv,
):
    at = Place()
    d, c, t, h, g = at.d, at.c, at.t, at.h, at.g
    other, away = 1 - c, 1 - h
    planes = (at.dx, at.dy, at.dd)
    others = [(t + k + 1) % 4 for k in range(3)]
    waits = []

    def begin(*copies):
        for copy in copies:
            copy.start()
            waits.append(copy)

    arrive = greet(at)

    for ref, start in ((wq_s, 0), (wk_s, LANES), (wv_s, 2 * LANES)):
        q_land[h, d, :, start + 128 : start + 256] = jnp.zeros((192, 128), BF)
        q_land[h, d, :, start : start + 192] = ref[...].astype(BF)
    arrive()

    def q_half(a, owner, which):
        return q_land.at[a, owner, rows_at(which * 96, 96, 96)]

    def q_piece(a, owner, n):
        if n is None:
            return q_half(a, owner, c), 0
        return q_land.at[a, owner, rows_at(c * 96 + n * 48, 48, 48)], n

    def q_plane(a, i, owner, n=None):
        block, n = q_piece(a, owner, n)
        return remote(block, block, q_send.at[a, i, n], q_recv.at[a, owner, n], dp=planes[i])

    def q_twin(n):
        block, n = q_piece(h, d, n)
        return remote(block, block, qt_send.at[n], q_recv.at[h, d, n], tensor=at.twin)

    def q_core(a, owner):
        half = q_half(a, owner, c)
        return remote(half, half, qc_send.at[a, owner], qc_recv.at[a, owner], ctx=other)

    def q_core_wait(a, owner):
        half = q_half(a, owner, other)
        remote(half, half, qc_send.at[a, owner], qc_recv.at[a, owner], ctx=other).wait_recv()

    def q_wait(a, owner, n=None):
        block, n = q_piece(a, owner, n)
        remote(block, block, qt_send.at[0], q_recv.at[a, owner, n], tensor=t).wait_recv()

    begin(q_twin(0), q_twin(1))
    for i in range(3):
        begin(q_plane(h, i, d))

    turned = wo_s[...].T
    turned = jnp.where(c == 0, turned[:96], turned[96:]).astype(BF)
    mine = rows_at(d * 192 + c * 96, 96, 96)
    wo_land[t, mine, 128:256] = jnp.zeros((96, 128), BF)
    wo_land[t, mine, 0:192] = turned

    def wo_rows(owner, which):
        return wo_land.at[:, rows_at(owner * 192 + which * 96, 96, 96)]

    def wo_line(k, owner):
        block = wo_land.at[owner, mine]
        return remote(block, block, wz_send.at[k], wz_recv.at[owner], tensor=others[k])

    def normed_rows(s):
        scaled, _ = norm_parts(hidden[s])
        return (scaled * gain_a[...].reshape(1, 768) + shift_a[...].reshape(1, 768)).astype(BF)

    def row_copy(src, owner, k, dest):
        return remote(src, normed.at[owner], z_send.at[k], z_recv.at[owner], tensor=dest)

    def row_wait(p):
        row_copy(normed.at[p], p, 0, t).wait_recv()

    pass_end = row_copy(normed.at[at.far_end], at.far_end, 2, at.mate)
    pass_mid = row_copy(normed.at[at.far_mid], at.far_mid, 3, at.mate)
    far_rows[...] = normed_rows(away)
    begin(row_copy(far_rows, t, 1, at.far_mid))
    normed[t] = normed_rows(h)
    begin(row_copy(normed.at[t], t, 0, at.mate))

    here = rows_at(d * 192, 192, 192)

    @pl.when(c == 0)
    def _():
        ffw[0, h, here, :] = win_s[...].astype(BF)

    @pl.when(c == 1)
    def _():
        ffw[1, h, here, :] = wout_s[...].astype(BF)

    def ff_block(which, a, owner):
        return ffw.at[which, a, rows_at(owner * 192, 192, 192)]

    def ff_half(which, a, owner, n):
        return ffw.at[which, a, rows_at(owner * 192 + n * 96, 96, 96)]

    def ff_twin(n):
        block = ff_half(c, h, d, n)
        return remote(block, block, ct_send.at[n], c_recv.at[h, d, n], tensor=at.twin)

    def ff_plane(axis, a, owner, n, dest):
        block = ff_half(c, a, owner, n)
        return remote(block, block, cp_send.at[axis, a, n], c_recv.at[a, owner, n], dp=dest)

    def ff_core(a, owner, n):
        block = ff_half(c, a, owner, n)
        return remote(block, block, cc_send.at[a, owner, n], s_recv.at[a, owner, n], ctx=other)

    def ff_wait(a, owner, n):
        block = ff_half(c, a, owner, n)
        remote(block, block, ct_send.at[n], c_recv.at[a, owner, n], dp=d).wait_recv()

    def ff_core_wait(a, owner, n):
        block = ff_half(other, a, owner, n)
        remote(block, block, cc_send.at[a, owner, n], s_recv.at[a, owner, n], ctx=other).wait_recv()

    ff_sends = []

    def ff_begin(*copies):
        for copy in copies:
            copy.start()
            ff_sends.append(copy)

    def spread(a, n):
        ff_begin(ff_plane(0, a, d, n, at.dx), ff_plane(1, a, d, n, at.dy), ff_core(a, d, n))

    def near_far(a):
        near = at.dx + a * (at.dy - at.dx)
        return near, at.dx + at.dy - near

    def diag(a, n):
        near, far = near_far(a)
        ff_wait(a, near, n)
        ff_begin(ff_plane(2, a, near, n, far), ff_core(a, near, n))
        ff_wait(a, far, n)
        ff_begin(ff_core(a, far, n))

    def last(a, n):
        ff_wait(a, at.dd, n)
        ff_begin(ff_core(a, at.dd, n))

    left[1, 0] = cot[...].reshape(256, 768).astype(BF)
    sums[...] = jnp.zeros_like(sums)
    late[...] = jnp.zeros_like(late)
    wide[...] = jnp.zeros_like(wide)
    part_wo[...] = jnp.zeros_like(part_wo)
    for p in range(2):

        @pl.when(g == p)
        def _(p=p):
            for a in range(2):
                cols = slice((p + 2 * a) * 192, (p + 2 * a) * 192 + 192)
                bias_row[:, a * 192 : a * 192 + 192] = bias_q[...].reshape(1, 768)[:, cols]
                bias_row[:, 768 + a * 192 : 960 + a * 192] = bias_v[...].reshape(1, 768)[:, cols]

    bias_row[:, 384:768] = jnp.zeros((1, 384), F32)
    for p in range(4):
        inner_rows[p] = bias_in[...].reshape(1, 3072)[:, p * 768 : (p + 1) * 768]

    row = jnp.where(h == 0, seg[0:1, :], seg[1:2, :])
    places = lax.broadcasted_iota(jnp.int32, (1, 1024), 1)
    row = jnp.where(row >= 0, row, -1 - places).astype(F32)
    seg_query = jnp.where(c == 0, row[:, :512], row[:, 512:])
    keys_seg[...] = jnp.broadcast_to(row, (128, 1024)).T

    for i in range(3):
        q_wait(h, planes[i])
        begin(q_core(h, planes[i]))
    for k in range(3):
        begin(wo_line(k, t))

    for n in range(2):
        q_wait(away, d, n)
        for i in range(3):
            begin(q_plane(away, i, d, n))
    begin(q_core(away, d))

    @pl.when(at.mid == 1)
    def _():
        row_wait(at.far_end)
        pass_end.start()
        row_wait(at.far_mid)
        pass_mid.start()

    for i in range(3):
        q_wait(away, planes[i], 0)
        q_wait(away, planes[i], 1)
        begin(q_core(away, planes[i]))
    for k in range(3):
        p = others[k]
        block = wo_land.at[p, mine]
        remote(block, block, wz_send.at[k], wz_recv.at[p], tensor=p).wait_recv()
    for i in range(3):
        begin(remote(wo_rows(d, c), wo_rows(d, c), wp_send.at[i], wp_recv.at[d], dp=planes[i]))
    begin(remote(wo_rows(d, c), wo_rows(d, c), wc_send.at[d], wc_recv.at[d], ctx=other))
    for n in range(2):
        spread(h, n)
    for i in range(3):
        q_core_wait(h, planes[i])
        q_core_wait(away, planes[i])
    q_core_wait(away, d)

    def gather_columns(i, carry):
        rows = rows_at(i * 192, 192, 192)
        for k in range(3):
            pair = [q_land[a, i, :, k * LANES : k * LANES + 192] for a in range(2)]
            wqkv[rows, k * 384 : (k + 1) * 384] = jnp.concatenate(pair, axis=1)
        return carry

    lax.fori_loop(0, 4, gather_columns, 0)

    def kvf_copy(p):
        block = kv.at[:, c, p]
        return remote(block, block, kvf_send.at[p], kvf_recv.at[p], ctx=other)

    def project(k, carry):
        p = at.source(k)

        @pl.when((k == 1) | ((k > 1) & (at.mid == 0)))
        def _():
            row_wait(p)

        out = jnp.dot(normed[p], wqkv[...], preferred_element_type=F32)
        out = (out + bias_row[...]).astype(BF)
        for u in range(3):
            cols = out[:, u * 128 : (u + 1) * 128]
            queries[u, rows_at(p * 128, 128, 128), :] = cols * jnp.asarray(HDIM**-0.5, BF)
        for u in range(6):
            kv[u, c, p] = out[:, 384 + u * 128 : 512 + u * 128]
        kvf_copy(p).start()
        return carry

    for n in range(2):
        ff_begin(ff_twin(n))
    begin(remote(left.at[1, 0], left.at[1, 1], u_send.at[1], u_recv.at[1], tensor=at.mate))
    lax.fori_loop(0, 4, project, 0)

    lane_head = lax.broadcasted_iota(jnp.int32, (1, 128), 1) // HDIM

    def head_pair(ref, u):
        return ref[u].reshape(1024, 128)

    def masked_scores(u, b, q_here):
        seg_here = jnp.where(b == 0, seg_query[:, :256], seg_query[:, 256:])
        scores = dims(head_pair(kv, u), q_here, 1, 1)
        column = keys_seg[...]
        visible = jnp.concatenate([column, column], axis=1) == seg_here
        return jnp.where(visible, scores, HIDE)

    def one_head(w, block):
        return jnp.where(lane_head == w, block.astype(F32), 0.0).astype(BF)

    def mf_copy(k, p):
        return remote(mixed.at[p], mixed_in.at[g, h], mf_send.at[k], mf_recv.at[t], tensor=p)

    for p in range(4):
        block = kv.at[:, other, p]
        remote(block, block, kvf_send.at[p], kvf_recv.at[p], ctx=other).wait_recv()
    for u in range(3):
        turn[u * 128 : (u + 1) * 128, :] = head_pair(kv, 3 + u).T

    def attend(b):
        block = rows_at(b * 256, 256, 256)

        def step(i, carry):
            u, w = i // 2, i % 2
            scores = masked_scores(u, b, one_head(w, queries[u, block, :]))
            peak = jnp.max(scores, axis=0, keepdims=True)
            expo = jnp.exp(scores - peak)
            total = jnp.sum(expo, axis=0, keepdims=True)
            rows = rows_at(i * HDIM, HDIM, HDIM)
            turned = jnp.dot(turn[rows, :], expo.astype(BF), preferred_element_type=F32)
            q_turn[rows, :] = turned / total
            return carry

        lax.fori_loop(0, 6, step, 0)
        mixed[pl.ds(2 * b, 2)] = q_turn[...].T.astype(BF).reshape(2, 128, 384)

    attend(away)
    mf_copy(0, 2 * away).start()
    mf_copy(1, 2 * away + 1).start()
    for n in range(2):
        diag(h, n)
    attend(h)
    mf_copy(2, at.mate).start()
    mixed_in[g, h] = mixed[t]
    ff_wait(away, d, 0)
    spread(away, 0)
    for n in range(2):
        last(h, n)
    for i in range(3):
        p = planes[i]
        remote(wo_rows(p, c), wo_rows(p, c), wp_send.at[i], wp_recv.at[p], dp=p).wait_recv()
        begin(remote(wo_rows(p, c), wo_rows(p, c), wc_send.at[p], wc_recv.at[p], ctx=other))
    normed_turn[...] = normed[...].reshape(512, 768).T
    for p in range(4):
        remote(wo_rows(p, other), wo_rows(p, other), wc_send.at[p], wc_recv.at[p], ctx=other).wait_recv()
    for p in range(2):
        for i in range(4):
            rows = slice(i * 192, (i + 1) * 192)
            pair = [wo_land[p + 2 * a, rows, :192] for a in range(2)]
            wout[p, rows, :] = jnp.concatenate(pair, axis=1)
    ff_wait(away, d, 1)
    spread(away, 1)
    diag(away, 0)

    for k in range(3):
        p = others[k]
        block = mixed_in.at[p % 2, p // 2]
        remote(block, block, mf_send.at[k], mf_recv.at[p], tensor=p).wait_recv()
    for s in range(2):
        total = hidden[s] + bias_o[...].reshape(1, 768)
        for p in range(2):
            total = total + dims(mixed_in[p, s], wout[p], 1, 1)
        block_out[s] = total
        scaled, _ = norm_parts(total)
        left[0, 0, s * 128 : (s + 1) * 128, :] = (
            scaled * gain_f[...].reshape(1, 768) + shift_f[...].reshape(1, 768)
        ).astype(BF)
    begin(remote(left.at[0, 0], left.at[0, 1], u_send.at[0], u_recv.at[0], tensor=at.mate))
    begin(remote(mixed_in, mixed_sib, x_send.at[0], x_recv.at[0], ctx=other))

    diag(away, 1)
    for p in range(4):
        for n in range(2):
            ff_core_wait(h, p, n)

    def right_copy(a, r):
        return remote(
            right.at[other, a, r], right_in.at[a, r], r_send.at[a, r], r_recv.at[a, r], ctx=other
        )

    def units(a, r):
        unit = g + 2 * a
        top = pl.multiple_of(r * 512, 512)
        for j in range(3):
            cols = slice(j * 256, (j + 1) * 256)
            w_in, w_out = ffw[0, a, :, cols], ffw[1, a, :, cols]
            inner = jnp.dot(left[0, r], w_in, preferred_element_type=F32) + inner_rows[unit, :, cols]
            cdf, slope = erf_parts(inner)
            active = (inner * cdf).astype(BF)
            right[1, a, r, :, cols] = active
            grad_inner = jnp.dot(left[1, r], w_out, preferred_element_type=F32) * slope
            grad_inner = grad_inner.astype(BF)
            right[0, a, r, :, cols] = grad_inner
            sums[pl.ds(6 + unit, 1), cols] += jnp.sum(grad_inner.astype(F32), axis=0, keepdims=True)
            up, down = dims(active, w_out, 1, 1), dims(grad_inner, w_in, 1, 1)
            for k in range(6):
                wide[k, pl.ds(top, 256), :] += up[:, k * 128 : (k + 1) * 128]
                wide[k, pl.ds(top + 256, 256), :] += down[:, k * 128 : (k + 1) * 128]
        right_copy(a, r).start()

    def wide_rows(start, size=64):
        return jnp.concatenate([wide[k, start : start + size, :] for k in range(6)], axis=1)

    def own_slot(r, carry):
        @pl.when(r == 1)
        def _():
            for which in range(2):
                block = left.at[which, 1]
                remote(block, block, u_send.at[which], u_recv.at[which], tensor=at.mate).wait_recv()
            left_copy.start()

        units(h, r)
        return carry

    left_copy = remote(left.at[other], left_in, l_send.at[0], l_recv.at[0], ctx=other)
    waits.append(left_copy)
    lax.fori_loop(0, 2, own_slot, 0)
    for n in range(2):
        last(away, n)
    for p in range(4):
        for n in range(2):
            ff_core_wait(away, p, n)

    nf_copy = remote(nf_out, nf_in, n_send.at[0], n_recv.at[0], tensor=at.mate)
    waits.append(nf_copy)
    for copy in ff_sends:
        copy.wait_send()

    def turn_left():
        left_turn[0] = left[c, 0].T
        left_turn[1] = left[c, 1].T
        remote(left.at[c], left_in, l_send.at[0], l_recv.at[0], ctx=other).wait_recv()
        left_turn[2] = left_in[0].T
        left_turn[3] = left_in[1].T

    def first(a, j):
        near, _ = near_far(a)
        owner = near if j == 0 else at.dd
        return remote(ff_block(0, a, owner), rx1.at[a, j], p1_send.at[a, j], p1_recv.at[a, j], dp=near)

    def second(a):
        _, far = near_far(a)
        return remote(ff_block(0, a, far), rx2.at[a], p2_send.at[a], p2_recv.at[a], dp=far)

    def to_second(a):
        _, far = near_far(a)
        first(a, 1).wait_recv()
        add_to(ff_block(0, a, far), rx1.at[a, 1])
        second(a).start()
        first(a, 0).start()

    def plane_done(a):
        first(a, 0).wait_recv()
        second(a).wait_recv()
        add_to(ff_block(0, a, d), rx1.at[a, 0], rx2.at[a])

    def weight_gradient(a):
        for r in range(2):
            right_copy(a, r).wait_recv()

        def rows_of(q, carry):
            rows = rows_at(q * 192, 192, 192)
            out = jnp.dot(left_turn[0, rows, :], right[c, a, 0], preferred_element_type=F32)
            out = out + jnp.dot(left_turn[1, rows, :], right[c, a, 1], preferred_element_type=F32)
            out = out + jnp.dot(left_turn[2, rows, :], right_in[a, 0], preferred_element_type=F32)
            out = out + jnp.dot(left_turn[3, rows, :], right_in[a, 1], preferred_element_type=F32)
            ffw[0, a, rows, :] = out.astype(BF)
            return carry

        lax.fori_loop(0, 4, rows_of, 0)
        first(a, 1).start()

    def twin_slot(i, carry):
        @pl.when(i == 1)
        def _():
            for q in range(4):
                rows = slice(q * 64, (q + 1) * 64)
                nf_out[rows, :] = wide_rows(768 + q * 64).astype(BF)
            nf_copy.start()
            turn_left()
            weight_gradient(h)

        units(away, 1 - i)
        return carry

    lax.fori_loop(0, 2, twin_slot, 0)
    weight_gradient(away)
    for q in range(4):
        rows = slice(q * 64, (q + 1) * 64)
        bf_out[rows, :] = wide_rows(512 + q * 64).astype(BF)

    def add_row(i, value):
        sums[i : i + 1, :] += jnp.sum(value, axis=0, keepdims=True)

    def norm_back(source, grad_out, gain):
        scaled, inverse = norm_parts(source)
        grad_scaled = grad_out * gain[...].reshape(1, 768)
        plain = jnp.mean(grad_scaled, axis=-1, keepdims=True)
        cross = jnp.mean(grad_scaled * scaled, axis=-1, keepdims=True)
        return inverse * (grad_scaled - plain - scaled * cross), scaled

    nf_copy.wait_recv()
    to_second(h)
    for s in range(2):
        for half in range(2):
            rows = slice(half * 64, half * 64 + 64)
            start = s * 128 + half * 64
            cot_here = cot[s, rows, :]
            grad_out = wide_rows(256 + start) + nf_in[start : start + 64, :].astype(F32)
            middle = block_out[s, rows, :]
            grad_rows, scaled = norm_back(middle, grad_out, gain_f)
            block_out[s, rows, :] = middle + wide_rows(start) + bias_out[...].reshape(1, 768)
            grad_rows = grad_rows + cot_here
            grad_input[s, rows, :] = grad_rows
            branch[0, start : start + 64, :] = grad_rows.astype(BF)
            add_row(2, grad_out * scaled)
            add_row(3, grad_out)
            add_row(4, grad_rows)
            add_row(5, cot_here)
    begin(remote(branch.at[0], branch.at[1], b_send.at[0], b_recv.at[0], ctx=other))

    def m_copy(k):
        p = others[k]
        return remote(mixed.at[p], g_mix.at[t], m_send.at[k], m_recv.at[t], tensor=p)

    mf_copy(0, 2 * away).wait_send()
    mf_copy(1, 2 * away + 1).wait_send()
    mf_copy(2, at.mate).wait_send()
    for p in range(2):
        out = jnp.dot(branch[0], wout[p], preferred_element_type=F32).astype(BF)
        for s in range(2):
            mixed[2 * s + p] = out[s * 128 : (s + 1) * 128, :]
    for k in range(3):
        begin(m_copy(k))
    g_mix[t] = mixed[t]

    branch_turn[0] = branch[0].T
    remote(branch.at[0], branch.at[1], b_send.at[0], b_recv.at[0], ctx=other).wait_recv()
    branch_turn[1] = branch[1].T
    remote(mixed_in, mixed_sib, x_send.at[0], x_recv.at[0], ctx=other).wait_recv()
    for p in range(2):
        for q in range(4):
            rows = slice(q * 192, (q + 1) * 192)
            out = jnp.dot(branch_turn[0, rows, :], mixed_in[p].reshape(256, 384), preferred_element_type=F32)
            out = out + jnp.dot(
                branch_turn[1, rows, :], mixed_sib[p].reshape(256, 384), preferred_element_type=F32
            )
            for a in range(2):
                part_wo[p + 2 * a, rows, :192] = out[:, a * 192 : (a + 1) * 192].astype(BF)

    def wo_part(owner):
        return part_wo.at[:, rows_at(owner * 192 + c * 96, 96, 96)]

    to_second(away)
    for i in range(3):
        begin(remote(wo_part(planes[i]), rxw.at[d], gp_send.at[i], gp_recv.at[d], dp=planes[i]))

    zz_copy = remote(ff_block(0, away, d), rz, zz_send.at[0], zz_recv.at[0], tensor=at.twin)
    waits.append(zz_copy)

    for u in range(3):
        turn[u * 128 : (u + 1) * 128, :] = head_pair(kv, u).T
    wide[...] = jnp.zeros_like(wide)

    def m_wait(p):
        block = g_mix.at[p]
        remote(block, block, m_send.at[0], m_recv.at[p], tensor=p).wait_recv()

    theirs = rows_at(other * 512, 512, 512)
    ours = rows_at(c * 512, 512, 512)

    def kv_copy(u):
        return remote(kv_out.at[u], kv_in.at[u], kv_send.at[u], kv_recv.at[u], ctx=other)

    gz_copies = [
        remote(sumw.at[p], rzw.at[t], gz_send.at[k], gz_recv.at[t], tensor=p) for k, p in enumerate(others)
    ]
    waits.extend(gz_copies)

    def wo_plane_done():
        for i in range(3):
            p = planes[i]
            remote(wo_part(p), rxw.at[p], gp_send.at[i], gp_recv.at[p], dp=p).wait_recv()
        total = part_wo[:, mine, :].astype(F32)
        for i in range(3):
            total = total + rxw[planes[i]].astype(F32)
        sumw[...] = total.astype(BF)
        for copy in gz_copies:
            copy.start()

    def attend_back(b, last):
        block = rows_at(b * 256, 256, 256)

        def step(u, carry):
            cols = pl.ds(pl.multiple_of(u * 128, 128), 128)
            g_pair = g_mix[pl.ds(2 * b, 2), :, cols].reshape(256, 128)
            for w in range(2):
                q_here = one_head(w, queries[u, block, :])
                g_here = one_head(w, g_pair)
                scores = masked_scores(u, b, q_here)
                peak = jnp.max(scores, axis=0, keepdims=True)
                expo = jnp.exp(scores - peak)
                probs = expo * (1.0 / jnp.sum(expo, axis=0, keepdims=True))
                grad_probs = dims(head_pair(kv, 3 + u), g_here, 1, 1)
                centre = jnp.sum(probs * grad_probs, axis=0, keepdims=True)
                wide[3 + u] += jnp.dot(probs.astype(BF), g_here, preferred_element_type=F32)
                grad_scores = (probs * (grad_probs - centre)).astype(BF)
                wide[u] += jnp.dot(grad_scores, q_here, preferred_element_type=F32)
                rows = rows_at(u * 128 + w * HDIM, HDIM, HDIM)
                q_turn[rows, :] = jnp.dot(turn[rows, :], grad_scores, preferred_element_type=F32)
            if not last:

                @pl.when(u == 1)
                def _():
                    plane_done(away)
                    zz_copy.start()

            if last:
                @pl.when(u == 0)
                def _():
                    plane_done(h)

                @pl.when(u == 2)
                def _():
                    wo_plane_done()

                kv_out[u, :, :128] = wide[u, theirs, :].astype(BF)
                kv_out[u, :, 128:] = wide[3 + u, theirs, :].astype(BF)
                kv_copy(u).start()
            return carry

        lax.fori_loop(0, 3, step, 0)
        dqkv[block, :384] = (q_turn[...].T * HDIM**-0.5).astype(BF)

    m_wait(at.mate)
    begin(remote(bf_out, bf_in, n_send.at[1], n_recv.at[1], tensor=at.mate))
    attend_back(h, False)
    m_wait(at.far_mid)
    m_wait(at.far_end)
    attend_back(away, True)

    def part_cols(k):
        return pl.ds(0, 384) if k == 0 else pl.ds(384, 768)

    def sib_copy(k):
        block, landing = qkv_sib.at[0, :, :, part_cols(k)], qkv_sib.at[1, :, :, part_cols(k)]
        return remote(block, landing, qs_send.at[k], qs_recv.at[k], ctx=other)

    def qkv_part(k):
        def rows_of(i, carry):
            rows = rows_at(i * 192, 192, 192)
            out = jnp.dot(normed_turn[rows, :], dqkv[:, part_cols(k)], preferred_element_type=F32)
            qkv_own[i, :, part_cols(k)] = jnp.where(c == 0, out[:96], out[96:])
            qkv_sib[0, i, :, part_cols(k)] = jnp.where(c == 0, out[96:], out[:96]).astype(BF)
            return carry

        lax.fori_loop(0, 4, rows_of, 0)
        begin(sib_copy(k))

    def qkv_out(k):
        sib_copy(k).wait_recv()
        cols = part_cols(k)
        for p in range(4):
            qkv_in[0, p, :, cols] = (qkv_own[p, :, cols] + qkv_sib[1, p, :, cols].astype(F32)).astype(BF)
        for i in range(3):
            block, landing = qkv_in.at[0, planes[i], :, cols], qkv_in.at[1, d, :, cols]
            begin(remote(block, landing, qp_send.at[k, i], qp_recv.at[k, d], dp=planes[i]))
        qkv_in[1, d, :, cols] = qkv_in[0, d, :, cols]

    def twin_copy(k):
        cols = pl.ds(0, LANES) if k == 0 else pl.ds(LANES, 2 * LANES)
        block, landing = qkv_twin.at[0, :, cols], qkv_twin.at[1, :, cols]
        return remote(block, landing, qz_send.at[k], qz_recv.at[k], tensor=at.twin)

    def qkv_to_twin(k):
        for i in range(3):
            block = qkv_in.at[1, planes[i], :, part_cols(k)]
            remote(block, block, qp_send.at[k, i], qp_recv.at[k, planes[i]], dp=d).wait_recv()
        for j in ((0,), (1, 2))[k]:
            cols = slice(j * 384, (j + 1) * 384)
            total = qkv_in[1, 0, :, cols].astype(F32)
            for p in range(1, 4):
                total = total + qkv_in[1, p, :, cols].astype(F32)
            low, high = total[:, :192], total[:, 192:]
            qkv_sum[0, :, j * LANES : j * LANES + 192] = jnp.where(h == 0, low, high)
            qkv_twin[0, :, j * LANES : j * LANES + 192] = jnp.where(h == 0, high, low).astype(BF)
        begin(twin_copy(k))

    qkv_part(0)


    for u in range(3):
        kv_copy(u).wait_recv()
        for k in range(2):
            cols = slice(384 * (k + 1) + u * 128, 384 * (k + 1) + (u + 1) * 128)
            theirs_here = kv_in[u, :, k * 128 : (k + 1) * 128].astype(F32)
            dqkv[:, cols] = (wide[3 * k + u, ours, :] + theirs_here).astype(BF)

    qkv_out(0)

    def line_copy(owner, slot, k, dest):
        return remote(gna.at[owner], rzn.at[slot], rn_send.at[k], rn_recv.at[slot], tensor=dest)

    def line_wait(slot):
        line_copy(t, slot, 0, t).wait_recv()

    by_mate = [line_copy(at.far_end, 2, 1, at.mate), line_copy(at.far_mid, 3, 2, at.mate)]
    on_sums = [line_copy(at.far_end, 1, 1, at.far_end), line_copy(at.far_mid, 1, 2, at.far_mid)]

    def rows_back(p):
        rows = dqkv[rows_at(p * 128, 128, 128), :]
        gna[p] = dims(rows, wqkv[...], 1, 1).astype(BF)

    for i, p in enumerate((at.far_end, at.far_mid)):
        rows_back(p)

        @pl.when(at.mid == 0)
        def _(i=i):
            by_mate[i].start()

    rows_back(at.mate)
    begin(line_copy(at.mate, 0, 0, at.mate))
    rows_back(t)
    total = jnp.sum(dqkv[...].astype(F32), axis=0, keepdims=True)
    sums[pl.ds(10 + g, 1), :384] = total[:, :384]
    sums[pl.ds(10 + g, 1), 384:] = total[:, 768:]

    core_sum = remote(sums, sums_core, t_send.at[0], t_recv.at[0], ctx=other)
    begin(core_sum)

    def plane_sum(k, owner):
        block = sums_plane.at[owner]
        return remote(block, block, t_send.at[1 + k], t_recv.at[1 + owner], dp=planes[k])

    def line_sum(k, owner):
        block = sums_line.at[owner]
        return remote(block, block, t_send.at[4 + k], t_recv.at[5 + owner], tensor=others[k])

    qkv_part(1)
    @pl.when(at.mid == 1)
    def _():
        for i, p in enumerate((at.far_end, at.far_mid)):
            line_wait(2 + i)
            add_to(gna.at[p], rzn.at[2 + i])
            on_sums[i].start()

    core_sum.wait_recv()
    sums_plane[d] = sums[...] + sums_core[...]
    for k in range(3):
        begin(plane_sum(k, d))
    qkv_out(1)
    qkv_to_twin(0)

    def result_copy(i, ref):
        return remote(ref.at[c], ref.at[c], f_send.at[i], f_recv.at[i], ctx=other)

    remote(rz, rz, zz_send.at[0], zz_recv.at[0], tensor=t).wait_recv()
    res_ff[c] = ffw[0, h, here, :].astype(F32) + rz[...].astype(F32)
    begin(result_copy(1, res_ff))
    rzw[t] = sumw[t]
    for k in range(3):
        p = others[k]
        remote(rzw.at[p], rzw.at[p], gz_send.at[k], gz_recv.at[p], tensor=p).wait_recv()
    total = rzw[0].astype(F32)
    for p in range(1, 4):
        total = total + rzw[p].astype(F32)
    res_wo[c] = total
    begin(result_copy(2, res_wo))

    for k in range(3):
        plane_sum(k, planes[k]).wait_recv()
    sums_line[t] = (sums_plane[0] + sums_plane[1]) + (sums_plane[2] + sums_plane[3])
    for k in range(3):
        begin(line_sum(k, t))

    qkv_to_twin(1)

    remote(bf_out, bf_in, n_send.at[1], n_recv.at[1], tensor=at.mate).wait_recv()
    for s in range(2):
        block_out[s] += bf_in[s * 128 : (s + 1) * 128, :].astype(F32)

    for slot in range(2):
        line_wait(slot)

    for s in range(2):
        for half in range(2):
            rows = slice(half * 64, half * 64 + 64)
            near = gna[t, rows, :].astype(F32) + rzn[0, rows, :].astype(F32)
            grad_out = jnp.where(h == s, near, rzn[1, rows, :].astype(F32))
            grad_rows, scaled = norm_back(hidden[s, rows, :], grad_out, gain_a)
            grad_input[s, rows, :] += grad_rows
            late[0:1, :] += jnp.sum(grad_out * scaled, axis=0, keepdims=True)
            late[1:2, :] += jnp.sum(grad_out, axis=0, keepdims=True)

    late_line[c, t] = late[...]
    peers = [(c, p) for p in others] + [(other, p) for p in others] + [(other, t)]
    for k, (core, p) in enumerate(peers):
        block = late_line.at[c, t]
        begin(remote(block, block, ta_send.at[k], ta_recv.at[c, t], ctx=core, tensor=p))
    for k in range(2):
        twin_copy(k).wait_recv()
    res_qkv[c] = qkv_sum[0] + qkv_twin[1].astype(F32)
    begin(result_copy(0, res_qkv))
    for k, (core, p) in enumerate(peers):
        block = late_line.at[core, p]
        remote(block, block, ta_send.at[k], ta_recv.at[core, p], ctx=core, tensor=p).wait_recv()
    total = late_line[0, 0]
    for k in range(1, 8):
        total = total + late_line[k // 4, k % 4]
    late_plane[d] = total
    for k in range(3):
        block = late_plane.at[d]
        begin(remote(block, block, tb_send.at[k], tb_recv.at[d], dp=planes[k]))

    for i, ref in enumerate((res_qkv, res_ff, res_wo)):
        block = ref.at[other]
        remote(block, block, f_send.at[i], f_recv.at[i], ctx=other).wait_recv()
    for which in range(2):
        rows = slice(which * 96, (which + 1) * 96)
        for ref, start in ((g_wq, 0), (g_wk, LANES), (g_wv, 2 * LANES)):
            ref[rows, :] = res_qkv[which, :, start : start + 192]
    g_win[...] = res_ff[0]
    g_wout[...] = res_ff[1]
    g_wo[...] = res_wo[...].reshape(192, LANES).T[:192, :]

    for k in range(3):
        line_sum(k, others[k]).wait_recv()
    total = (sums_line[0] + sums_line[1]) + (sums_line[2] + sums_line[3])
    for i, ref in enumerate((g_gain_f, g_shift_f, g_bias_o, g_bias_out)):
        ref[...] = total[2 + i]
    g_bias_in[...] = jnp.concatenate([total[6 + i : 7 + i, :] for i in range(4)], axis=1).reshape(3072)
    for ref, start in ((g_bias_q, 0), (g_bias_v, 384)):
        pieces = []
        for p in range(4):
            first_lane = start + (p // 2) * 192
            pieces.append(total[10 + p % 2 : 11 + p % 2, first_lane : first_lane + 192])
        ref[...] = jnp.concatenate(pieces, axis=1).reshape(768)
    for k in range(3):
        block = late_plane.at[planes[k]]
        remote(block, block, tb_send.at[k], tb_recv.at[planes[k]], dp=d).wait_recv()
    total = (late_plane[0] + late_plane[1]) + (late_plane[2] + late_plane[3])
    g_gain_a[...] = total[0]
    g_shift_a[...] = total[1]

    for copy in waits:
        copy.wait_send()
    for p in range(4):
        kvf_copy(p).wait_send()
    for u in range(3):
        kv_copy(u).wait_send()
    for a in range(2):
        first(a, 0).wait_send()
        first(a, 1).wait_send()
        second(a).wait_send()
        for r in range(2):
            right_copy(a, r).wait_send()

    @pl.when(at.mid == 1)
    def _():
        pass_end.wait_send()
        pass_mid.wait_send()
        for copy in on_sums:
            copy.wait_send()

    @pl.when(at.mid == 0)
    def _():
        for copy in by_mate:
            copy.wait_send()


def deliver_kernel(*refs):
    count = (len(refs) - 2) // 3
    made, outs, held = refs[:count], refs[count : 2 * count], refs[2 * count : 3 * count]
    fetches = [pltpu.make_async_copy(made[i], held[i], refs[-2].at[i]) for i in range(count)]
    puts = [pltpu.make_async_copy(held[i], outs[i], refs[-1].at[i]) for i in range(count)]
    for fetch in fetches:
        fetch.start()
    for fetch, put in zip(fetches, puts):
        fetch.wait()
        put.start()
    for put in puts:
        put.wait()


VM = pl.BlockSpec(memory_space=pltpu.VMEM)
ANY = pl.BlockSpec(memory_space=pl.ANY)


def body(*operands):
    struct = jax.ShapeDtypeStruct
    dma = pltpu.SemaphoreType.DMA
    vm = pltpu.VMEM
    operands = operands[:16] + (operands[16].T, operands[17])
    hidden, cotangent, _, gain, _, wq, wk, wv, bq, bv, wo, bo, gf, sf, win, bin_, wout, bout = operands
    results = (hidden, hidden, gain, gain, wq, wk, wv, bq, bv, wo, bo, gf, sf, win, bin_, wout, bout)
    shapes = tuple(struct(r.shape, F32) for r in results)
    made = pl.pallas_call(
        layer_kernel,
        out_shape=shapes,
        in_specs=[VM] * len(operands),
        out_specs=(VM,) * len(results),
        scratch_shapes=[
            vm((4, 128, 768), BF),
            vm((128, 768), BF),
            vm((768, 512), BF),
            vm((3, 512, 128), BF),
            vm((6, 2, 4, 128, 128), BF),
            vm((2, 2, 128, 384), BF),
            vm((2, 2, 128, 384), BF),
            vm((2, 4, 192, 768), BF),
            vm((768, 1152), BF),
            vm((4, 768, LANES), BF),
            vm((2, 768, 384), BF),
            vm((2, 2, 768, 768), BF),
            vm((384, 1024), BF),
            vm((384, 256), F32),
            vm((4, 128, 384), BF),
            vm((4, 128, 384), BF),
            vm((1024, 128), F32),
            vm((2, 2, 256, 768), BF),
            vm((2, 256, 768), BF),
            vm((4, 768, 256), BF),
            vm((2, 2, 2, 256, 768), BF),
            vm((2, 2, 256, 768), BF),
            vm((256, 768), BF),
            vm((256, 768), BF),
            vm((256, 768), BF),
            vm((256, 768), BF),
            vm((2, 256, 768), BF),
            vm((2, 768, 256), BF),
            vm((4, 768, LANES), BF),
            vm((4, 4, 96, LANES), BF),
            vm((4, 96, LANES), BF),
            vm((4, 96, LANES), BF),
            vm((2, 2, 192, 768), BF),
            vm((2, 192, 768), BF),
            vm((192, 768), BF),
            vm((6, 1024, 128), F32),
            vm((3, 512, 256), BF),
            vm((3, 512, 256), BF),
            vm((512, 1152), BF),
            vm((4, 128, 768), BF),
            vm((4, 128, 768), BF),
            vm((4, 96, 1152), F32),
            vm((2, 4, 96, 1152), BF),
            vm((2, 4, 96, 1152), BF),
            vm((1, 96, 768), F32),
            vm((2, 96, 768), BF),
            vm((16, 768), F32),
            vm((16, 768), F32),
            vm((4, 16, 768), F32),
            vm((4, 16, 768), F32),
            vm((2, 768), F32),
            vm((2, 4, 2, 768), F32),
            vm((4, 2, 768), F32),
            vm((2, 192, 768), F32),
            vm((2, 96, LANES), F32),
            vm((2, 96, 768), F32),
            vm((1, 1152), F32),
            vm((4, 1, 768), F32),
            dma((2,)), dma((2, 3, 2)), dma((2, 4, 2)), dma((2, 4)), dma((2, 4)),
            dma((4,)), dma((4,)), dma((4,)), dma((4,)), dma((3,)), dma((4,)),
            dma((2,)), dma((3, 2, 2)), dma((2, 4, 2)), dma((2, 4, 2)), dma((2, 4, 2)),
            dma((3,)), dma((4,)), dma((3,)), dma((4,)), dma((4,)), dma((4,)),
            dma((2,)), dma((2,)), dma((1,)), dma((1,)), dma((2, 2)), dma((2, 2)),
            dma((2,)), dma((2,)), dma((1,)), dma((1,)), dma((1,)), dma((1,)),
            dma((3,)), dma((4,)),
            dma((2, 2)), dma((2, 2)), dma((2,)), dma((2,)), dma((1,)), dma((1,)),
            dma((3,)), dma((4,)), dma((3,)), dma((4,)),
            dma((3,)), dma((3,)), dma((3,)), dma((4,)),
            dma((2,)), dma((2,)), dma((2, 3)), dma((2, 4)), dma((2,)), dma((2,)),
            dma((3,)), dma((3,)), dma((7,)), dma((9,)),
            dma((7,)), dma((2, 4)), dma((3,)), dma((4,)),
        ],
        compiler_params=pltpu.CompilerParams(
            collective_id=1, has_side_effects=True, vmem_limit_bytes=63 << 20
        ),
        name="layer",
    )(*operands)
    made = pl.pallas_call(
        deliver_kernel,
        out_shape=shapes,
        in_specs=[ANY] * len(shapes),
        out_specs=(ANY,) * len(shapes),
        scratch_shapes=[vm(r.shape, F32) for r in shapes] + [dma((len(shapes),))] * 2,
        name="deliver",
    )(*made)
    return tuple(made[:15]) + (made[15].T, made[16])


root_half = 0.7071067811865476
inv_root_two_pi = 0.3989422804014327


def general_gate(values):
    return values * (0.5 * (1.0 + lax.erf(values * root_half)))


def general_slope(values):
    normal_cdf = 0.5 * (1.0 + lax.erf(values * root_half))
    normal_pdf = jnp.exp(-0.5 * values * values) * inv_root_two_pi
    return normal_cdf + values * normal_pdf


def general_norm(rows, gain, shift):
    centred = rows - jnp.mean(rows, axis=-1, keepdims=True)
    inverse = lax.rsqrt(jnp.mean(centred * centred, axis=-1, keepdims=True) + 1e-05)
    scaled = centred * inverse
    return (scaled * gain + shift, scaled, inverse)


def general_norm_backward(grad_out, scaled, inverse, gain):
    grad_scaled = grad_out * gain
    plain_mean = jnp.mean(grad_scaled, axis=-1, keepdims=True)
    cross_mean = jnp.mean(grad_scaled * scaled, axis=-1, keepdims=True)
    grad_rows = inverse * (grad_scaled - plain_mean - scaled * cross_mean)
    return (grad_rows, jnp.sum(grad_out * scaled, axis=0), jnp.sum(grad_out, axis=0))


def tensor_rows(block):
    return lax.all_gather(block, "tensor", axis=0, tiled=True)


def tensor_sums(block):
    return lax.psum_scatter(block, "tensor", scatter_dimension=0, tiled=True)


def fetch_weights(shards):
    return (
        lax.all_gather(shards[0], "dp", axis=0, tiled=True),
        lax.all_gather(shards[1], "dp", axis=0, tiled=True),
        lax.all_gather(shards[2], "dp", axis=0, tiled=True),
        lax.all_gather(shards[3], "dp", axis=0, tiled=True),
        lax.all_gather(shards[4], "dp", axis=1, tiled=True),
        lax.all_gather(shards[5], "dp", axis=1, tiled=True),
    )


def general_piece(piece, total, start):
    return lax.dynamic_update_slice(jnp.zeros((total,), jnp.float32), piece, (start,))


def general_body(
    hidden_in,
    cotangent,
    segment_ids,
    attn_gain,
    attn_shift,
    query_weight,
    key_weight,
    value_weight,
    query_bias,
    value_bias,
    output_weight,
    output_bias,
    ffn_gain,
    ffn_shift,
    inner_weight,
    inner_bias,
    outer_weight,
    outer_bias,
):
    width = hidden_in.shape[2]
    part_width = query_weight.shape[1]
    unit_width = inner_weight.shape[1]
    unit_total = inner_bias.shape[0]
    heads_here = part_width // HDIM
    tensor_at = lax.axis_index("tensor")
    ctx_at = lax.axis_index("ctx")
    half_rows = hidden_in.shape[1] * lax.axis_size("tensor")
    seq_rows = segment_ids.shape[1]
    factor = HDIM ** (-0.5)
    query_piece = lax.dynamic_slice_in_dim(query_bias, tensor_at * part_width, part_width)
    value_piece = lax.dynamic_slice_in_dim(value_bias, tensor_at * part_width, part_width)
    inner_piece = lax.dynamic_slice_in_dim(inner_bias, tensor_at * unit_width, unit_width)
    shards = (
        query_weight.astype(jnp.bfloat16),
        key_weight.astype(jnp.bfloat16),
        value_weight.astype(jnp.bfloat16),
        inner_weight.astype(jnp.bfloat16),
        output_weight.astype(jnp.bfloat16),
        outer_weight.astype(jnp.bfloat16),
    )
    key_index = jnp.arange(seq_rows)
    query_index = ctx_at * half_rows + jnp.arange(half_rows)

    def masked_scores(queries, key_all, allowed):
        scores = (
            jnp.einsum("qhd,khd->hqk", queries, key_all, preferred_element_type=jnp.float32)
            * factor
        )
        return jnp.where(allowed[None, :, :], scores, -1e30)

    def micro(weights_bf, carry, item):
        w_query, w_key, w_value, w_inner, w_output, w_outer = weights_bf
        rows, cot_rows, segment_row = item
        query_seg = lax.dynamic_slice_in_dim(segment_row, ctx_at * half_rows, half_rows)
        allowed = (query_seg[:, None] == segment_row[None, :]) & (
            (segment_row[None, :] >= 0) | (query_index[:, None] == key_index[None, :])
        )
        normed, scaled_a, inverse_a = general_norm(rows, attn_gain, attn_shift)
        normed_all = tensor_rows(normed.astype(jnp.bfloat16))
        queries = (
            jnp.dot(normed_all, w_query, preferred_element_type=jnp.float32) + query_piece
        ).astype(jnp.bfloat16)
        key_half = jnp.dot(normed_all, w_key, preferred_element_type=jnp.float32).astype(
            jnp.bfloat16
        )
        value_half = (
            jnp.dot(normed_all, w_value, preferred_element_type=jnp.float32) + value_piece
        ).astype(jnp.bfloat16)
        key_all, value_all = (
            lax.all_gather(key_half, "ctx", axis=0, tiled=True),
            lax.all_gather(value_half, "ctx", axis=0, tiled=True),
        )
        queries = queries.reshape(half_rows, heads_here, HDIM)
        key_all = key_all.reshape(seq_rows, heads_here, HDIM)
        value_all = value_all.reshape(seq_rows, heads_here, HDIM)
        masked = masked_scores(queries, key_all, allowed)
        peak = jnp.max(masked, axis=-1, keepdims=True)
        expo = jnp.exp(masked - peak)
        total = jnp.sum(expo, axis=-1, keepdims=True)
        log_total = peak + jnp.log(total)
        probs = (expo / total).astype(jnp.bfloat16)
        mixed = jnp.einsum("hqk,khd->qhd", probs, value_all, preferred_element_type=jnp.float32)
        mixed = mixed.reshape(half_rows, part_width).astype(jnp.bfloat16)
        branch_a = tensor_sums(jnp.dot(mixed, w_output, preferred_element_type=jnp.float32))
        middle = rows + branch_a + output_bias
        normed_f, scaled_f, inverse_f = general_norm(middle, ffn_gain, ffn_shift)
        normed_f_all = tensor_rows(normed_f.astype(jnp.bfloat16))
        inner = jnp.dot(normed_f_all, w_inner, preferred_element_type=jnp.float32) + inner_piece
        active = general_gate(inner).astype(jnp.bfloat16)
        branch_f = tensor_sums(jnp.dot(active, w_outer, preferred_element_type=jnp.float32))
        result_rows = middle + branch_f + outer_bias
        grad_up = tensor_rows(cot_rows.astype(jnp.bfloat16))
        grad_outer_w = jnp.einsum("tf,td->fd", active, grad_up, preferred_element_type=jnp.float32)
        grad_active = jnp.einsum("td,fd->tf", grad_up, w_outer, preferred_element_type=jnp.float32)
        grad_inner = (grad_active * general_slope(inner)).astype(jnp.bfloat16)
        grad_inner_w = jnp.einsum(
            "td,tf->df", normed_f_all, grad_inner, preferred_element_type=jnp.float32
        )
        grad_inner_b = jnp.sum(grad_inner.astype(jnp.float32), axis=0)
        grad_normed_f = tensor_sums(
            jnp.einsum("tf,df->td", grad_inner, w_inner, preferred_element_type=jnp.float32)
        )
        grad_rows_f, grad_ffn_g, grad_ffn_s = general_norm_backward(
            grad_normed_f, scaled_f, inverse_f, ffn_gain
        )
        grad_middle = cot_rows + grad_rows_f
        grad_branch = tensor_rows(grad_middle.astype(jnp.bfloat16))
        grad_output_w = jnp.einsum(
            "tc,td->cd", mixed, grad_branch, preferred_element_type=jnp.float32
        )
        grad_mixed = jnp.einsum(
            "td,cd->tc", grad_branch, w_output, preferred_element_type=jnp.float32
        )
        grad_mixed = grad_mixed.astype(jnp.bfloat16).reshape(half_rows, heads_here, HDIM)
        grad_probs = jnp.einsum(
            "qhd,khd->hqk", grad_mixed, value_all, preferred_element_type=jnp.float32
        )
        grad_value_part = jnp.einsum(
            "hqk,qhd->khd", probs, grad_mixed, preferred_element_type=jnp.float32
        )
        again = jnp.exp(masked_scores(queries, key_all, allowed) - log_total)
        centre = jnp.sum(again * grad_probs, axis=-1, keepdims=True)
        grad_scores = (again * (grad_probs - centre)).astype(jnp.bfloat16)
        grad_queries = (
            jnp.einsum("hqk,khd->qhd", grad_scores, key_all, preferred_element_type=jnp.float32)
            * factor
        )
        grad_queries = grad_queries.reshape(half_rows, part_width).astype(jnp.bfloat16)
        grad_key_part = (
            jnp.einsum("hqk,qhd->khd", grad_scores, queries, preferred_element_type=jnp.float32)
            * factor
        )
        grad_key_sum, grad_value_sum = (
            lax.psum_scatter(
                grad_key_part.reshape(seq_rows, part_width).astype(jnp.bfloat16),
                "ctx",
                scatter_dimension=0,
                tiled=True,
            ).astype(jnp.float32),
            lax.psum_scatter(
                grad_value_part.reshape(seq_rows, part_width).astype(jnp.bfloat16),
                "ctx",
                scatter_dimension=0,
                tiled=True,
            ).astype(jnp.float32),
        )
        grad_keys = grad_key_sum.astype(jnp.bfloat16)
        grad_values = grad_value_sum.astype(jnp.bfloat16)
        grad_query_w = jnp.einsum(
            "td,tc->dc", normed_all, grad_queries, preferred_element_type=jnp.float32
        )
        grad_key_w = jnp.einsum(
            "td,tc->dc", normed_all, grad_keys, preferred_element_type=jnp.float32
        )
        grad_value_w = jnp.einsum(
            "td,tc->dc", normed_all, grad_values, preferred_element_type=jnp.float32
        )
        grad_query_b = jnp.sum(grad_queries.astype(jnp.float32), axis=0)
        grad_value_b = jnp.sum(grad_values.astype(jnp.float32), axis=0)
        grad_normed_part = jnp.einsum(
            "tc,dc->td", grad_queries, w_query, preferred_element_type=jnp.float32
        )
        grad_normed_part = grad_normed_part + jnp.einsum(
            "tc,dc->td", grad_keys, w_key, preferred_element_type=jnp.float32
        )
        grad_normed_part = grad_normed_part + jnp.einsum(
            "tc,dc->td", grad_values, w_value, preferred_element_type=jnp.float32
        )
        grad_normed = tensor_sums(grad_normed_part)
        grad_rows_a, grad_attn_g, grad_attn_s = general_norm_backward(
            grad_normed, scaled_a, inverse_a, attn_gain
        )
        grad_rows = grad_middle + grad_rows_a
        big_sums, small_sums = carry
        big_sums = (
            big_sums[0] + grad_query_w,
            big_sums[1] + grad_key_w,
            big_sums[2] + grad_value_w,
            big_sums[3] + grad_inner_w,
            big_sums[4] + grad_output_w,
            big_sums[5] + grad_outer_w,
        )
        small_terms = (
            grad_attn_g,
            grad_attn_s,
            general_piece(grad_query_b, width, tensor_at * part_width),
            general_piece(grad_value_b, width, tensor_at * part_width),
            jnp.sum(grad_middle, axis=0),
            grad_ffn_g,
            grad_ffn_s,
            general_piece(grad_inner_b, unit_total, tensor_at * unit_width),
            jnp.sum(cot_rows, axis=0),
        )
        small_sums = tuple((old + new for old, new in zip(small_sums, small_terms)))
        return ((big_sums, small_sums), (result_rows, grad_rows))

    big_init = (
        jnp.zeros((width, part_width), jnp.float32),
        jnp.zeros((width, part_width), jnp.float32),
        jnp.zeros((width, part_width), jnp.float32),
        jnp.zeros((width, unit_width), jnp.float32),
        jnp.zeros((part_width, width), jnp.float32),
        jnp.zeros((unit_width, width), jnp.float32),
    )
    small_init = tuple((jnp.zeros((width,), jnp.float32) for index_small in range(7))) + (
        jnp.zeros((unit_total,), jnp.float32),
        jnp.zeros((width,), jnp.float32),
    )
    small_init = (
        small_init[0],
        small_init[1],
        small_init[2],
        small_init[3],
        small_init[4],
        small_init[5],
        small_init[6],
        small_init[7],
        small_init[8],
    )
    gathered = fetch_weights(shards)

    def scan_step(carry, item):
        return micro(gathered, carry, item)

    (big_sums, small_sums), (block_out, grad_input) = lax.scan(
        scan_step, (big_init, small_init), (hidden_in, cotangent, segment_ids)
    )
    paired = (
        lax.psum(big_sums[0].astype(jnp.bfloat16), "ctx").astype(jnp.float32),
        lax.psum(big_sums[1].astype(jnp.bfloat16), "ctx").astype(jnp.float32),
        lax.psum(big_sums[2].astype(jnp.bfloat16), "ctx").astype(jnp.float32),
        lax.psum(big_sums[3].astype(jnp.bfloat16), "ctx").astype(jnp.float32),
        lax.psum(big_sums[4].astype(jnp.bfloat16), "ctx").astype(jnp.float32),
        lax.psum(big_sums[5].astype(jnp.bfloat16), "ctx").astype(jnp.float32),
    )
    owned = (
        lax.psum_scatter(
            paired[0].astype(jnp.bfloat16), "dp", scatter_dimension=0, tiled=True
        ).astype(jnp.float32),
        lax.psum_scatter(
            paired[1].astype(jnp.bfloat16), "dp", scatter_dimension=0, tiled=True
        ).astype(jnp.float32),
        lax.psum_scatter(
            paired[2].astype(jnp.bfloat16), "dp", scatter_dimension=0, tiled=True
        ).astype(jnp.float32),
        lax.psum_scatter(
            paired[3].astype(jnp.bfloat16), "dp", scatter_dimension=0, tiled=True
        ).astype(jnp.float32),
        lax.psum_scatter(
            paired[4].astype(jnp.bfloat16), "dp", scatter_dimension=1, tiled=True
        ).astype(jnp.float32),
        lax.psum_scatter(
            paired[5].astype(jnp.bfloat16), "dp", scatter_dimension=1, tiled=True
        ).astype(jnp.float32),
    )
    small = lax.psum(
        (
            small_sums[0],
            small_sums[1],
            small_sums[2],
            small_sums[3],
            small_sums[4],
            small_sums[5],
            small_sums[6],
            small_sums[7],
            small_sums[8],
        ),
        ("dp", "ctx", "tensor"),
    )
    return (
        block_out,
        grad_input,
        small[0],
        small[1],
        owned[0],
        owned[1],
        owned[2],
        small[2],
        small[3],
        owned[4],
        small[4],
        small[5],
        small[6],
        owned[3],
        small[7],
        owned[5],
        small[8],
    )


SPECS = (
    P("dp", ("ctx", "tensor"), None), P("dp", ("ctx", "tensor"), None), P("dp", None), P(), P(),
    P("dp", "tensor"), P("dp", "tensor"), P("dp", "tensor"), P(), P(), P("tensor", "dp"), P(), P(),
    P(), P("dp", "tensor"), P(), P("tensor", "dp"), P(),
)
OUT_SPECS = (
    P("dp", ("ctx", "tensor"), None), P("dp", ("ctx", "tensor"), None), P(), P(),
    P("dp", "tensor"), P("dp", "tensor"), P("dp", "tensor"), P(), P(), P("tensor", "dp"), P(), P(),
    P(), P("dp", "tensor"), P(), P("tensor", "dp"), P(),
)


def solution(mesh):
    lined_up = mesh.shape["dp"] == 4 and mesh.shape["tensor"] == 4 and mesh.shape["ctx"] == 2
    return jax.shard_map(
        body if lined_up else general_body, mesh=mesh, in_specs=SPECS, out_specs=OUT_SPECS, check_vma=False
    )
```

```python
import functools

import jax
import jax.numpy as jnp
from jax import lax
from jax.experimental import pallas as pl
from jax.experimental.pallas import tpu as pltpu
from jax.sharding import PartitionSpec as P

HDIM = 64
LANES = 256
ROOT_HALF = 0.7071067811865476
INV_ROOT_TWO_PI = 0.3989422804014327
MESH = pl.DeviceIdType.MESH
BF = jnp.bfloat16
F32 = jnp.float32
HIDE = -1e30


def dims(left, right, a, b):
    return lax.dot_general(left, right, (((a,), (b,)), ((), ())), preferred_element_type=F32)


def norm_parts(rows):
    centred = rows - jnp.mean(rows, axis=-1, keepdims=True)
    inverse = lax.rsqrt(jnp.mean(centred * centred, axis=-1, keepdims=True) + 1e-05)
    return centred * inverse, inverse


class Place:
    def __init__(self):
        self.d = lax.axis_index("dp")
        self.c = lax.axis_index("ctx")
        self.t = lax.axis_index("tensor")
        col, row = self.d % 2, self.d // 2
        self.dx = row * 2 + (1 - col)
        self.dy = (1 - row) * 2 + col
        self.dd = (1 - row) * 2 + (1 - col)
        self.h = self.t // 2
        self.g = self.t % 2
        self.mid = self.g + self.h * (1 - 2 * self.g)
        self.mate = 2 * self.h + 1 - self.g
        self.twin = (self.t + 2) % 4
        self.far_mid = 2 - self.h
        self.far_end = 3 * (1 - self.h)

    def source(self, k):
        first = 1 - jnp.minimum(k, 1)
        second = jnp.minimum(k, 1) * (1 - jnp.minimum(jnp.maximum(k - 1, 0), 1))
        third = jnp.minimum(jnp.maximum(k - 1, 0), 1) * (1 - jnp.maximum(k - 2, 0))
        fourth = jnp.maximum(k - 2, 0)
        return first * self.t + second * self.mate + third * self.far_mid + fourth * self.far_end


def remote(src, dst, send, recv, **where):
    return pltpu.make_async_remote_copy(
        src_ref=src, dst_ref=dst, send_sem=send, recv_sem=recv, device_id=where, device_id_type=MESH
    )


def greet(place):
    barrier = pltpu.get_barrier_semaphore()
    for k in range(1, 4):
        pl.semaphore_signal(
            barrier, inc=1, device_id={"tensor": (place.t + k) % 4}, device_id_type=MESH
        )
    for peer in (place.dx, place.dy, place.dd):
        pl.semaphore_signal(barrier, inc=1, device_id={"dp": peer}, device_id_type=MESH)
    pl.semaphore_signal(barrier, inc=1, device_id={"ctx": 1 - place.c}, device_id_type=MESH)
    for k in range(1, 4):
        where = {"ctx": 1 - place.c, "tensor": (place.t + k) % 4}
        pl.semaphore_signal(barrier, inc=1, device_id=where, device_id_type=MESH)
    return lambda: pl.semaphore_wait(barrier, 10)


class Several:
    def __init__(self, *copies):
        self.copies = copies

    def start(self):
        for copy in self.copies:
            copy.start()

    def wait_send(self):
        for copy in self.copies:
            copy.wait_send()

    def wait_recv(self):
        for copy in self.copies:
            copy.wait_recv()


def rows_at(start, size, step):
    return pl.ds(pl.multiple_of(start, step), size)


def erf_parts(values):
    cdf = 0.5 * (1.0 + lax.erf(values * ROOT_HALF))
    return cdf, cdf + values * (jnp.exp(-0.5 * values * values) * INV_ROOT_TWO_PI)


def add_to(target, *terms):
    total = target[...].astype(F32)
    for term in terms:
        total = total + term[...].astype(F32)
    target[...] = total.astype(BF)


def layer_kernel(
    hidden, cot, seg, gain_a, shift_a, wq_s, wk_s, wv_s, bias_q, bias_v, wo_s, bias_o, gain_f, shift_f,
    win_s, bias_in, wout_s, bias_out,
    block_out, grad_input, g_gain_a, g_shift_a, g_wq, g_wk, g_wv, g_bias_q, g_bias_v, g_wo, g_bias_o,
    g_gain_f, g_shift_f, g_win, g_bias_in, g_wout, g_bias_out,
    normed, far_rows, normed_turn, queries, kv, mixed_in, mixed_sib, q_land, wqkv, wo_land, wout, ffw,
    turn, q_turn, mixed, g_mix, keys_seg, left, left_in, left_turn, right, right_in, nf_out, nf_in,
    bf_out, bf_in, branch, branch_turn, part_wo, rxw, sumw, rzw, rx1, rx2, rz, wide, kv_out, kv_in, dqkv,
    gna, rzn, qkv_own, qkv_sib, qkv_in, qkv_sum, qkv_twin, sums, sums_core, sums_plane, sums_line,
    late, late_line, late_plane, res_ff, res_wo, res_qkv, bias_row, inner_rows,
    qt_send, q_send, q_recv, qc_send, qc_recv, z_send, z_recv, kvf_send, kvf_recv, mf_send, mf_recv,
    ct_send, cp_send, c_recv, cc_send, s_recv, wz_send, wz_recv, wp_send, wp_recv, wc_send, wc_recv,
    u_send, u_recv, l_send, l_recv, r_send, r_recv, n_send, n_recv, b_send, b_recv, x_send, x_recv,
    m_send, m_recv, p1_send, p1_recv, p2_send, p2_recv, zz_send, zz_recv, gp_send, gp_recv, gz_send, gz_recv,
    kv_send, kv_recv, rn_send, rn_recv, qs_send, qs_recv, qp_send, qp_recv, qz_send, qz_recv,
    f_send, f_recv, t_send, t_recv, ta_send, ta_recv, tb_send, tb_recv,
):
    at = Place()
    d, c, t, h, g = at.d, at.c, at.t, at.h, at.g
    other, away = 1 - c, 1 - h
    planes = (at.dx, at.dy, at.dd)
    others = [(t + k + 1) % 4 for k in range(3)]
    waits = []

    def begin(*copies):
        for copy in copies:
            copy.start()
            waits.append(copy)

    arrive = greet(at)

    for ref, start in ((wq_s, 0), (wk_s, LANES), (wv_s, 2 * LANES)):
        q_land[h, d, :, start + 128 : start + 256] = jnp.zeros((192, 128), BF)
        q_land[h, d, :, start : start + 192] = ref[...].astype(BF)
    arrive()

    def q_half(a, owner, which):
        return q_land.at[a, owner, rows_at(which * 96, 96, 96)]

    def q_piece(a, owner, n):
        if n is None:
            return q_half(a, owner, c), 0
        return q_land.at[a, owner, rows_at(c * 96 + n * 48, 48, 48)], n

    def q_plane(a, i, owner, n=None):
        block, n = q_piece(a, owner, n)
        return remote(block, block, q_send.at[a, i, n], q_recv.at[a, owner, n], dp=planes[i])

    def q_twin(n):
        block, n = q_piece(h, d, n)
        return remote(block, block, qt_send.at[n], q_recv.at[h, d, n], tensor=at.twin)

    def q_core(a, owner):
        half = q_half(a, owner, c)
        return remote(half, half, qc_send.at[a, owner], qc_recv.at[a, owner], ctx=other)

    def q_core_wait(a, owner):
        half = q_half(a, owner, other)
        remote(half, half, qc_send.at[a, owner], qc_recv.at[a, owner], ctx=other).wait_recv()

    def q_wait(a, owner, n=None):
        block, n = q_piece(a, owner, n)
        remote(block, block, qt_send.at[0], q_recv.at[a, owner, n], tensor=t).wait_recv()

    begin(q_twin(0), q_twin(1))
    for i in range(3):
        begin(q_plane(h, i, d))

    turned = wo_s[...].T
    turned = jnp.where(c == 0, turned[:96], turned[96:]).astype(BF)
    mine = rows_at(d * 192 + c * 96, 96, 96)
    wo_land[t, mine, 128:256] = jnp.zeros((96, 128), BF)
    wo_land[t, mine, 0:192] = turned

    def wo_rows(owner, which):
        return wo_land.at[:, rows_at(owner * 192 + which * 96, 96, 96)]

    def wo_line(k, owner):
        block = wo_land.at[owner, mine]
        return remote(block, block, wz_send.at[k], wz_recv.at[owner], tensor=others[k])

    def normed_rows(s):
        scaled, _ = norm_parts(hidden[s])
        return (scaled * gain_a[...].reshape(1, 768) + shift_a[...].reshape(1, 768)).astype(BF)

    def row_copy(src, owner, k, dest):
        return remote(src, normed.at[owner], z_send.at[k], z_recv.at[owner], tensor=dest)

    def row_wait(p):
        row_copy(normed.at[p], p, 0, t).wait_recv()

    pass_end = row_copy(normed.at[at.far_end], at.far_end, 2, at.mate)
    pass_mid = row_copy(normed.at[at.far_mid], at.far_mid, 3, at.mate)
    far_rows[...] = normed_rows(away)
    begin(row_copy(far_rows, t, 1, at.far_mid))
    normed[t] = normed_rows(h)
    begin(row_copy(normed.at[t], t, 0, at.mate))

    here = rows_at(d * 192, 192, 192)

    @pl.when(c == 0)
    def _():
        ffw[0, h, here, :] = win_s[...].astype(BF)

    @pl.when(c == 1)
    def _():
        ffw[1, h, here, :] = wout_s[...].astype(BF)

    def ff_block(which, a, owner):
        return ffw.at[which, a, rows_at(owner * 192, 192, 192)]

    def ff_half(which, a, owner, n):
        if n is None:
            return ff_block(which, a, owner)
        return ffw.at[which, a, rows_at(owner * 192 + n * 96, 96, 96)]

    def ff_twin(n):
        block = ff_half(c, h, d, n)
        return remote(block, block, ct_send.at[n], c_recv.at[h, d, n], tensor=at.twin)

    def ff_plane(axis, a, owner, n, dest):
        block = ff_half(c, a, owner, n)
        return remote(block, block, cp_send.at[axis, a, n or 0], c_recv.at[a, owner, n or 0], dp=dest)

    def ff_core(a, owner, n):
        block = ff_half(c, a, owner, n)
        return remote(block, block, cc_send.at[a, owner, n or 0], s_recv.at[a, owner, n or 0], ctx=other)

    def ff_wait(a, owner, n):
        block = ff_half(c, a, owner, n)
        remote(block, block, ct_send.at[n or 0], c_recv.at[a, owner, n or 0], dp=d).wait_recv()

    def ff_core_wait(a, owner, n):
        block = ff_half(other, a, owner, n)
        remote(block, block, cc_send.at[a, owner, n or 0], s_recv.at[a, owner, n or 0], ctx=other).wait_recv()

    ff_sends = []

    def ff_begin(*copies):
        for copy in copies:
            copy.start()
            ff_sends.append(copy)

    def spread(a, n):
        ff_begin(ff_plane(0, a, d, n, at.dx), ff_plane(1, a, d, n, at.dy), ff_core(a, d, n))

    def near_far(a):
        near = at.dx + a * (at.dy - at.dx)
        return near, at.dx + at.dy - near

    def diag(a, n):
        near, far = near_far(a)
        ff_wait(a, near, n)
        ff_begin(ff_plane(2, a, near, n, far), ff_core(a, near, n))
        ff_wait(a, far, n)
        ff_begin(ff_core(a, far, n))

    def last(a, n):
        ff_wait(a, at.dd, n)
        ff_begin(ff_core(a, at.dd, n))

    left[1, 0] = cot[...].reshape(256, 768).astype(BF)
    sums[...] = jnp.zeros_like(sums)
    late[...] = jnp.zeros_like(late)
    wide[...] = jnp.zeros_like(wide)
    part_wo[...] = jnp.zeros_like(part_wo)
    for p in range(2):

        @pl.when(g == p)
        def _(p=p):
            for a in range(2):
                cols = slice((p + 2 * a) * 192, (p + 2 * a) * 192 + 192)
                bias_row[:, a * 192 : a * 192 + 192] = bias_q[...].reshape(1, 768)[:, cols]
                bias_row[:, 768 + a * 192 : 960 + a * 192] = bias_v[...].reshape(1, 768)[:, cols]

    bias_row[:, 384:768] = jnp.zeros((1, 384), F32)
    for p in range(4):
        inner_rows[p] = bias_in[...].reshape(1, 3072)[:, p * 768 : (p + 1) * 768]

    row = jnp.where(h == 0, seg[0:1, :], seg[1:2, :])
    places = lax.broadcasted_iota(jnp.int32, (1, 1024), 1)
    row = jnp.where(row >= 0, row, -1 - places).astype(F32)
    seg_query = jnp.where(c == 0, row[:, :512], row[:, 512:])
    keys_seg[...] = jnp.broadcast_to(row, (128, 1024)).T

    for i in range(3):
        q_wait(h, planes[i])
        begin(q_core(h, planes[i]))
    for k in range(3):
        begin(wo_line(k, t))

    for n in range(2):
        q_wait(away, d, n)
        for i in range(3):
            begin(q_plane(away, i, d, n))
    begin(q_core(away, d))

    @pl.when(at.mid == 1)
    def _():
        row_wait(at.far_end)
        pass_end.start()
        row_wait(at.far_mid)
        pass_mid.start()

    for i in range(3):
        q_wait(away, planes[i], 0)
        q_wait(away, planes[i], 1)
        begin(q_core(away, planes[i]))
    for k in range(3):
        p = others[k]
        block = wo_land.at[p, mine]
        remote(block, block, wz_send.at[k], wz_recv.at[p], tensor=p).wait_recv()
    for i in range(3):
        begin(remote(wo_rows(d, c), wo_rows(d, c), wp_send.at[i], wp_recv.at[d], dp=planes[i]))
    begin(remote(wo_rows(d, c), wo_rows(d, c), wc_send.at[d], wc_recv.at[d], ctx=other))
    spread(h, None)
    for i in range(3):
        q_core_wait(h, planes[i])
        q_core_wait(away, planes[i])
    q_core_wait(away, d)

    def gather_columns(i, carry):
        rows = rows_at(i * 192, 192, 192)
        for k in range(3):
            pair = [q_land[a, i, :, k * LANES : k * LANES + 192] for a in range(2)]
            wqkv[rows, k * 384 : (k + 1) * 384] = jnp.concatenate(pair, axis=1)
        return carry

    lax.fori_loop(0, 4, gather_columns, 0)

    def kvf_copy(p):
        block = kv.at[:, c, p]
        return remote(block, block, kvf_send.at[p], kvf_recv.at[p], ctx=other)

    def project(k, carry):
        p = at.source(k)

        @pl.when((k == 1) | ((k > 1) & (at.mid == 0)))
        def _():
            row_wait(p)

        out = jnp.dot(normed[p], wqkv[...], preferred_element_type=F32)
        out = (out + bias_row[...]).astype(BF)
        for u in range(3):
            cols = out[:, u * 128 : (u + 1) * 128]
            queries[u, rows_at(p * 128, 128, 128), :] = cols * jnp.asarray(HDIM**-0.5, BF)
        for u in range(6):
            kv[u, c, p] = out[:, 384 + u * 128 : 512 + u * 128]
        kvf_copy(p).start()
        return carry

    ff_begin(ff_twin(0))
    begin(remote(left.at[1, 0], left.at[1, 1], u_send.at[1], u_recv.at[1], tensor=at.mate))
    lax.fori_loop(0, 4, project, 0)
    ff_begin(ff_twin(1))

    lane_head = lax.broadcasted_iota(jnp.int32, (1, 128), 1) // HDIM

    def head_pair(ref, u):
        return ref[u].reshape(1024, 128)

    def masked_scores(u, b, q_here):
        seg_here = jnp.where(b == 0, seg_query[:, :256], seg_query[:, 256:])
        scores = dims(head_pair(kv, u), q_here, 1, 1)
        column = keys_seg[...]
        visible = jnp.concatenate([column, column], axis=1) == seg_here
        return jnp.where(visible, scores, HIDE)

    def one_head(w, block):
        return jnp.where(lane_head == w, block.astype(F32), 0.0).astype(BF)

    def mf_copy(k, p):
        return remote(mixed.at[p], mixed_in.at[g, h], mf_send.at[k], mf_recv.at[t], tensor=p)

    for p in range(4):
        block = kv.at[:, other, p]
        remote(block, block, kvf_send.at[p], kvf_recv.at[p], ctx=other).wait_recv()
    for u in range(3):
        turn[u * 128 : (u + 1) * 128, :] = head_pair(kv, 3 + u).T

    def attend(b):
        block = rows_at(b * 256, 256, 256)

        def step(i, carry):
            u, w = i // 2, i % 2
            scores = masked_scores(u, b, one_head(w, queries[u, block, :]))
            peak = jnp.max(scores, axis=0, keepdims=True)
            expo = jnp.exp(scores - peak)
            total = jnp.sum(expo, axis=0, keepdims=True)
            rows = rows_at(i * HDIM, HDIM, HDIM)
            turned = jnp.dot(turn[rows, :], expo.astype(BF), preferred_element_type=F32)
            q_turn[rows, :] = turned / total
            return carry

        lax.fori_loop(0, 6, step, 0)
        mixed[pl.ds(2 * b, 2)] = q_turn[...].T.astype(BF).reshape(2, 128, 384)

    attend(away)
    mf_copy(0, 2 * away).start()
    mf_copy(1, 2 * away + 1).start()
    diag(h, None)
    attend(h)
    mf_copy(2, at.mate).start()
    mixed_in[g, h] = mixed[t]
    ff_wait(away, d, 0)
    spread(away, 0)
    last(h, None)
    for i in range(3):
        p = planes[i]
        remote(wo_rows(p, c), wo_rows(p, c), wp_send.at[i], wp_recv.at[p], dp=p).wait_recv()
        begin(remote(wo_rows(p, c), wo_rows(p, c), wc_send.at[p], wc_recv.at[p], ctx=other))
    normed_turn[...] = normed[...].reshape(512, 768).T
    for p in range(4):
        remote(wo_rows(p, other), wo_rows(p, other), wc_send.at[p], wc_recv.at[p], ctx=other).wait_recv()
    for p in range(2):
        for i in range(4):
            rows = slice(i * 192, (i + 1) * 192)
            pair = [wo_land[p + 2 * a, rows, :192] for a in range(2)]
            wout[p, rows, :] = jnp.concatenate(pair, axis=1)
    ff_wait(away, d, 1)
    spread(away, 1)
    diag(away, 0)

    for k in range(3):
        p = others[k]
        block = mixed_in.at[p % 2, p // 2]
        remote(block, block, mf_send.at[k], mf_recv.at[p], tensor=p).wait_recv()
    for s in range(2):
        total = hidden[s] + bias_o[...].reshape(1, 768)
        for p in range(2):
            total = total + dims(mixed_in[p, s], wout[p], 1, 1)
        block_out[s] = total
        scaled, _ = norm_parts(total)
        left[0, 0, s * 128 : (s + 1) * 128, :] = (
            scaled * gain_f[...].reshape(1, 768) + shift_f[...].reshape(1, 768)
        ).astype(BF)
    begin(remote(left.at[0, 0], left.at[0, 1], u_send.at[0], u_recv.at[0], tensor=at.mate))
    begin(remote(mixed_in, mixed_sib, x_send.at[0], x_recv.at[0], ctx=other))

    diag(away, 1)
    for p in range(4):
        ff_core_wait(h, p, None)

    def right_copy(a, r):
        return remote(
            right.at[other, a, r], right_in.at[a, r], r_send.at[a, r], r_recv.at[a, r], ctx=other
        )

    def units(a, r):
        unit = g + 2 * a
        top = pl.multiple_of(r * 512, 512)
        for j in range(3):
            cols = slice(j * 256, (j + 1) * 256)
            w_in, w_out = ffw[0, a, :, cols], ffw[1, a, :, cols]
            inner = jnp.dot(left[0, r], w_in, preferred_element_type=F32) + inner_rows[unit, :, cols]
            cdf, slope = erf_parts(inner)
            active = (inner * cdf).astype(BF)
            right[1, a, r, :, cols] = active
            grad_inner = jnp.dot(left[1, r], w_out, preferred_element_type=F32) * slope
            grad_inner = grad_inner.astype(BF)
            right[0, a, r, :, cols] = grad_inner
            sums[pl.ds(6 + unit, 1), cols] += jnp.sum(grad_inner.astype(F32), axis=0, keepdims=True)
            up, down = dims(active, w_out, 1, 1), dims(grad_inner, w_in, 1, 1)
            for k in range(6):
                wide[k, pl.ds(top, 256), :] += up[:, k * 128 : (k + 1) * 128]
                wide[k, pl.ds(top + 256, 256), :] += down[:, k * 128 : (k + 1) * 128]
        right_copy(a, r).start()

    def wide_rows(start, size=64):
        return jnp.concatenate([wide[k, start : start + size, :] for k in range(6)], axis=1)

    def own_slot(r, carry):
        @pl.when(r == 1)
        def _():
            for which in range(2):
                block = left.at[which, 1]
                remote(block, block, u_send.at[which], u_recv.at[which], tensor=at.mate).wait_recv()
            left_copy.start()

        units(h, r)
        return carry

    left_copy = remote(left.at[other], left_in, l_send.at[0], l_recv.at[0], ctx=other)
    waits.append(left_copy)
    lax.fori_loop(0, 2, own_slot, 0)
    for n in range(2):
        last(away, n)
    for p in range(4):
        for n in range(2):
            ff_core_wait(away, p, n)

    nf_copy = remote(nf_out, nf_in, n_send.at[0], n_recv.at[0], tensor=at.mate)
    waits.append(nf_copy)
    for copy in ff_sends:
        copy.wait_send()

    def turn_left():
        left_turn[0] = left[c, 0].T
        left_turn[1] = left[c, 1].T
        remote(left.at[c], left_in, l_send.at[0], l_recv.at[0], ctx=other).wait_recv()
        left_turn[2] = left_in[0].T
        left_turn[3] = left_in[1].T

    def first(a, j):
        near, _ = near_far(a)
        owner = near if j == 0 else at.dd
        return remote(ff_block(0, a, owner), rx1.at[a, j], p1_send.at[a, j], p1_recv.at[a, j], dp=near)

    def second(a):
        _, far = near_far(a)
        return remote(ff_block(0, a, far), rx2.at[a], p2_send.at[a], p2_recv.at[a], dp=far)

    def to_second(a):
        _, far = near_far(a)
        first(a, 1).wait_recv()
        add_to(ff_block(0, a, far), rx1.at[a, 1])
        second(a).start()
        first(a, 0).start()

    def plane_done(a):
        first(a, 0).wait_recv()
        second(a).wait_recv()
        add_to(ff_block(0, a, d), rx1.at[a, 0], rx2.at[a])

    def weight_gradient(a):
        for r in range(2):
            right_copy(a, r).wait_recv()

        def rows_of(q, carry):
            rows = rows_at(q * 192, 192, 192)
            out = jnp.dot(left_turn[0, rows, :], right[c, a, 0], preferred_element_type=F32)
            out = out + jnp.dot(left_turn[1, rows, :], right[c, a, 1], preferred_element_type=F32)
            out = out + jnp.dot(left_turn[2, rows, :], right_in[a, 0], preferred_element_type=F32)
            out = out + jnp.dot(left_turn[3, rows, :], right_in[a, 1], preferred_element_type=F32)
            ffw[0, a, rows, :] = out.astype(BF)
            return carry

        lax.fori_loop(0, 4, rows_of, 0)
        first(a, 1).start()

    def twin_slot(i, carry):
        @pl.when(i == 1)
        def _():
            for q in range(4):
                rows = slice(q * 64, (q + 1) * 64)
                nf_out[rows, :] = wide_rows(768 + q * 64).astype(BF)
            nf_copy.start()
            turn_left()
            weight_gradient(h)

        units(away, 1 - i)
        return carry

    lax.fori_loop(0, 2, twin_slot, 0)
    weight_gradient(away)
    for q in range(4):
        rows = slice(q * 64, (q + 1) * 64)
        bf_out[rows, :] = wide_rows(512 + q * 64).astype(BF)

    def add_row(i, value):
        sums[i : i + 1, :] += jnp.sum(value, axis=0, keepdims=True)

    def norm_back(source, grad_out, gain):
        scaled, inverse = norm_parts(source)
        grad_scaled = grad_out * gain[...].reshape(1, 768)
        plain = jnp.mean(grad_scaled, axis=-1, keepdims=True)
        cross = jnp.mean(grad_scaled * scaled, axis=-1, keepdims=True)
        return inverse * (grad_scaled - plain - scaled * cross), scaled

    nf_copy.wait_recv()
    to_second(h)
    for s in range(2):
        for half in range(2):
            rows = slice(half * 64, half * 64 + 64)
            start = s * 128 + half * 64
            cot_here = cot[s, rows, :]
            grad_out = wide_rows(256 + start) + nf_in[start : start + 64, :].astype(F32)
            middle = block_out[s, rows, :]
            grad_rows, scaled = norm_back(middle, grad_out, gain_f)
            block_out[s, rows, :] = middle + wide_rows(start) + bias_out[...].reshape(1, 768)
            grad_rows = grad_rows + cot_here
            grad_input[s, rows, :] = grad_rows
            branch[0, start : start + 64, :] = grad_rows.astype(BF)
            add_row(2, grad_out * scaled)
            add_row(3, grad_out)
            add_row(4, grad_rows)
            add_row(5, cot_here)
    begin(remote(branch.at[0], branch.at[1], b_send.at[0], b_recv.at[0], ctx=other))

    def m_copy(k):
        p = others[k]
        return remote(mixed.at[p], g_mix.at[t], m_send.at[k], m_recv.at[t], tensor=p)

    mf_copy(0, 2 * away).wait_send()
    mf_copy(1, 2 * away + 1).wait_send()
    mf_copy(2, at.mate).wait_send()
    for p in range(2):
        out = jnp.dot(branch[0], wout[p], preferred_element_type=F32).astype(BF)
        for s in range(2):
            mixed[2 * s + p] = out[s * 128 : (s + 1) * 128, :]
    for k in range(3):
        begin(m_copy(k))
    g_mix[t] = mixed[t]

    branch_turn[0] = branch[0].T
    remote(branch.at[0], branch.at[1], b_send.at[0], b_recv.at[0], ctx=other).wait_recv()
    branch_turn[1] = branch[1].T
    remote(mixed_in, mixed_sib, x_send.at[0], x_recv.at[0], ctx=other).wait_recv()
    for p in range(2):
        for q in range(4):
            rows = slice(q * 192, (q + 1) * 192)
            out = jnp.dot(branch_turn[0, rows, :], mixed_in[p].reshape(256, 384), preferred_element_type=F32)
            out = out + jnp.dot(
                branch_turn[1, rows, :], mixed_sib[p].reshape(256, 384), preferred_element_type=F32
            )
            for a in range(2):
                part_wo[p + 2 * a, rows, :192] = out[:, a * 192 : (a + 1) * 192].astype(BF)

    def wo_part(owner):
        return part_wo.at[:, rows_at(owner * 192 + c * 96, 96, 96)]

    to_second(away)
    for i in range(3):
        begin(remote(wo_part(planes[i]), rxw.at[d], gp_send.at[i], gp_recv.at[d], dp=planes[i]))

    zz_copy = remote(ff_block(0, away, d), rz, zz_send.at[0], zz_recv.at[0], tensor=at.twin)
    waits.append(zz_copy)

    for u in range(3):
        turn[u * 128 : (u + 1) * 128, :] = head_pair(kv, u).T
    wide[...] = jnp.zeros_like(wide)

    def m_wait(p):
        block = g_mix.at[p]
        remote(block, block, m_send.at[0], m_recv.at[p], tensor=p).wait_recv()

    theirs = rows_at(other * 512, 512, 512)
    ours = rows_at(c * 512, 512, 512)

    def kv_copy(u):
        return remote(kv_out.at[u], kv_in.at[u], kv_send.at[u], kv_recv.at[u], ctx=other)

    gz_copies = [
        remote(sumw.at[p], rzw.at[t], gz_send.at[k], gz_recv.at[t], tensor=p) for k, p in enumerate(others)
    ]
    waits.extend(gz_copies)

    def wo_plane_done():
        for i in range(3):
            p = planes[i]
            remote(wo_part(p), rxw.at[p], gp_send.at[i], gp_recv.at[p], dp=p).wait_recv()
        total = part_wo[:, mine, :].astype(F32)
        for i in range(3):
            total = total + rxw[planes[i]].astype(F32)
        sumw[...] = total.astype(BF)
        for copy in gz_copies:
            copy.start()

    def attend_back(b, last):
        block = rows_at(b * 256, 256, 256)

        def step(u, carry):
            cols = pl.ds(pl.multiple_of(u * 128, 128), 128)
            g_pair = g_mix[pl.ds(2 * b, 2), :, cols].reshape(256, 128)
            for w in range(2):
                q_here = one_head(w, queries[u, block, :])
                g_here = one_head(w, g_pair)
                scores = masked_scores(u, b, q_here)
                peak = jnp.max(scores, axis=0, keepdims=True)
                expo = jnp.exp(scores - peak)
                probs = expo * (1.0 / jnp.sum(expo, axis=0, keepdims=True))
                grad_probs = dims(head_pair(kv, 3 + u), g_here, 1, 1)
                centre = jnp.sum(probs * grad_probs, axis=0, keepdims=True)
                wide[3 + u] += jnp.dot(probs.astype(BF), g_here, preferred_element_type=F32)
                grad_scores = (probs * (grad_probs - centre)).astype(BF)
                wide[u] += jnp.dot(grad_scores, q_here, preferred_element_type=F32)
                rows = rows_at(u * 128 + w * HDIM, HDIM, HDIM)
                q_turn[rows, :] = jnp.dot(turn[rows, :], grad_scores, preferred_element_type=F32)
            if not last:

                @pl.when(u == 1)
                def _():
                    plane_done(away)
                    zz_copy.start()

            if last:
                @pl.when(u == 0)
                def _():
                    plane_done(h)

                @pl.when(u == 2)
                def _():
                    wo_plane_done()

                kv_out[u, :, :128] = wide[u, theirs, :].astype(BF)
                kv_out[u, :, 128:] = wide[3 + u, theirs, :].astype(BF)
                kv_copy(u).start()
            return carry

        lax.fori_loop(0, 3, step, 0)
        dqkv[block, :384] = (q_turn[...].T * HDIM**-0.5).astype(BF)

    m_wait(at.mate)
    begin(remote(bf_out, bf_in, n_send.at[1], n_recv.at[1], tensor=at.mate))
    attend_back(h, False)
    m_wait(at.far_mid)
    m_wait(at.far_end)
    attend_back(away, True)

    def part_cols(k):
        return pl.ds(0, 384) if k == 0 else pl.ds(384, 768)

    def sib_copy(k):
        block, landing = qkv_sib.at[0, :, :, part_cols(k)], qkv_sib.at[1, :, :, part_cols(k)]
        return remote(block, landing, qs_send.at[k], qs_recv.at[k], ctx=other)

    def qkv_part(k):
        def rows_of(i, carry):
            rows = rows_at(i * 192, 192, 192)
            out = jnp.dot(normed_turn[rows, :], dqkv[:, part_cols(k)], preferred_element_type=F32)
            qkv_own[i, :, part_cols(k)] = jnp.where(c == 0, out[:96], out[96:])
            qkv_sib[0, i, :, part_cols(k)] = jnp.where(c == 0, out[96:], out[:96]).astype(BF)
            return carry

        lax.fori_loop(0, 4, rows_of, 0)
        begin(sib_copy(k))

    def qkv_out(k):
        sib_copy(k).wait_recv()
        cols = part_cols(k)
        for p in range(4):
            qkv_in[0, p, :, cols] = (qkv_own[p, :, cols] + qkv_sib[1, p, :, cols].astype(F32)).astype(BF)
        for i in range(3):
            block, landing = qkv_in.at[0, planes[i], :, cols], qkv_in.at[1, d, :, cols]
            begin(remote(block, landing, qp_send.at[k, i], qp_recv.at[k, d], dp=planes[i]))
        qkv_in[1, d, :, cols] = qkv_in[0, d, :, cols]

    def twin_copy(k):
        cols = pl.ds(0, LANES) if k == 0 else pl.ds(LANES, 2 * LANES)
        block, landing = qkv_twin.at[0, :, cols], qkv_twin.at[1, :, cols]
        return remote(block, landing, qz_send.at[k], qz_recv.at[k], tensor=at.twin)

    def qkv_to_twin(k):
        for i in range(3):
            block = qkv_in.at[1, planes[i], :, part_cols(k)]
            remote(block, block, qp_send.at[k, i], qp_recv.at[k, planes[i]], dp=d).wait_recv()
        for j in ((0,), (1, 2))[k]:
            cols = slice(j * 384, (j + 1) * 384)
            total = qkv_in[1, 0, :, cols].astype(F32)
            for p in range(1, 4):
                total = total + qkv_in[1, p, :, cols].astype(F32)
            low, high = total[:, :192], total[:, 192:]
            qkv_sum[0, :, j * LANES : j * LANES + 192] = jnp.where(h == 0, low, high)
            qkv_twin[0, :, j * LANES : j * LANES + 192] = jnp.where(h == 0, high, low).astype(BF)
        begin(twin_copy(k))

    qkv_part(0)


    for u in range(3):
        kv_copy(u).wait_recv()
        for k in range(2):
            cols = slice(384 * (k + 1) + u * 128, 384 * (k + 1) + (u + 1) * 128)
            theirs_here = kv_in[u, :, k * 128 : (k + 1) * 128].astype(F32)
            dqkv[:, cols] = (wide[3 * k + u, ours, :] + theirs_here).astype(BF)

    qkv_out(0)

    def line_copy(owner, slot, k, dest):
        return remote(gna.at[owner], rzn.at[slot], rn_send.at[k], rn_recv.at[slot], tensor=dest)

    def line_wait(slot):
        line_copy(t, slot, 0, t).wait_recv()

    by_mate = [line_copy(at.far_end, 2, 1, at.mate), line_copy(at.far_mid, 3, 2, at.mate)]
    on_sums = [line_copy(at.far_end, 1, 1, at.far_end), line_copy(at.far_mid, 1, 2, at.far_mid)]

    def rows_back(p):
        rows = dqkv[rows_at(p * 128, 128, 128), :]
        gna[p] = dims(rows, wqkv[...], 1, 1).astype(BF)

    for i, p in enumerate((at.far_end, at.far_mid)):
        rows_back(p)

        @pl.when(at.mid == 0)
        def _(i=i):
            by_mate[i].start()

    rows_back(at.mate)
    begin(line_copy(at.mate, 0, 0, at.mate))
    rows_back(t)
    total = jnp.sum(dqkv[...].astype(F32), axis=0, keepdims=True)
    sums[pl.ds(10 + g, 1), :384] = total[:, :384]
    sums[pl.ds(10 + g, 1), 384:] = total[:, 768:]

    core_sum = remote(sums, sums_core, t_send.at[0], t_recv.at[0], ctx=other)
    begin(core_sum)

    def plane_sum(k, owner):
        block = sums_plane.at[owner]
        return remote(block, block, t_send.at[1 + k], t_recv.at[1 + owner], dp=planes[k])

    def line_sum(k, owner):
        block = sums_line.at[owner]
        return remote(block, block, t_send.at[4 + k], t_recv.at[5 + owner], tensor=others[k])

    qkv_part(1)
    @pl.when(at.mid == 1)
    def _():
        for i, p in enumerate((at.far_end, at.far_mid)):
            line_wait(2 + i)
            add_to(gna.at[p], rzn.at[2 + i])
            on_sums[i].start()

    core_sum.wait_recv()
    sums_plane[d] = sums[...] + sums_core[...]
    for k in range(3):
        begin(plane_sum(k, d))
    qkv_out(1)
    qkv_to_twin(0)

    def result_copy(i, ref):
        return remote(ref.at[c], ref.at[c], f_send.at[i], f_recv.at[i], ctx=other)

    remote(rz, rz, zz_send.at[0], zz_recv.at[0], tensor=t).wait_recv()
    res_ff[c] = ffw[0, h, here, :].astype(F32) + rz[...].astype(F32)
    begin(result_copy(1, res_ff))
    rzw[t] = sumw[t]
    for k in range(3):
        p = others[k]
        remote(rzw.at[p], rzw.at[p], gz_send.at[k], gz_recv.at[p], tensor=p).wait_recv()
    total = rzw[0].astype(F32)
    for p in range(1, 4):
        total = total + rzw[p].astype(F32)
    res_wo[c] = total
    begin(result_copy(2, res_wo))

    for k in range(3):
        plane_sum(k, planes[k]).wait_recv()
    sums_line[t] = (sums_plane[0] + sums_plane[1]) + (sums_plane[2] + sums_plane[3])
    for k in range(3):
        begin(line_sum(k, t))

    qkv_to_twin(1)

    for slot in range(2):
        line_wait(slot)

    for s in range(2):
        for half in range(2):
            rows = slice(half * 64, half * 64 + 64)
            near = gna[t, rows, :].astype(F32) + rzn[0, rows, :].astype(F32)
            grad_out = jnp.where(h == s, near, rzn[1, rows, :].astype(F32))
            grad_rows, scaled = norm_back(hidden[s, rows, :], grad_out, gain_a)
            grad_input[s, rows, :] += grad_rows
            late[0:1, :] += jnp.sum(grad_out * scaled, axis=0, keepdims=True)
            late[1:2, :] += jnp.sum(grad_out, axis=0, keepdims=True)

    late_line[c, t] = late[...]
    peers = [(c, p) for p in others] + [(other, p) for p in others] + [(other, t)]
    for k, (core, p) in enumerate(peers):
        block = late_line.at[c, t]
        begin(remote(block, block, ta_send.at[k], ta_recv.at[c, t], ctx=core, tensor=p))
    remote(bf_out, bf_in, n_send.at[1], n_recv.at[1], tensor=at.mate).wait_recv()
    for s in range(2):
        block_out[s] += bf_in[s * 128 : (s + 1) * 128, :].astype(F32)

    for k in range(2):
        twin_copy(k).wait_recv()
    res_qkv[c] = qkv_sum[0] + qkv_twin[1].astype(F32)
    begin(result_copy(0, res_qkv))
    for k, (core, p) in enumerate(peers):
        block = late_line.at[core, p]
        remote(block, block, ta_send.at[k], ta_recv.at[core, p], ctx=core, tensor=p).wait_recv()
    total = late_line[0, 0]
    for k in range(1, 8):
        total = total + late_line[k // 4, k % 4]
    late_plane[d] = total
    for k in range(3):
        block = late_plane.at[d]
        begin(remote(block, block, tb_send.at[k], tb_recv.at[d], dp=planes[k]))

    for i, ref in enumerate((res_qkv, res_ff, res_wo)):
        block = ref.at[other]
        remote(block, block, f_send.at[i], f_recv.at[i], ctx=other).wait_recv()
    for which in range(2):
        rows = slice(which * 96, (which + 1) * 96)
        for ref, start in ((g_wq, 0), (g_wk, LANES), (g_wv, 2 * LANES)):
            ref[rows, :] = res_qkv[which, :, start : start + 192]
    g_win[...] = res_ff[0]
    g_wout[...] = res_ff[1]
    g_wo[...] = res_wo[...].reshape(192, LANES).T[:192, :]

    for k in range(3):
        line_sum(k, others[k]).wait_recv()
    total = (sums_line[0] + sums_line[1]) + (sums_line[2] + sums_line[3])
    for i, ref in enumerate((g_gain_f, g_shift_f, g_bias_o, g_bias_out)):
        ref[...] = total[2 + i]
    g_bias_in[...] = jnp.concatenate([total[6 + i : 7 + i, :] for i in range(4)], axis=1).reshape(3072)
    for ref, start in ((g_bias_q, 0), (g_bias_v, 384)):
        pieces = []
        for p in range(4):
            first_lane = start + (p // 2) * 192
            pieces.append(total[10 + p % 2 : 11 + p % 2, first_lane : first_lane + 192])
        ref[...] = jnp.concatenate(pieces, axis=1).reshape(768)
    for k in range(3):
        block = late_plane.at[planes[k]]
        remote(block, block, tb_send.at[k], tb_recv.at[planes[k]], dp=d).wait_recv()
    total = (late_plane[0] + late_plane[1]) + (late_plane[2] + late_plane[3])
    g_gain_a[...] = total[0]
    g_shift_a[...] = total[1]

    for copy in waits:
        copy.wait_send()
    for p in range(4):
        kvf_copy(p).wait_send()
    for u in range(3):
        kv_copy(u).wait_send()
    for a in range(2):
        first(a, 0).wait_send()
        first(a, 1).wait_send()
        second(a).wait_send()
        for r in range(2):
            right_copy(a, r).wait_send()

    @pl.when(at.mid == 1)
    def _():
        pass_end.wait_send()
        pass_mid.wait_send()
        for copy in on_sums:
            copy.wait_send()

    @pl.when(at.mid == 0)
    def _():
        for copy in by_mate:
            copy.wait_send()


def deliver_kernel(*refs):
    count = (len(refs) - 2) // 3
    made, outs, held = refs[:count], refs[count : 2 * count], refs[2 * count : 3 * count]
    fetches = [pltpu.make_async_copy(made[i], held[i], refs[-2].at[i]) for i in range(count)]
    puts = [pltpu.make_async_copy(held[i], outs[i], refs[-1].at[i]) for i in range(count)]
    for fetch in fetches:
        fetch.start()
    for fetch, put in zip(fetches, puts):
        fetch.wait()
        put.start()
    for put in puts:
        put.wait()


VM = pl.BlockSpec(memory_space=pltpu.VMEM)
ANY = pl.BlockSpec(memory_space=pl.ANY)


def body(*operands):
    struct = jax.ShapeDtypeStruct
    dma = pltpu.SemaphoreType.DMA
    vm = pltpu.VMEM
    operands = operands[:16] + (operands[16].T, operands[17])
    hidden, cotangent, _, gain, _, wq, wk, wv, bq, bv, wo, bo, gf, sf, win, bin_, wout, bout = operands
    results = (hidden, hidden, gain, gain, wq, wk, wv, bq, bv, wo, bo, gf, sf, win, bin_, wout, bout)
    shapes = tuple(struct(r.shape, F32) for r in results)
    made = pl.pallas_call(
        layer_kernel,
        out_shape=shapes,
        in_specs=[VM] * len(operands),
        out_specs=(VM,) * len(results),
        scratch_shapes=[
            vm((4, 128, 768), BF),
            vm((128, 768), BF),
            vm((768, 512), BF),
            vm((3, 512, 128), BF),
            vm((6, 2, 4, 128, 128), BF),
            vm((2, 2, 128, 384), BF),
            vm((2, 2, 128, 384), BF),
            vm((2, 4, 192, 768), BF),
            vm((768, 1152), BF),
            vm((4, 768, LANES), BF),
            vm((2, 768, 384), BF),
            vm((2, 2, 768, 768), BF),
            vm((384, 1024), BF),
            vm((384, 256), F32),
            vm((4, 128, 384), BF),
            vm((4, 128, 384), BF),
            vm((1024, 128), F32),
            vm((2, 2, 256, 768), BF),
            vm((2, 256, 768), BF),
            vm((4, 768, 256), BF),
            vm((2, 2, 2, 256, 768), BF),
            vm((2, 2, 256, 768), BF),
            vm((256, 768), BF),
            vm((256, 768), BF),
            vm((256, 768), BF),
            vm((256, 768), BF),
            vm((2, 256, 768), BF),
            vm((2, 768, 256), BF),
            vm((4, 768, LANES), BF),
            vm((4, 4, 96, LANES), BF),
            vm((4, 96, LANES), BF),
            vm((4, 96, LANES), BF),
            vm((2, 2, 192, 768), BF),
            vm((2, 192, 768), BF),
            vm((192, 768), BF),
            vm((6, 1024, 128), F32),
            vm((3, 512, 256), BF),
            vm((3, 512, 256), BF),
            vm((512, 1152), BF),
            vm((4, 128, 768), BF),
            vm((4, 128, 768), BF),
            vm((4, 96, 1152), F32),
            vm((2, 4, 96, 1152), BF),
            vm((2, 4, 96, 1152), BF),
            vm((1, 96, 768), F32),
            vm((2, 96, 768), BF),
            vm((16, 768), F32),
            vm((16, 768), F32),
            vm((4, 16, 768), F32),
            vm((4, 16, 768), F32),
            vm((2, 768), F32),
            vm((2, 4, 2, 768), F32),
            vm((4, 2, 768), F32),
            vm((2, 192, 768), F32),
            vm((2, 96, LANES), F32),
            vm((2, 96, 768), F32),
            vm((1, 1152), F32),
            vm((4, 1, 768), F32),
            dma((2,)), dma((2, 3, 2)), dma((2, 4, 2)), dma((2, 4)), dma((2, 4)),
            dma((4,)), dma((4,)), dma((4,)), dma((4,)), dma((3,)), dma((4,)),
            dma((2,)), dma((3, 2, 2)), dma((2, 4, 2)), dma((2, 4, 2)), dma((2, 4, 2)),
            dma((3,)), dma((4,)), dma((3,)), dma((4,)), dma((4,)), dma((4,)),
            dma((2,)), dma((2,)), dma((1,)), dma((1,)), dma((2, 2)), dma((2, 2)),
            dma((2,)), dma((2,)), dma((1,)), dma((1,)), dma((1,)), dma((1,)),
            dma((3,)), dma((4,)),
            dma((2, 2)), dma((2, 2)), dma((2,)), dma((2,)), dma((1,)), dma((1,)),
            dma((3,)), dma((4,)), dma((3,)), dma((4,)),
            dma((3,)), dma((3,)), dma((3,)), dma((4,)),
            dma((2,)), dma((2,)), dma((2, 3)), dma((2, 4)), dma((2,)), dma((2,)),
            dma((3,)), dma((3,)), dma((7,)), dma((9,)),
            dma((7,)), dma((2, 4)), dma((3,)), dma((4,)),
        ],
        compiler_params=pltpu.CompilerParams(
            collective_id=1, has_side_effects=True, vmem_limit_bytes=63 << 20
        ),
        name="layer",
    )(*operands)
    made = pl.pallas_call(
        deliver_kernel,
        out_shape=shapes,
        in_specs=[ANY] * len(shapes),
        out_specs=(ANY,) * len(shapes),
        scratch_shapes=[vm(r.shape, F32) for r in shapes] + [dma((len(shapes),))] * 2,
        name="deliver",
    )(*made)
    return tuple(made[:15]) + (made[15].T, made[16])


root_half = 0.7071067811865476
inv_root_two_pi = 0.3989422804014327


def general_gate(values):
    return values * (0.5 * (1.0 + lax.erf(values * root_half)))


def general_slope(values):
    normal_cdf = 0.5 * (1.0 + lax.erf(values * root_half))
    normal_pdf = jnp.exp(-0.5 * values * values) * inv_root_two_pi
    return normal_cdf + values * normal_pdf


def general_norm(rows, gain, shift):
    centred = rows - jnp.mean(rows, axis=-1, keepdims=True)
    inverse = lax.rsqrt(jnp.mean(centred * centred, axis=-1, keepdims=True) + 1e-05)
    scaled = centred * inverse
    return (scaled * gain + shift, scaled, inverse)


def general_norm_backward(grad_out, scaled, inverse, gain):
    grad_scaled = grad_out * gain
    plain_mean = jnp.mean(grad_scaled, axis=-1, keepdims=True)
    cross_mean = jnp.mean(grad_scaled * scaled, axis=-1, keepdims=True)
    grad_rows = inverse * (grad_scaled - plain_mean - scaled * cross_mean)
    return (grad_rows, jnp.sum(grad_out * scaled, axis=0), jnp.sum(grad_out, axis=0))


def tensor_rows(block):
    return lax.all_gather(block, "tensor", axis=0, tiled=True)


def tensor_sums(block):
    return lax.psum_scatter(block, "tensor", scatter_dimension=0, tiled=True)


def fetch_weights(shards):
    return (
        lax.all_gather(shards[0], "dp", axis=0, tiled=True),
        lax.all_gather(shards[1], "dp", axis=0, tiled=True),
        lax.all_gather(shards[2], "dp", axis=0, tiled=True),
        lax.all_gather(shards[3], "dp", axis=0, tiled=True),
        lax.all_gather(shards[4], "dp", axis=1, tiled=True),
        lax.all_gather(shards[5], "dp", axis=1, tiled=True),
    )


def general_piece(piece, total, start):
    return lax.dynamic_update_slice(jnp.zeros((total,), jnp.float32), piece, (start,))


def general_body(
    hidden_in,
    cotangent,
    segment_ids,
    attn_gain,
    attn_shift,
    query_weight,
    key_weight,
    value_weight,
    query_bias,
    value_bias,
    output_weight,
    output_bias,
    ffn_gain,
    ffn_shift,
    inner_weight,
    inner_bias,
    outer_weight,
    outer_bias,
):
    width = hidden_in.shape[2]
    part_width = query_weight.shape[1]
    unit_width = inner_weight.shape[1]
    unit_total = inner_bias.shape[0]
    heads_here = part_width // HDIM
    tensor_at = lax.axis_index("tensor")
    ctx_at = lax.axis_index("ctx")
    half_rows = hidden_in.shape[1] * lax.axis_size("tensor")
    seq_rows = segment_ids.shape[1]
    factor = HDIM ** (-0.5)
    query_piece = lax.dynamic_slice_in_dim(query_bias, tensor_at * part_width, part_width)
    value_piece = lax.dynamic_slice_in_dim(value_bias, tensor_at * part_width, part_width)
    inner_piece = lax.dynamic_slice_in_dim(inner_bias, tensor_at * unit_width, unit_width)
    shards = (
        query_weight.astype(jnp.bfloat16),
        key_weight.astype(jnp.bfloat16),
        value_weight.astype(jnp.bfloat16),
        inner_weight.astype(jnp.bfloat16),
        output_weight.astype(jnp.bfloat16),
        outer_weight.astype(jnp.bfloat16),
    )
    key_index = jnp.arange(seq_rows)
    query_index = ctx_at * half_rows + jnp.arange(half_rows)

    def masked_scores(queries, key_all, allowed):
        scores = (
            jnp.einsum("qhd,khd->hqk", queries, key_all, preferred_element_type=jnp.float32)
            * factor
        )
        return jnp.where(allowed[None, :, :], scores, -1e30)

    def micro(weights_bf, carry, item):
        w_query, w_key, w_value, w_inner, w_output, w_outer = weights_bf
        rows, cot_rows, segment_row = item
        query_seg = lax.dynamic_slice_in_dim(segment_row, ctx_at * half_rows, half_rows)
        allowed = (query_seg[:, None] == segment_row[None, :]) & (
            (segment_row[None, :] >= 0) | (query_index[:, None] == key_index[None, :])
        )
        normed, scaled_a, inverse_a = general_norm(rows, attn_gain, attn_shift)
        normed_all = tensor_rows(normed.astype(jnp.bfloat16))
        queries = (
            jnp.dot(normed_all, w_query, preferred_element_type=jnp.float32) + query_piece
        ).astype(jnp.bfloat16)
        key_half = jnp.dot(normed_all, w_key, preferred_element_type=jnp.float32).astype(
            jnp.bfloat16
        )
        value_half = (
            jnp.dot(normed_all, w_value, preferred_element_type=jnp.float32) + value_piece
        ).astype(jnp.bfloat16)
        key_all, value_all = (
            lax.all_gather(key_half, "ctx", axis=0, tiled=True),
            lax.all_gather(value_half, "ctx", axis=0, tiled=True),
        )
        queries = queries.reshape(half_rows, heads_here, HDIM)
        key_all = key_all.reshape(seq_rows, heads_here, HDIM)
        value_all = value_all.reshape(seq_rows, heads_here, HDIM)
        masked = masked_scores(queries, key_all, allowed)
        peak = jnp.max(masked, axis=-1, keepdims=True)
        expo = jnp.exp(masked - peak)
        total = jnp.sum(expo, axis=-1, keepdims=True)
        log_total = peak + jnp.log(total)
        probs = (expo / total).astype(jnp.bfloat16)
        mixed = jnp.einsum("hqk,khd->qhd", probs, value_all, preferred_element_type=jnp.float32)
        mixed = mixed.reshape(half_rows, part_width).astype(jnp.bfloat16)
        branch_a = tensor_sums(jnp.dot(mixed, w_output, preferred_element_type=jnp.float32))
        middle = rows + branch_a + output_bias
        normed_f, scaled_f, inverse_f = general_norm(middle, ffn_gain, ffn_shift)
        normed_f_all = tensor_rows(normed_f.astype(jnp.bfloat16))
        inner = jnp.dot(normed_f_all, w_inner, preferred_element_type=jnp.float32) + inner_piece
        active = general_gate(inner).astype(jnp.bfloat16)
        branch_f = tensor_sums(jnp.dot(active, w_outer, preferred_element_type=jnp.float32))
        result_rows = middle + branch_f + outer_bias
        grad_up = tensor_rows(cot_rows.astype(jnp.bfloat16))
        grad_outer_w = jnp.einsum("tf,td->fd", active, grad_up, preferred_element_type=jnp.float32)
        grad_active = jnp.einsum("td,fd->tf", grad_up, w_outer, preferred_element_type=jnp.float32)
        grad_inner = (grad_active * general_slope(inner)).astype(jnp.bfloat16)
        grad_inner_w = jnp.einsum(
            "td,tf->df", normed_f_all, grad_inner, preferred_element_type=jnp.float32
        )
        grad_inner_b = jnp.sum(grad_inner.astype(jnp.float32), axis=0)
        grad_normed_f = tensor_sums(
            jnp.einsum("tf,df->td", grad_inner, w_inner, preferred_element_type=jnp.float32)
        )
        grad_rows_f, grad_ffn_g, grad_ffn_s = general_norm_backward(
            grad_normed_f, scaled_f, inverse_f, ffn_gain
        )
        grad_middle = cot_rows + grad_rows_f
        grad_branch = tensor_rows(grad_middle.astype(jnp.bfloat16))
        grad_output_w = jnp.einsum(
            "tc,td->cd", mixed, grad_branch, preferred_element_type=jnp.float32
        )
        grad_mixed = jnp.einsum(
            "td,cd->tc", grad_branch, w_output, preferred_element_type=jnp.float32
        )
        grad_mixed = grad_mixed.astype(jnp.bfloat16).reshape(half_rows, heads_here, HDIM)
        grad_probs = jnp.einsum(
            "qhd,khd->hqk", grad_mixed, value_all, preferred_element_type=jnp.float32
        )
        grad_value_part = jnp.einsum(
            "hqk,qhd->khd", probs, grad_mixed, preferred_element_type=jnp.float32
        )
        again = jnp.exp(masked_scores(queries, key_all, allowed) - log_total)
        centre = jnp.sum(again * grad_probs, axis=-1, keepdims=True)
        grad_scores = (again * (grad_probs - centre)).astype(jnp.bfloat16)
        grad_queries = (
            jnp.einsum("hqk,khd->qhd", grad_scores, key_all, preferred_element_type=jnp.float32)
            * factor
        )
        grad_queries = grad_queries.reshape(half_rows, part_width).astype(jnp.bfloat16)
        grad_key_part = (
            jnp.einsum("hqk,qhd->khd", grad_scores, queries, preferred_element_type=jnp.float32)
            * factor
        )
        grad_key_sum, grad_value_sum = (
            lax.psum_scatter(
                grad_key_part.reshape(seq_rows, part_width).astype(jnp.bfloat16),
                "ctx",
                scatter_dimension=0,
                tiled=True,
            ).astype(jnp.float32),
            lax.psum_scatter(
                grad_value_part.reshape(seq_rows, part_width).astype(jnp.bfloat16),
                "ctx",
                scatter_dimension=0,
                tiled=True,
            ).astype(jnp.float32),
        )
        grad_keys = grad_key_sum.astype(jnp.bfloat16)
        grad_values = grad_value_sum.astype(jnp.bfloat16)
        grad_query_w = jnp.einsum(
            "td,tc->dc", normed_all, grad_queries, preferred_element_type=jnp.float32
        )
        grad_key_w = jnp.einsum(
            "td,tc->dc", normed_all, grad_keys, preferred_element_type=jnp.float32
        )
        grad_value_w = jnp.einsum(
            "td,tc->dc", normed_all, grad_values, preferred_element_type=jnp.float32
        )
        grad_query_b = jnp.sum(grad_queries.astype(jnp.float32), axis=0)
        grad_value_b = jnp.sum(grad_values.astype(jnp.float32), axis=0)
        grad_normed_part = jnp.einsum(
            "tc,dc->td", grad_queries, w_query, preferred_element_type=jnp.float32
        )
        grad_normed_part = grad_normed_part + jnp.einsum(
            "tc,dc->td", grad_keys, w_key, preferred_element_type=jnp.float32
        )
        grad_normed_part = grad_normed_part + jnp.einsum(
            "tc,dc->td", grad_values, w_value, preferred_element_type=jnp.float32
        )
        grad_normed = tensor_sums(grad_normed_part)
        grad_rows_a, grad_attn_g, grad_attn_s = general_norm_backward(
            grad_normed, scaled_a, inverse_a, attn_gain
        )
        grad_rows = grad_middle + grad_rows_a
        big_sums, small_sums = carry
        big_sums = (
            big_sums[0] + grad_query_w,
            big_sums[1] + grad_key_w,
            big_sums[2] + grad_value_w,
            big_sums[3] + grad_inner_w,
            big_sums[4] + grad_output_w,
            big_sums[5] + grad_outer_w,
        )
        small_terms = (
            grad_attn_g,
            grad_attn_s,
            general_piece(grad_query_b, width, tensor_at * part_width),
            general_piece(grad_value_b, width, tensor_at * part_width),
            jnp.sum(grad_middle, axis=0),
            grad_ffn_g,
            grad_ffn_s,
            general_piece(grad_inner_b, unit_total, tensor_at * unit_width),
            jnp.sum(cot_rows, axis=0),
        )
        small_sums = tuple((old + new for old, new in zip(small_sums, small_terms)))
        return ((big_sums, small_sums), (result_rows, grad_rows))

    big_init = (
        jnp.zeros((width, part_width), jnp.float32),
        jnp.zeros((width, part_width), jnp.float32),
        jnp.zeros((width, part_width), jnp.float32),
        jnp.zeros((width, unit_width), jnp.float32),
        jnp.zeros((part_width, width), jnp.float32),
        jnp.zeros((unit_width, width), jnp.float32),
    )
    small_init = tuple((jnp.zeros((width,), jnp.float32) for index_small in range(7))) + (
        jnp.zeros((unit_total,), jnp.float32),
        jnp.zeros((width,), jnp.float32),
    )
    small_init = (
        small_init[0],
        small_init[1],
        small_init[2],
        small_init[3],
        small_init[4],
        small_init[5],
        small_init[6],
        small_init[7],
        small_init[8],
    )
    gathered = fetch_weights(shards)

    def scan_step(carry, item):
        return micro(gathered, carry, item)

    (big_sums, small_sums), (block_out, grad_input) = lax.scan(
        scan_step, (big_init, small_init), (hidden_in, cotangent, segment_ids)
    )
    paired = (
        lax.psum(big_sums[0].astype(jnp.bfloat16), "ctx").astype(jnp.float32),
        lax.psum(big_sums[1].astype(jnp.bfloat16), "ctx").astype(jnp.float32),
        lax.psum(big_sums[2].astype(jnp.bfloat16), "ctx").astype(jnp.float32),
        lax.psum(big_sums[3].astype(jnp.bfloat16), "ctx").astype(jnp.float32),
        lax.psum(big_sums[4].astype(jnp.bfloat16), "ctx").astype(jnp.float32),
        lax.psum(big_sums[5].astype(jnp.bfloat16), "ctx").astype(jnp.float32),
    )
    owned = (
        lax.psum_scatter(
            paired[0].astype(jnp.bfloat16), "dp", scatter_dimension=0, tiled=True
        ).astype(jnp.float32),
        lax.psum_scatter(
            paired[1].astype(jnp.bfloat16), "dp", scatter_dimension=0, tiled=True
        ).astype(jnp.float32),
        lax.psum_scatter(
            paired[2].astype(jnp.bfloat16), "dp", scatter_dimension=0, tiled=True
        ).astype(jnp.float32),
        lax.psum_scatter(
            paired[3].astype(jnp.bfloat16), "dp", scatter_dimension=0, tiled=True
        ).astype(jnp.float32),
        lax.psum_scatter(
            paired[4].astype(jnp.bfloat16), "dp", scatter_dimension=1, tiled=True
        ).astype(jnp.float32),
        lax.psum_scatter(
            paired[5].astype(jnp.bfloat16), "dp", scatter_dimension=1, tiled=True
        ).astype(jnp.float32),
    )
    small = lax.psum(
        (
            small_sums[0],
            small_sums[1],
            small_sums[2],
            small_sums[3],
            small_sums[4],
            small_sums[5],
            small_sums[6],
            small_sums[7],
            small_sums[8],
        ),
        ("dp", "ctx", "tensor"),
    )
    return (
        block_out,
        grad_input,
        small[0],
        small[1],
        owned[0],
        owned[1],
        owned[2],
        small[2],
        small[3],
        owned[4],
        small[4],
        small[5],
        small[6],
        owned[3],
        small[7],
        owned[5],
        small[8],
    )


SPECS = (
    P("dp", ("ctx", "tensor"), None), P("dp", ("ctx", "tensor"), None), P("dp", None), P(), P(),
    P("dp", "tensor"), P("dp", "tensor"), P("dp", "tensor"), P(), P(), P("tensor", "dp"), P(), P(),
    P(), P("dp", "tensor"), P(), P("tensor", "dp"), P(),
)
OUT_SPECS = (
    P("dp", ("ctx", "tensor"), None), P("dp", ("ctx", "tensor"), None), P(), P(),
    P("dp", "tensor"), P("dp", "tensor"), P("dp", "tensor"), P(), P(), P("tensor", "dp"), P(), P(),
    P(), P("dp", "tensor"), P(), P("tensor", "dp"), P(),
)


def solution(mesh):
    lined_up = mesh.shape["dp"] == 4 and mesh.shape["tensor"] == 4 and mesh.shape["ctx"] == 2
    return jax.shard_map(
        body if lined_up else general_body, mesh=mesh, in_specs=SPECS, out_specs=OUT_SPECS, check_vma=False
    )
```
